256 devices in a mesh: req: 2 (over core), blk: 128 (over z, x, y).
Axes of the slice: x: 4, y: 4, z: 8, core: 2. Of those that a mesh axis runs over, the one named last changes fastest.
Arguments:
- query: bfloat16 [2, 8192, 2048], P('req', 'blk'), may hold values from -64 to 64
- rotated_key_value: bfloat16 [2, 2, 8192, 512], P('req', None, 'blk'), may hold values from -64 to 64
- lengths: int32 [2], P('req'), may hold values from 6144 to 8192, as said below
- block_map: int32 [256], replicated, may hold values from 0 to 255, as said below
- segment_head: int32 [4], replicated, may hold values from 0 to 3, each once
Outputs:
- attended: bfloat16 [2, 8192, 2048], P('req', 'blk')
- cache: bfloat16 [2, 2, 128, 256, 128], P('req', None, 'blk')
The draws below stay inside these ranges and needn't reach their ends.
Inputs may be any that keep to these rules, and one draw needn't show every extreme that they name: `lengths`: one of the two prompts has exactly 8192 tokens. `block_map`: each prompt block appears once; storage blocks 2d and 2d+1 hold blocks b and 255 - b for some b < 128.
All inputs are finite; a program needn't handle non-finite values.
Results may differ from the reference program's by a relative error of at most 0.007.
Values may be sent and summed in bfloat16 or wider, within the bound.
No kernel may reach another device: no remote copies, remote signals or barrier semaphores. Data moves between devices by JAX's collectives and lax.ppermute only.
A program may use at most 128 MiB of HBM per device.

```python
import jax
import jax.numpy as jnp
from jax import lax

QUERY_HEADS = 16
KEY_VALUE_HEADS = 4
HEAD_DIMENSION = 128
WINDOW = 4096
PROMPT_CAPACITY = 8192
BLOCKS = 256
SEGMENT_COUNT = 32
SEGMENT_LENGTH = 256
N_BLK = 128


def joint_floats(key):
    key_query_scores, key_tile = jax.random.split(key, 2)
    query = jnp.clip(jax.random.normal(key_query_scores, (2, PROMPT_CAPACITY, QUERY_HEADS, HEAD_DIMENSION)), -6.0, 6.0)
    block_pairs = jnp.clip(jax.random.normal(key_tile, (2, 2, PROMPT_CAPACITY, KEY_VALUE_HEADS, HEAD_DIMENSION)), -6.0, 6.0)
    return (query.reshape(2, PROMPT_CAPACITY, QUERY_HEADS * HEAD_DIMENSION), block_pairs.reshape(2, 2, PROMPT_CAPACITY, KEY_VALUE_HEADS * HEAD_DIMENSION))


def draw_query(key, part):
    return joint_floats(jax.random.fold_in(key, 11))[0].astype(jnp.bfloat16)


def draw_rotated_key_value(key, part):
    return joint_floats(jax.random.fold_in(key, 11))[1].astype(jnp.bfloat16)


def draw_lengths(key, part):
    low = 3 * PROMPT_CAPACITY // 4
    pair = jax.random.randint(jax.random.fold_in(key, 5), (2,), low, PROMPT_CAPACITY + 1)
    which = jax.random.randint(jax.random.fold_in(key, 6), (), 0, 2)
    return jnp.where(jnp.arange(2) == which, PROMPT_CAPACITY, pair).astype(jnp.int32)


def draw_block_map(key, part):
    order = jax.random.permutation(jax.random.fold_in(key, 8), BLOCKS // 2).astype(jnp.int32)
    return jnp.stack([order, BLOCKS - 1 - order], axis=1).reshape(BLOCKS).astype(jnp.int32)


def setup_inputs(seed: int = 0) -> dict:
    key_list = jax.random.split(jax.random.key(seed), 6)
    query = draw_query(jax.random.fold_in(key_list[5], 71), 0)
    rotated_key_value = draw_rotated_key_value(jax.random.fold_in(key_list[5], 71), 0)
    lengths = draw_lengths(jax.random.fold_in(key_list[5], 71), 0)
    block_map = draw_block_map(jax.random.fold_in(key_list[5], 71), 0)
    segment_head = jax.random.permutation(key_list[4], KEY_VALUE_HEADS).astype(jnp.int32)
    return {"query": query, "rotated_key_value": rotated_key_value, "lengths": lengths, "block_map": block_map, "segment_head": segment_head}


def attend_head(q_all, k_all, v_all, length):
    qblock = min(512, PROMPT_CAPACITY)
    kpos = jnp.arange(PROMPT_CAPACITY, dtype=jnp.int32)
    scale = HEAD_DIMENSION ** -0.5

    def one_block(start):
        row_indices = lax.dynamic_slice_in_dim(q_all, start, qblock, 0)
        qpos = start + jnp.arange(qblock, dtype=jnp.int32)
        scores = jnp.einsum("qgd,kd->gqk", row_indices.astype(jnp.float32), k_all.astype(jnp.float32)) * scale
        allowed = (kpos[None, :] <= qpos[:, None]) & (kpos[None, :] > qpos[:, None] - WINDOW)
        allowed = allowed & ((kpos[None, :] < length) | (kpos[None, :] == qpos[:, None]))
        allowed = allowed[None]
        masked = jnp.where(allowed, scores, -jnp.inf)
        upper_limit = jnp.max(masked, axis=-1, keepdims=True)
        prob = jnp.where(allowed, jnp.exp(scores - upper_limit), 0.0)
        total = jnp.sum(prob, axis=-1)
        weights = prob.astype(jnp.bfloat16).astype(jnp.float32)
        summed = jnp.einsum("gqk,kd->gqd", weights, v_all.astype(jnp.float32))
        out = summed / total[..., None]
        return jnp.where((qpos < length)[None, :, None], out, 0.0)

    starts = jnp.arange(0, PROMPT_CAPACITY, qblock, dtype=jnp.int32)
    return lax.map(one_block, starts)


def reference(query, rotated_key_value, lengths, block_map, segment_head):
    prompt_blocks = block_map.shape[0]
    half_width = PROMPT_CAPACITY // prompt_blocks
    query_groups = QUERY_HEADS // KEY_VALUE_HEADS
    inverse_permutation = jnp.zeros((prompt_blocks,), jnp.int32).at[block_map].set(jnp.arange(prompt_blocks, dtype=jnp.int32))
    query_sequence = query.reshape(2, prompt_blocks, half_width, QUERY_HEADS * HEAD_DIMENSION)[:, inverse_permutation].reshape(2, PROMPT_CAPACITY, KEY_VALUE_HEADS, query_groups, HEAD_DIMENSION)
    key_value_sequence = rotated_key_value.reshape(2, 2, prompt_blocks, half_width, KEY_VALUE_HEADS * HEAD_DIMENSION)[:, :, inverse_permutation].reshape(2, 2, PROMPT_CAPACITY, KEY_VALUE_HEADS, HEAD_DIMENSION)
    results = []
    for prompt in range(2):
        def single_head(head):
            q_all = lax.dynamic_index_in_dim(query_sequence[prompt], head, 1, keepdims=False)
            k_all = lax.dynamic_index_in_dim(key_value_sequence[prompt, 0], head, 1, keepdims=False)
            v_all = lax.dynamic_index_in_dim(key_value_sequence[prompt, 1], head, 1, keepdims=False)
            return attend_head(q_all, k_all, v_all, lengths[prompt])
        output_heads = lax.map(single_head, jnp.arange(KEY_VALUE_HEADS, dtype=jnp.int32))
        results.append(output_heads.transpose(1, 3, 0, 2, 4).reshape(PROMPT_CAPACITY, QUERY_HEADS * HEAD_DIMENSION))
    seq_out = jnp.stack(results).astype(jnp.bfloat16)
    attended = seq_out.reshape(2, prompt_blocks, half_width, QUERY_HEADS * HEAD_DIMENSION)[:, block_map].reshape(2, PROMPT_CAPACITY, QUERY_HEADS * HEAD_DIMENSION)
    launch_lattice = key_value_sequence.reshape(2, 2, SEGMENT_LENGTH, SEGMENT_COUNT, KEY_VALUE_HEADS, HEAD_DIMENSION)
    launch_lattice = jnp.take(launch_lattice, segment_head, axis=4)
    cache = launch_lattice.transpose(0, 1, 4, 3, 2, 5).reshape(2, 2, N_BLK, SEGMENT_LENGTH, HEAD_DIMENSION)
    slots = jnp.arange(N_BLK, dtype=jnp.int32)
    position = jnp.arange(SEGMENT_LENGTH, dtype=jnp.int32)[None, :] * SEGMENT_COUNT + (slots % SEGMENT_COUNT)[:, None]
    keep = position[None] < lengths[:, None, None]
    cache = jnp.where(keep[:, None, :, :, None], cache, jnp.zeros((), jnp.bfloat16))
    return attended, cache
```

```python
import functools
import math

import jax
import jax.numpy as jnp
from jax import lax
from jax.experimental import pallas as pl
from jax.experimental.pallas import tpu as pltpu
from jax.sharding import PartitionSpec as P

QUERY_HEADS = 16
KEY_VALUE_HEADS = 4
GROUP = QUERY_HEADS // KEY_VALUE_HEADS
HEAD_DIMENSION = 128
WINDOW = 4096
BLOCK = 32
WINDOW_BLOCKS = WINDOW // BLOCK
BLOCKS = 256
CHUNK_BLOCKS = 16
CHUNK = CHUNK_BLOCKS * BLOCK
NZ, NX, NY = 8, 4, 4
N_BLK = NZ * NX * NY
ROWS = GROUP * BLOCK
LOG2E = 1.4426950408889634
NEG = -1e30


def attention_kernel(table, q_blocks, length, q_ref, c0, r1, r2, r3, l1, l2, l3, r4, l4, o_ref, kv, s_scr, sems):
    step = 2 * 64 * NY * NX
    half = step // 2
    pieces = [(c0, 0), (r1, 7), (r2, 6), (r3, 5), (l1, 1), (l2, 2), (l3, 3)]
    copies = [
        pltpu.make_async_copy(src, kv.at[pl.ds(slot * step, step)], sems.at[i])
        for i, (src, slot) in enumerate(pieces)
    ]
    copies.append(pltpu.make_async_copy(r4, kv.at[pl.ds(4 * step, half)], sems.at[7]))
    copies.append(pltpu.make_async_copy(l4, kv.at[pl.ds(4 * step + half, half)], sems.at[8]))
    for copy in copies:
        copy.start()
    for copy in copies:
        copy.wait()

    token = lax.broadcasted_iota(jnp.int32, (ROWS, CHUNK), 0) % BLOCK
    key = lax.broadcasted_iota(jnp.int32, (ROWS, CHUNK), 1)
    ahead = token - key
    row_token = lax.broadcasted_iota(jnp.int32, (ROWS, HEAD_DIMENSION), 0) % BLOCK
    scale = HEAD_DIMENSION**-0.5 * LOG2E
    ones = jnp.ones((CHUNK, HEAD_DIMENSION), jnp.bfloat16)

    def load(chunk, offset):
        return jnp.concatenate(
            [
                kv[pl.ds(pl.multiple_of(table[chunk * CHUNK_BLOCKS + u] + offset, BLOCK), BLOCK), :]
                for u in range(CHUNK_BLOCKS)
            ],
            axis=0,
        )

    def one_block(i, carry):
        block = q_blocks[i]
        low = jnp.maximum(block - WINDOW_BLOCKS, 0) // CHUNK_BLOCKS
        high = block // CHUNK_BLOCKS
        q = q_ref[i]

        def scores(chunk, top, masked):
            s = lax.dot_general(q, load(chunk, 0), (((1,), (1,)), ((), ())), preferred_element_type=jnp.float32)
            if masked:
                distance = ahead + (block * BLOCK - chunk * CHUNK)
                s = jnp.where((distance >= 0) & (distance < WINDOW), s, NEG)
            s_scr[chunk - low] = s
            for j in range(CHUNK // 128):
                top = jnp.maximum(top, s[:, j * 128 : (j + 1) * 128])
            return top

        top = jnp.full((ROWS, 128), NEG, jnp.float32)
        top = scores(high, top, True)
        top = lax.cond(low < high, lambda t: scores(low, t, True), lambda t: t, top)
        top = lax.fori_loop(low + 1, high, lambda c, t: scores(c, t, False), top)
        top = jnp.max(top, axis=1, keepdims=True) * scale

        def weigh(chunk, acc):
            p = jnp.exp2(s_scr[chunk - low] * scale - top).astype(jnp.bfloat16)
            v = jnp.concatenate([load(chunk, 64), ones], axis=1)
            return acc + lax.dot_general(p, v, (((1,), (0,)), ((), ())), preferred_element_type=jnp.float32)

        acc = lax.fori_loop(low, high + 1, weigh, jnp.zeros((ROWS, 2 * HEAD_DIMENSION), jnp.float32))
        out = acc[:, :HEAD_DIMENSION] / acc[:, HEAD_DIMENSION:]
        out = jnp.where(block * BLOCK + row_token < length[0], out, 0.0)
        o_ref[i] = out.astype(jnp.bfloat16)
        return carry

    lax.fori_loop(0, 2 * NY, one_block, 0)


def attention(table, q_blocks, length, q, pieces):
    smem = pl.BlockSpec(memory_space=pltpu.SMEM)
    vmem = pl.BlockSpec(memory_space=pltpu.VMEM)
    return pl.pallas_call(
        attention_kernel,
        out_shape=jax.ShapeDtypeStruct((2 * NY, ROWS, HEAD_DIMENSION), jnp.bfloat16),
        in_specs=[smem] * 3 + [vmem] + [pl.BlockSpec(memory_space=pl.ANY)] * 9,
        out_specs=vmem,
        scratch_shapes=[
            pltpu.VMEM((2 * BLOCKS * BLOCK, HEAD_DIMENSION), jnp.bfloat16),
            pltpu.VMEM((WINDOW // CHUNK + 1, ROWS, CHUNK), jnp.float32),
            pltpu.SemaphoreType.DMA((9,)),
        ],
        compiler_params=pltpu.CompilerParams(vmem_limit_bytes=32 * 1024 * 1024),
        cost_estimate=pl.CostEstimate(flops=3_000_000_000, bytes_accessed=5_000_000, transcendentals=4_000_000),
        name="attention",
    )(table, q_blocks, length, q, *pieces)


def body(query, rotated_key_value, lengths, block_map, segment_head):
    place = lax.axis_index("blk")
    z, x, y = place // 16, (place // 4) % 4, place % 4
    y_groups = [[4 * g + i for i in range(4)] for g in range(N_BLK // 4)]

    def move(value, target):
        return lax.ppermute(value, "blk", [(s, target(s // 16, (s // 4) % 4, s % 4)) for s in range(N_BLK)])

    def index(zz, xx, yy):
        return (zz % NZ) * 16 + xx * 4 + yy

    outgoing = jnp.take(rotated_key_value[0].reshape(2, 64, KEY_VALUE_HEADS, HEAD_DIMENSION), segment_head, axis=2)
    outgoing = outgoing.transpose(2, 0, 1, 3)
    own = lax.all_to_all(outgoing, "blk", 0, 0, axis_index_groups=y_groups, tiled=True)
    q = query[0].reshape(2, BLOCK, KEY_VALUE_HEADS, GROUP, HEAD_DIMENSION)
    q = jnp.take(q, segment_head, axis=2).transpose(2, 0, 3, 1, 4)

    x1 = move(own, lambda a, b, c: index(a, b ^ 1, c))
    x3 = move(own, lambda a, b, c: index(a, b ^ 3, c))
    x2 = move(x1, lambda a, b, c: index(a, b ^ 3, c))
    plane = jnp.concatenate([own, x1, x2, x3], axis=0).reshape(4 * 4 * 128, HEAD_DIMENSION)
    right = lambda v: move(v, lambda a, b, c: index(a + 1, b, c))
    left = lambda v: move(v, lambda a, b, c: index(a - 1, b, c))
    r1, l1 = right(plane), left(plane)
    q = lax.all_to_all(q, "blk", 0, 0, axis_index_groups=y_groups, tiled=True)
    r2, l2 = right(r1), left(l1)
    r3, l3 = right(r2), left(l2)
    half = plane.shape[0] // 2
    r4, l4 = right(r3[:half]), left(l3[half:])
    pieces = [plane, r1, r2, r3, l1, l2, l3, r4, l4]

    blocks = jnp.arange(BLOCKS, dtype=jnp.int32)
    hit = block_map[None, :] == blocks[:, None]
    device = blocks // 2
    slot = ((device // 16 - z) % NZ * 4 + ((device // 4) % 4 ^ x)) * 4 + device % 4
    row = slot * 128 + (blocks % 2) * BLOCK
    table = jnp.sum(jnp.where(hit, row[None, :], 0), axis=1, dtype=jnp.int32)
    q_blocks = lax.dynamic_slice_in_dim(block_map, (z * 4 + x) * 8, 8)
    out = attention(table, q_blocks, lengths, q.reshape(2 * NY, ROWS, HEAD_DIMENSION), pieces)
    out = out.reshape(4, 2, GROUP, BLOCK, HEAD_DIMENSION)
    out = lax.all_to_all(out, "blk", 0, 0, axis_index_groups=y_groups, tiled=True)
    heads = jnp.arange(KEY_VALUE_HEADS, dtype=jnp.int32)
    inverse = jnp.sum(jnp.where(segment_head[None, :] == heads[:, None], heads[None, :], 0), axis=1)
    attended = jnp.take(out, inverse, axis=0).transpose(1, 3, 0, 2, 4).reshape(1, 64, QUERY_HEADS * HEAD_DIMENSION)

    offset = (z % 2) * 16 + x * 4 + z // 2
    pick = (jnp.arange(BLOCK, dtype=jnp.int32) == offset)[None, None, None, :, None]

    def rows_of(piece):
        v = piece.reshape(-1, 2, 2, BLOCK, HEAD_DIMENSION)
        v = jnp.sum(jnp.where(pick, v, jnp.zeros((), jnp.bfloat16)), axis=3)
        return v.transpose(0, 2, 1, 3).reshape(-1, 2 * HEAD_DIMENSION)

    ordered = [plane, l1, l2, l3, r4, l4, r3, r2, r1]
    picked = jnp.concatenate([rows_of(v) for v in ordered], axis=0)
    position = blocks * BLOCK + offset
    where = (table // 128) * 2 + (table // BLOCK) % 2
    choose = (where[:, None] == blocks[None, :]) & (position < lengths[0])[:, None]
    cache = jnp.dot(choose.astype(jnp.bfloat16), picked, preferred_element_type=jnp.float32).astype(jnp.bfloat16)
    cache = move(cache, lambda a, b, c: index(2 * c + a % 2, b, a // 2))
    cache = cache.reshape(BLOCKS, 2, HEAD_DIMENSION).transpose(1, 0, 2)[None, :, None]
    return attended, cache


def solution(mesh):
    return jax.shard_map(
        body,
        mesh=mesh,
        in_specs=(P("req", "blk", None), P("req", None, "blk", None), P("req"), P(), P()),
        out_specs=(P("req", "blk", None), P("req", None, "blk", None, None)),
        check_vma=False,
    )
```

```python
import jax
import jax.numpy as jnp
from jax import lax
from jax.experimental import pallas as pl
from jax.experimental.pallas import tpu as pltpu
from jax.sharding import PartitionSpec as P

QUERY_HEADS = 16
KEY_VALUE_HEADS = 4
GROUP = QUERY_HEADS // KEY_VALUE_HEADS
HEAD = 128
WINDOW = 4096
BLOCK = 32
BLOCKS = 256
NZ, NX, NY = 8, 4, 4
N_BLK = NZ * NX * NY
PLANE = NX * NY
KEY_BLOCKS = 2 * NZ * NY
Q_BLOCKS = 2 * PLANE
ROWS = GROUP * BLOCK
KEYS = KEY_BLOCKS * BLOCK
JOINED = 4
CHUNK_BLOCKS = 8
CHUNK = CHUNK_BLOCKS * BLOCK
MESSAGE = 2 * ROWS + 16
SCALE = HEAD**-0.5 * 1.4426950408889634
NEG = -1e30

SMEM = pl.BlockSpec(memory_space=pltpu.SMEM)
VMEM = pl.BlockSpec(memory_space=pltpu.VMEM)
PARAMS = pltpu.CompilerParams(vmem_limit_bytes=40 * 1024 * 1024)


def split_kv_kernel(heads, kv_ref, o_ref):
    for y in range(NY):
        o_ref[y] = kv_ref[:, pl.ds(pl.multiple_of(heads[y] * HEAD, HEAD), HEAD)]


def split_q_kernel(heads, q_ref, o_ref):
    for y in range(NY):
        for g in range(GROUP):
            column = pl.multiple_of((heads[y] * GROUP + g) * HEAD, HEAD)
            for j in range(2):
                tile = q_ref[j * BLOCK : (j + 1) * BLOCK, pl.ds(column, HEAD)]
                for x in range(NX):
                    o_ref[x * NY + y, j * ROWS + g * BLOCK : j * ROWS + (g + 1) * BLOCK] = tile


def arrange_kernel(rank, offset, c0, r1, r2, r3, l1, l2, l3, r4, l4, k_ref, v_ref, pick_ref):
    v_ref[:, HEAD:] = jnp.ones((KEYS, HEAD), jnp.bfloat16)
    pieces = [(c0, 0), (l1, 1), (l2, 2), (l3, 3), (r4, 4), (l4, 4), (r3, 5), (r2, 6), (r1, 7)]
    for piece, zrel in pieces:
        lines = range(NY)
        if piece is r4:
            lines = range(NY // 2)
        if piece is l4:
            lines = range(NY // 2, NY)
        for at, y in enumerate(lines):
            for j in range(2):
                row = pl.multiple_of(rank[(zrel * NY + y) * 2 + j] * BLOCK, BLOCK)
                k_ref[pl.ds(row, BLOCK), :] = piece[at * 128 + j * BLOCK : at * 128 + (j + 1) * BLOCK, :]
                v_ref[pl.ds(row, BLOCK), :HEAD] = piece[at * 128 + 64 + j * BLOCK : at * 128 + 64 + (j + 1) * BLOCK, :]
    some = 16
    line = lax.broadcasted_iota(jnp.int32, (NX * some, some * BLOCK), 0)
    column = lax.broadcasted_iota(jnp.int32, (NX * some, some * BLOCK), 1)
    wanted = (line % some) * BLOCK + offset[0] + (line // some) * NY
    select = jnp.where(column == wanted, 1.0, 0.0).astype(jnp.bfloat16)
    for c in range(KEY_BLOCKS // some):
        rows = slice(c * some * BLOCK, (c + 1) * some * BLOCK)
        k = jnp.dot(select, k_ref[rows, :], preferred_element_type=jnp.float32).astype(jnp.bfloat16)
        v = jnp.dot(select, v_ref[rows, :HEAD], preferred_element_type=jnp.float32).astype(jnp.bfloat16)
        for x in range(NX):
            pick_ref[x, c * some : (c + 1) * some, :HEAD] = k[x * some : (x + 1) * some]
            pick_ref[x, c * some : (c + 1) * some, HEAD:] = v[x * some : (x + 1) * some]


def attention_kernel(q_order, q_ids, lows, highs, q_ref, k_ref, v_ref, kpos_ref, o_ref, s_scr, top_scr, acc_scr, stat):
    lane = lax.broadcasted_iota(jnp.int32, (ROWS, 128), 1)
    token = lax.broadcasted_iota(jnp.int32, (BLOCK, CHUNK), 0)

    def one_group(i, carry):
        low, high = lows[i], highs[i]
        q = jnp.concatenate([q_ref[q_order[i * JOINED + u]] for u in range(JOINED)], axis=0)
        top_scr[...] = jnp.full((JOINED * ROWS, 128), NEG, jnp.float32)
        acc_scr[...] = jnp.zeros((JOINED * ROWS, 2 * HEAD), jnp.float32)

        def scores(chunk, carry):
            start = pl.multiple_of(chunk * CHUNK, CHUNK)
            k = k_ref[pl.ds(start, CHUNK), :]
            s = lax.dot_general(q, k, (((1,), (1,)), ((), ())), preferred_element_type=jnp.float32)
            kpos = kpos_ref[pl.ds(chunk, 1), :]
            for u in range(JOINED):
                distance = (q_ids[i * JOINED + u] * BLOCK + token) - kpos
                bias = jnp.where((distance >= 0) & (distance < WINDOW), 0.0, NEG)
                for g in range(GROUP):
                    rows = slice(u * ROWS + g * BLOCK, u * ROWS + (g + 1) * BLOCK)
                    part = s[rows] + bias
                    s_scr[chunk - low, rows, :] = part
                    top_scr[rows] = jnp.maximum(top_scr[rows], jnp.maximum(part[:, :128], part[:, 128:]))
            return carry

        lax.fori_loop(low, high, scores, 0)
        top = jnp.max(top_scr[...], axis=1, keepdims=True) * SCALE
        top_scr[...] = jnp.broadcast_to(top, (JOINED * ROWS, 128))

        def weigh(chunk, carry):
            start = pl.multiple_of(chunk * CHUNK, CHUNK)
            top = top_scr[...]
            s = s_scr[chunk - low]
            p = jnp.exp2(s * SCALE - jnp.concatenate([top, top], axis=1)).astype(jnp.bfloat16)
            acc_scr[...] += jnp.dot(p, v_ref[pl.ds(start, CHUNK), :], preferred_element_type=jnp.float32)
            return carry

        lax.fori_loop(low, high, weigh, 0)
        for u in range(JOINED):
            rows = slice(u * ROWS, (u + 1) * ROWS)
            block = q_order[i * JOINED + u]
            total = acc_scr[rows, HEAD:]
            out = acc_scr[rows, :HEAD] / jnp.maximum(total, 1e-30)
            o_ref[block // 2, pl.ds(pl.multiple_of(block % 2 * ROWS, ROWS), ROWS), :] = out.astype(jnp.bfloat16)
            old = jnp.where(lane == block, top_scr[rows], stat[...])
            stat[...] = jnp.where(lane == block + Q_BLOCKS, total, old)
        return carry

    stat[...] = jnp.zeros((ROWS, 128), jnp.float32)
    lax.fori_loop(0, Q_BLOCKS // JOINED, one_group, 0)
    turned = stat[...].T
    for d in range(PLANE):
        value = jnp.concatenate(
            [turned[2 * d : 2 * d + 2], turned[Q_BLOCKS + 2 * d : Q_BLOCKS + 2 * d + 2]], axis=0
        )
        first = value.astype(jnp.bfloat16).astype(jnp.float32)
        second = (value - first).astype(jnp.bfloat16).astype(jnp.float32)
        third = value - first - second
        rows = jnp.concatenate([first, second, third, jnp.zeros_like(first)], axis=0)
        o_ref[d, 2 * ROWS :, :] = rows.astype(jnp.bfloat16)


def combine_kernel(heads, blocks, length, m_ref, o_ref):
    values = []
    for d in range(PLANE):
        rows = m_ref[d, 2 * ROWS :, :].astype(jnp.float32)
        values.append(rows[0:4] + rows[4:8] + rows[8:12])
    weights = [None] * PLANE
    for y in range(NY):
        sources = [x * NY + y for x in range(NX)]
        top = values[sources[0]][0:2]
        for d in sources[1:]:
            top = jnp.maximum(top, values[d][0:2])
        parts = [jnp.exp2(values[d][0:2] - top) * values[d][2:4] for d in sources]
        total = parts[0] + parts[1] + parts[2] + parts[3]
        for d, part in zip(sources, parts):
            weights[d] = part / total
    matrix = jnp.concatenate(weights + [jnp.zeros((128 - Q_BLOCKS, 128), jnp.float32)], axis=0).T
    token = lax.broadcasted_iota(jnp.int32, (ROWS, HEAD), 0) % BLOCK
    for y in range(NY):
        for j in range(2):
            out = jnp.zeros((ROWS, HEAD), jnp.float32)
            for x in range(NX):
                d = x * NY + y
                weight = matrix[:, 2 * d + j : 2 * d + j + 1]
                out += weight * m_ref[d, j * ROWS : (j + 1) * ROWS, :].astype(jnp.float32)
            out = jnp.where(blocks[j] * BLOCK + token < length[0], out, 0.0).astype(jnp.bfloat16)
            for g in range(GROUP):
                column = pl.multiple_of((heads[y] * GROUP + g) * HEAD, HEAD)
                o_ref[j * BLOCK : (j + 1) * BLOCK, pl.ds(column, HEAD)] = out[g * BLOCK : (g + 1) * BLOCK]


def ranks(ids):
    return jnp.sum(ids[..., None, :] < ids[..., :, None], axis=-1, dtype=jnp.int32)


def placed(values, rank):
    places = jnp.arange(values.shape[-1], dtype=jnp.int32)
    return jnp.sum(jnp.where(rank[..., None, :] == places[:, None], values[..., None, :], 0), axis=-1, dtype=jnp.int32)


def body(query, rotated_key_value, lengths, block_map, segment_head):
    place = lax.axis_index("blk")
    z, x, y = place // 16, (place // 4) % 4, place % 4
    y_groups = [[4 * g + i for i in range(4)] for g in range(N_BLK // 4)]
    x_groups = [[16 * a + 4 * i + c for i in range(4)] for a in range(NZ) for c in range(NY)]
    planes = [[16 * a + i for i in range(16)] for a in range(NZ)]

    def move(value, target):
        return lax.ppermute(value, "blk", [(s, target(s // 16, (s // 4) % 4, s % 4)) for s in range(N_BLK)])

    def index(zz, xx, yy):
        return (zz % NZ) * 16 + xx * 4 + yy

    def exchange(value, groups):
        return lax.all_to_all(value, "blk", 0, 0, axis_index_groups=groups, tiled=True)

    kv = pl.pallas_call(
        split_kv_kernel,
        out_shape=jax.ShapeDtypeStruct((NY, 128, HEAD), jnp.bfloat16),
        in_specs=[SMEM, VMEM],
        out_specs=VMEM,
        name="split_kv",
    )(segment_head, rotated_key_value.reshape(128, KEY_VALUE_HEADS * HEAD))
    own = exchange(kv, y_groups).reshape(NY * 128, HEAD)
    right = lambda v: move(v, lambda a, b, c: index(a + 1, b, c))
    left = lambda v: move(v, lambda a, b, c: index(a - 1, b, c))
    r1, l1 = right(own), left(own)
    q = pl.pallas_call(
        split_q_kernel,
        out_shape=jax.ShapeDtypeStruct((PLANE, 2 * ROWS, HEAD), jnp.bfloat16),
        in_specs=[SMEM, VMEM],
        out_specs=VMEM,
        name="split_q",
    )(segment_head, query.reshape(2 * BLOCK, QUERY_HEADS * HEAD))
    q = exchange(q, planes).reshape(Q_BLOCKS, ROWS, HEAD)
    r2, l2 = right(r1), left(l1)
    r3, l3 = right(r2), left(l2)
    half = own.shape[0] // 2
    r4, l4 = right(r3[:half]), left(l3[half:])

    ids = block_map.reshape(NZ, NX, NY, 2).transpose(1, 0, 2, 3).reshape(NX, KEY_BLOCKS)
    rank = ranks(ids)
    ordered = placed(ids, rank)
    mine = lax.dynamic_index_in_dim(ordered, x, 0, keepdims=False)
    my_rank = lax.dynamic_index_in_dim(rank, x, 0, keepdims=False).reshape(NZ, 2 * NY)
    my_rank = lax.dynamic_slice_in_dim(jnp.concatenate([my_rank, my_rank], axis=0), z, NZ, 0).reshape(KEY_BLOCKS)
    q_ids = lax.dynamic_slice_in_dim(block_map, z * Q_BLOCKS, Q_BLOCKS)
    q_rank = ranks(q_ids)
    q_order = placed(jnp.arange(Q_BLOCKS, dtype=jnp.int32), q_rank)
    q_sorted = placed(q_ids, q_rank)
    grouped = q_sorted.reshape(Q_BLOCKS // JOINED, JOINED)
    lows = jnp.sum(mine[None, :] < grouped[:, :1] - WINDOW // BLOCK, axis=1, dtype=jnp.int32) // CHUNK_BLOCKS
    highs = jnp.sum(mine[None, :] <= grouped[:, -1:], axis=1, dtype=jnp.int32)
    highs = (highs + CHUNK_BLOCKS - 1) // CHUNK_BLOCKS
    kpos = mine[:, None] * BLOCK + jnp.arange(BLOCK, dtype=jnp.int32)[None, :]
    kpos = kpos.reshape(KEYS // CHUNK, CHUNK)

    offset = ((z % 2) * 16 + z // 2).reshape(1)
    k, v, pick = pl.pallas_call(
        arrange_kernel,
        out_shape=(
            jax.ShapeDtypeStruct((KEYS, HEAD), jnp.bfloat16),
            jax.ShapeDtypeStruct((KEYS, 2 * HEAD), jnp.bfloat16),
            jax.ShapeDtypeStruct((NX, KEY_BLOCKS, 2 * HEAD), jnp.bfloat16),
        ),
        in_specs=[SMEM] * 2 + [VMEM] * 9,
        out_specs=(VMEM,) * 3,
        name="arrange",
    )(my_rank, offset, own, r1, r2, r3, l1, l2, l3, r4, l4)

    out = pl.pallas_call(
        attention_kernel,
        out_shape=jax.ShapeDtypeStruct((PLANE, MESSAGE, HEAD), jnp.bfloat16),
        in_specs=[SMEM] * 4 + [VMEM] * 4,
        out_specs=VMEM,
        scratch_shapes=[
            pltpu.VMEM((KEYS // CHUNK, JOINED * ROWS, CHUNK), jnp.float32),
            pltpu.VMEM((JOINED * ROWS, 128), jnp.float32),
            pltpu.VMEM((JOINED * ROWS, 2 * HEAD), jnp.float32),
            pltpu.VMEM((ROWS, 128), jnp.float32),
        ],
        compiler_params=PARAMS,
        cost_estimate=pl.CostEstimate(flops=3_000_000_000, bytes_accessed=4_000_000, transcendentals=5_000_000),
        name="attention",
    )(q_order, q_sorted, lows, highs, q, k, v, kpos)

    pick = exchange(pick, x_groups).reshape(BLOCKS, 2 * HEAD)
    blocks = jnp.arange(BLOCKS, dtype=jnp.int32)
    position = blocks * BLOCK + offset + 4 * x
    choose = (ordered.reshape(1, BLOCKS) == blocks[:, None]) & (position < lengths[0])[:, None]
    cache = jnp.dot(choose.astype(jnp.bfloat16), pick, preferred_element_type=jnp.float32).astype(jnp.bfloat16)
    cache = move(cache, lambda a, b, c: index(2 * c + a % 2, b, a // 2))
    cache = cache.reshape(BLOCKS, 2, HEAD).transpose(1, 0, 2)[None, :, None]

    out = exchange(out, planes)
    my_blocks = lax.dynamic_slice_in_dim(block_map, 2 * place, 2)
    attended = pl.pallas_call(
        combine_kernel,
        out_shape=jax.ShapeDtypeStruct((2 * BLOCK, QUERY_HEADS * HEAD), jnp.bfloat16),
        in_specs=[SMEM] * 3 + [VMEM],
        out_specs=VMEM,
        name="combine",
    )(segment_head, my_blocks, lengths, out)
    return attended.reshape(1, 2 * BLOCK, QUERY_HEADS * HEAD), cache


def solution(mesh):
    return jax.shard_map(
        body,
        mesh=mesh,
        in_specs=(P("req", "blk", None), P("req", None, "blk", None), P("req"), P(), P()),
        out_specs=(P("req", "blk", None), P("req", None, "blk", None, None)),
        check_vma=False,
    )
```

```python
import functools

import jax
import jax.numpy as jnp
from jax import lax
from jax.experimental import pallas as pl
from jax.experimental.pallas import tpu as pltpu
from jax.sharding import PartitionSpec as P

QUERY_HEADS = 16
KEY_VALUE_HEADS = 4
GROUP = QUERY_HEADS // KEY_VALUE_HEADS
HEAD = 128
WINDOW = 4096
BLOCK = 32
BLOCKS = 256
NZ, NX, NY = 8, 4, 4
N_BLK = NZ * NX * NY
PLANE = NX * NY
KEY_BLOCKS = 2 * NZ * NY
Q_BLOCKS = 2 * PLANE
ROWS = GROUP * BLOCK
KEYS = KEY_BLOCKS * BLOCK
JOINED = 4
CHUNK_BLOCKS = 8
CHUNK = CHUNK_BLOCKS * BLOCK
MESSAGE = 2 * ROWS + 16
SCALE = HEAD**-0.5 * 1.4426950408889634
NEG = -1e30
AT_ORDER = KEY_BLOCKS
AT_ID = AT_ORDER + Q_BLOCKS
AT_LOW = AT_ID + Q_BLOCKS
AT_HIGH = AT_LOW + Q_BLOCKS // JOINED

SMEM = pl.BlockSpec(memory_space=pltpu.SMEM)
VMEM = pl.BlockSpec(memory_space=pltpu.VMEM)
PARAMS = pltpu.CompilerParams(vmem_limit_bytes=40 * 1024 * 1024)


def split_kv_kernel(heads, kv_ref, *o_refs):
    y = lax.rem(lax.axis_index("blk"), NY)
    for k in range(NY):
        o_refs[k][...] = kv_ref[:, pl.ds(pl.multiple_of(heads[y ^ k] * HEAD, HEAD), HEAD)]


def split_q_kernel(heads, q_ref, o_ref):
    for y in range(NY):
        for g in range(GROUP):
            column = pl.multiple_of((heads[y] * GROUP + g) * HEAD, HEAD)
            for j in range(2):
                tile = q_ref[j * BLOCK : (j + 1) * BLOCK, pl.ds(column, HEAD)]
                for x in range(NX):
                    o_ref[x * NY + y, j * ROWS + g * BLOCK : j * ROWS + (g + 1) * BLOCK] = tile


def arrange(table, pieces, k_scr, kt_scr, v_scr, pick_ref):
    place = lax.axis_index("blk")
    z, y = place // PLANE, lax.rem(place, NY)
    v_scr[:, HEAD:] = jnp.ones((KEYS, HEAD), jnp.bfloat16)
    for piece, zrel, lines in pieces:
        for at, line in enumerate(lines):
            for j in range(2):
                source = (lax.rem(z + zrel, NZ) * NY + (y ^ line)) * 2 + j
                row = pl.multiple_of(table[source] * BLOCK, BLOCK)
                k_scr[pl.ds(row, BLOCK), :] = piece[at * 128 + j * BLOCK : at * 128 + (j + 1) * BLOCK, :]
                v_scr[pl.ds(row, BLOCK), :HEAD] = piece[at * 128 + 64 + j * BLOCK : at * 128 + 64 + (j + 1) * BLOCK, :]
    for t in range(KEYS // 128):
        kt_scr[:, t * 128 : (t + 1) * 128] = k_scr[t * 128 : (t + 1) * 128, :].T
    some = 16
    offset = lax.rem(z, 2) * 16 + z // 2
    line = lax.broadcasted_iota(jnp.int32, (NX * some, some * BLOCK), 0)
    column = lax.broadcasted_iota(jnp.int32, (NX * some, some * BLOCK), 1)
    wanted = (line % some) * BLOCK + offset + (line // some) * NY
    select = jnp.where(column == wanted, 1.0, 0.0).astype(jnp.bfloat16)
    for c in range(KEY_BLOCKS // some):
        rows = slice(c * some * BLOCK, (c + 1) * some * BLOCK)
        k = jnp.dot(select, k_scr[rows, :], preferred_element_type=jnp.float32).astype(jnp.bfloat16)
        v = jnp.dot(select, v_scr[rows, :HEAD], preferred_element_type=jnp.float32).astype(jnp.bfloat16)
        for x in range(NX):
            pick_ref[x, c * some : (c + 1) * some, :HEAD] = k[x * some : (x + 1) * some]
            pick_ref[x, c * some : (c + 1) * some, HEAD:] = v[x * some : (x + 1) * some]


def attention_kernel(table, q_ref, kpos_ref, *refs):
    pieces, (o_ref, pick_ref, k_scr, kt_scr, v_scr, s_scr, stat) = refs[:9], refs[9:]
    own, r1, r2, r3, l1, l2, l3, r4, l4 = pieces
    every, first, last = range(NY), range(NY // 2), range(NY // 2, NY)
    arrange(
        table,
        [(own, 0, every), (l1, 1, every), (l2, 2, every), (l3, 3, every), (r4, 4, first), (l4, 4, last)]
        + [(r3, 5, every), (r2, 6, every), (r1, 7, every)],
        k_scr,
        kt_scr,
        v_scr,
        pick_ref,
    )
    lane = lax.broadcasted_iota(jnp.int32, (ROWS, 128), 1)
    token = lax.broadcasted_iota(jnp.int32, (BLOCK, CHUNK), 0)

    def one_group(i, carry):
        low, high = table[AT_LOW + i], table[AT_HIGH + i]
        blocks = [table[AT_ORDER + i * JOINED + u] for u in range(JOINED)]
        ids = [table[AT_ID + i * JOINED + u] for u in range(JOINED)]

        def finish(u, out, total, top):
            place = pl.ds(pl.multiple_of(blocks[u] % 2 * ROWS, ROWS), ROWS)
            o_ref[blocks[u] // 2, place, :] = out.astype(jnp.bfloat16)
            old = jnp.where(lane == blocks[u], top, stat[...])
            stat[...] = jnp.where(lane == blocks[u] + Q_BLOCKS, total, old)

        def work(n):
            q = jnp.concatenate([q_ref[blocks[u]] for u in range(JOINED)], axis=0)
            tops = [None] * (JOINED * GROUP)
            for c in range(n):
                start = pl.multiple_of((low + c) * CHUNK, CHUNK)
                s = jnp.dot(q, kt_scr[:, pl.ds(start, CHUNK)], preferred_element_type=jnp.float32)
                kpos = kpos_ref[pl.ds(low + c, 1), :]
                for u in range(JOINED):
                    distance = (ids[u] * BLOCK + token) - kpos
                    bias = jnp.where((distance >= 0) & (distance < WINDOW), 0.0, NEG)
                    for g in range(GROUP):
                        r = u * GROUP + g
                        part = s[r * BLOCK : (r + 1) * BLOCK] + bias
                        s_scr[c, r * BLOCK : (r + 1) * BLOCK, :] = part
                        wide = jnp.maximum(part[:, :128], part[:, 128:])
                        tops[r] = wide if tops[r] is None else jnp.maximum(tops[r], wide)
            top = jnp.max(jnp.concatenate(tops, axis=0), axis=1, keepdims=True) * SCALE
            top = jnp.broadcast_to(top, (JOINED * ROWS, 128))
            twice = jnp.concatenate([top, top], axis=1)
            acc = None
            for c in range(n):
                start = pl.multiple_of((low + c) * CHUNK, CHUNK)
                p = jnp.exp2(s_scr[c] * SCALE - twice).astype(jnp.bfloat16)
                part = jnp.dot(p, v_scr[pl.ds(start, CHUNK), :], preferred_element_type=jnp.float32)
                acc = part if acc is None else acc + part
            for u in range(JOINED):
                rows = slice(u * ROWS, (u + 1) * ROWS)
                finish(u, acc[rows, :HEAD] / acc[rows, HEAD:], acc[rows, HEAD:], top[rows])

        @pl.when(high <= low)
        def _():
            nothing = jnp.zeros((ROWS, 128), jnp.float32)
            for u in range(JOINED):
                finish(u, nothing, nothing, nothing + NEG)

        for n in range(1, KEYS // CHUNK + 1):
            pl.when(high - low == n)(functools.partial(work, n))
        return carry

    stat[...] = jnp.zeros((ROWS, 128), jnp.float32)
    lax.fori_loop(0, Q_BLOCKS // JOINED, one_group, 0)
    turned = stat[...].T
    for d in range(PLANE):
        value = jnp.concatenate(
            [turned[2 * d : 2 * d + 2], turned[Q_BLOCKS + 2 * d : Q_BLOCKS + 2 * d + 2]], axis=0
        )
        first = value.astype(jnp.bfloat16).astype(jnp.float32)
        second = (value - first).astype(jnp.bfloat16).astype(jnp.float32)
        third = value - first - second
        rows = jnp.concatenate([first, second, third, jnp.zeros_like(first)], axis=0)
        o_ref[d, 2 * ROWS :, :] = rows.astype(jnp.bfloat16)


def combine_kernel(heads, blocks, length, m_ref, o_ref):
    values = []
    for d in range(PLANE):
        rows = m_ref[d, 2 * ROWS :, :].astype(jnp.float32)
        values.append(rows[0:4] + rows[4:8] + rows[8:12])
    weights = [None] * PLANE
    for y in range(NY):
        sources = [x * NY + y for x in range(NX)]
        top = values[sources[0]][0:2]
        for d in sources[1:]:
            top = jnp.maximum(top, values[d][0:2])
        parts = [jnp.exp2(values[d][0:2] - top) * values[d][2:4] for d in sources]
        total = parts[0] + parts[1] + parts[2] + parts[3]
        for d, part in zip(sources, parts):
            weights[d] = part / total
    matrix = jnp.concatenate(weights + [jnp.zeros((128 - Q_BLOCKS, 128), jnp.float32)], axis=0).T
    token = lax.broadcasted_iota(jnp.int32, (ROWS, HEAD), 0) % BLOCK
    for y in range(NY):
        for j in range(2):
            out = jnp.zeros((ROWS, HEAD), jnp.float32)
            for x in range(NX):
                d = x * NY + y
                weight = matrix[:, 2 * d + j : 2 * d + j + 1]
                out += weight * m_ref[d, j * ROWS : (j + 1) * ROWS, :].astype(jnp.float32)
            out = jnp.where(blocks[j] * BLOCK + token < length[0], out, 0.0).astype(jnp.bfloat16)
            for g in range(GROUP):
                column = pl.multiple_of((heads[y] * GROUP + g) * HEAD, HEAD)
                o_ref[j * BLOCK : (j + 1) * BLOCK, pl.ds(column, HEAD)] = out[g * BLOCK : (g + 1) * BLOCK]


def ranks(ids):
    return jnp.sum(ids[..., None, :] < ids[..., :, None], axis=-1, dtype=jnp.int32)


def placed(values, rank):
    places = jnp.arange(values.shape[-1], dtype=jnp.int32)
    return jnp.sum(jnp.where(rank[..., None, :] == places[:, None], values[..., None, :], 0), axis=-1, dtype=jnp.int32)


def body(query, rotated_key_value, lengths, block_map, segment_head):
    place = lax.axis_index("blk")
    z, x, y = place // 16, (place // 4) % 4, place % 4
    y_groups = [[4 * g + i for i in range(4)] for g in range(N_BLK // 4)]
    x_groups = [[16 * a + 4 * i + c for i in range(4)] for a in range(NZ) for c in range(NY)]
    planes = [[16 * a + i for i in range(16)] for a in range(NZ)]

    def move(value, target):
        return lax.ppermute(value, "blk", [(s, target(s // 16, (s // 4) % 4, s % 4)) for s in range(N_BLK)])

    def index(zz, xx, yy):
        return (zz % NZ) * 16 + xx * 4 + yy

    def exchange(value, groups):
        return lax.all_to_all(value, "blk", 0, 0, axis_index_groups=groups, tiled=True)

    kv = pl.pallas_call(
        split_kv_kernel,
        out_shape=(jax.ShapeDtypeStruct((128, HEAD), jnp.bfloat16),) * NY,
        in_specs=[SMEM, VMEM],
        out_specs=(VMEM,) * NY,
        name="split_kv",
    )(segment_head, rotated_key_value.reshape(128, KEY_VALUE_HEADS * HEAD))
    line = [kv[0]] + [move(kv[k], lambda a, b, c, k=k: index(a, b, c ^ k)) for k in range(1, NY)]
    own = jnp.concatenate(line, axis=0)
    right = lambda v: move(v, lambda a, b, c: index(a + 1, b, c))
    left = lambda v: move(v, lambda a, b, c: index(a - 1, b, c))
    r1, l1 = right(own), left(own)
    q = pl.pallas_call(
        split_q_kernel,
        out_shape=jax.ShapeDtypeStruct((PLANE, 2 * ROWS, HEAD), jnp.bfloat16),
        in_specs=[SMEM, VMEM],
        out_specs=VMEM,
        name="split_q",
    )(segment_head, query.reshape(2 * BLOCK, QUERY_HEADS * HEAD))
    q = exchange(q, planes).reshape(Q_BLOCKS, ROWS, HEAD)
    r2, l2 = right(r1), left(l1)
    r3, l3 = right(r2), left(l2)
    half = own.shape[0] // 2
    r4, l4 = right(r3[:half]), left(l3[half:])

    ids = block_map.reshape(NZ, NX, NY, 2).transpose(1, 0, 2, 3).reshape(NX, KEY_BLOCKS)
    rank = ranks(ids)
    ordered = placed(ids, rank)
    mine = lax.dynamic_index_in_dim(ordered, x, 0, keepdims=False)
    my_rank = lax.dynamic_index_in_dim(rank, x, 0, keepdims=False)
    q_ids = lax.dynamic_slice_in_dim(block_map, z * Q_BLOCKS, Q_BLOCKS)
    q_rank = ranks(q_ids)
    q_order = placed(jnp.arange(Q_BLOCKS, dtype=jnp.int32), q_rank)
    q_sorted = placed(q_ids, q_rank)
    grouped = q_sorted.reshape(Q_BLOCKS // JOINED, JOINED)
    lows = jnp.sum(mine[None, :] < grouped[:, :1] - WINDOW // BLOCK, axis=1, dtype=jnp.int32) // CHUNK_BLOCKS
    highs = jnp.sum(mine[None, :] <= grouped[:, -1:], axis=1, dtype=jnp.int32)
    highs = (highs + CHUNK_BLOCKS - 1) // CHUNK_BLOCKS
    table = jnp.concatenate([my_rank, q_order, q_sorted, lows, highs])
    kpos = mine[:, None] * BLOCK + jnp.arange(BLOCK, dtype=jnp.int32)[None, :]
    kpos = kpos.reshape(KEYS // CHUNK, CHUNK)

    out, pick = pl.pallas_call(
        attention_kernel,
        out_shape=(
            jax.ShapeDtypeStruct((PLANE, MESSAGE, HEAD), jnp.bfloat16),
            jax.ShapeDtypeStruct((NX, KEY_BLOCKS, 2 * HEAD), jnp.bfloat16),
        ),
        in_specs=[SMEM] + [VMEM] * 11,
        out_specs=(VMEM, VMEM),
        scratch_shapes=[
            pltpu.VMEM((KEYS, HEAD), jnp.bfloat16),
            pltpu.VMEM((HEAD, KEYS), jnp.bfloat16),
            pltpu.VMEM((KEYS, 2 * HEAD), jnp.bfloat16),
            pltpu.VMEM((KEYS // CHUNK, JOINED * ROWS, CHUNK), jnp.float32),
            pltpu.VMEM((ROWS, 128), jnp.float32),
        ],
        compiler_params=PARAMS,
        cost_estimate=pl.CostEstimate(flops=3_000_000_000, bytes_accessed=4_000_000, transcendentals=5_000_000),
        name="attention",
    )(table, q, kpos, own, r1, r2, r3, l1, l2, l3, r4, l4)
    out = exchange(out, planes)
    offset = (z % 2) * 16 + z // 2

    pick = exchange(pick, x_groups).reshape(BLOCKS, 2 * HEAD)
    blocks = jnp.arange(BLOCKS, dtype=jnp.int32)
    position = blocks * BLOCK + offset + 4 * x
    choose = (ordered.reshape(1, BLOCKS) == blocks[:, None]) & (position < lengths[0])[:, None]
    cache = jnp.dot(choose.astype(jnp.bfloat16), pick, preferred_element_type=jnp.float32).astype(jnp.bfloat16)
    cache = move(cache, lambda a, b, c: index(2 * c + a % 2, b, a // 2))
    cache = cache.reshape(BLOCKS, 2, HEAD).transpose(1, 0, 2)[None, :, None]

    my_blocks = lax.dynamic_slice_in_dim(block_map, 2 * place, 2)
    attended = pl.pallas_call(
        combine_kernel,
        out_shape=jax.ShapeDtypeStruct((2 * BLOCK, QUERY_HEADS * HEAD), jnp.bfloat16),
        in_specs=[SMEM] * 3 + [VMEM],
        out_specs=VMEM,
        name="combine",
    )(segment_head, my_blocks, lengths, out)
    return attended.reshape(1, 2 * BLOCK, QUERY_HEADS * HEAD), cache


def solution(mesh):
    return jax.shard_map(
        body,
        mesh=mesh,
        in_specs=(P("req", "blk", None), P("req", None, "blk", None), P("req"), P(), P()),
        out_specs=(P("req", "blk", None), P("req", None, "blk", None, None)),
        check_vma=False,
    )
```

```python
import functools

import jax
import jax.numpy as jnp
from jax import lax
from jax.experimental import pallas as pl
from jax.experimental.pallas import tpu as pltpu
from jax.sharding import PartitionSpec as P

QUERY_HEADS = 16
KEY_VALUE_HEADS = 4
GROUP = QUERY_HEADS // KEY_VALUE_HEADS
HEAD = 128
WINDOW = 4096
BLOCK = 32
BLOCKS = 256
NZ, NX, NY = 8, 4, 4
N_BLK = NZ * NX * NY
PLANE = NX * NY
KEY_BLOCKS = 2 * NZ * NY
Q_BLOCKS = 2 * PLANE
ROWS = GROUP * BLOCK
KEYS = KEY_BLOCKS * BLOCK
JOINED = 4
CHUNK_BLOCKS = 8
CHUNK = CHUNK_BLOCKS * BLOCK
MESSAGE = 2 * ROWS + 16
SCALE = HEAD**-0.5 * 1.4426950408889634
NEG = -1e30
AT_ORDER = KEY_BLOCKS
AT_ID = AT_ORDER + Q_BLOCKS
AT_LOW = AT_ID + Q_BLOCKS
AT_HIGH = AT_LOW + Q_BLOCKS // JOINED

SMEM = pl.BlockSpec(memory_space=pltpu.SMEM)
VMEM = pl.BlockSpec(memory_space=pltpu.VMEM)
PARAMS = pltpu.CompilerParams(vmem_limit_bytes=40 * 1024 * 1024)


def split_kv_kernel(heads, kv_ref, *o_refs):
    y = lax.rem(lax.axis_index("blk"), NY)
    for k in range(NY):
        o_refs[k][...] = kv_ref[:, pl.ds(pl.multiple_of(heads[y ^ k] * HEAD, HEAD), HEAD)]


def split_q_kernel(heads, q_ref, o_ref):
    for y in range(NY):
        for g in range(GROUP):
            column = pl.multiple_of((heads[y] * GROUP + g) * HEAD, HEAD)
            for j in range(2):
                tile = q_ref[j * BLOCK : (j + 1) * BLOCK, pl.ds(column, HEAD)]
                for x in range(NX):
                    o_ref[x * NY + y, j * ROWS + g * BLOCK : j * ROWS + (g + 1) * BLOCK] = tile


def arrange(table, pieces, k_scr, kt_scr, v_scr):
    place = lax.axis_index("blk")
    z, y = place // PLANE, lax.rem(place, NY)
    v_scr[:, HEAD:] = jnp.ones((KEYS, HEAD), jnp.bfloat16)
    for piece, zrel, lines in pieces:
        for at, line in enumerate(lines):
            for j in range(2):
                source = (lax.rem(z + zrel, NZ) * NY + (y ^ line)) * 2 + j
                row = pl.multiple_of(table[source] * BLOCK, BLOCK)
                k_scr[pl.ds(row, BLOCK), :] = piece[at * 128 + j * BLOCK : at * 128 + (j + 1) * BLOCK, :]
                v_scr[pl.ds(row, BLOCK), :HEAD] = piece[at * 128 + 64 + j * BLOCK : at * 128 + 64 + (j + 1) * BLOCK, :]
    for t in range(KEYS // 128):
        kt_scr[:, t * 128 : (t + 1) * 128] = k_scr[t * 128 : (t + 1) * 128, :].T


def pick_kernel(*refs):
    own, r1, r2, r3, l1, l2, l3, r4, l4 = refs[:9]
    o_refs = refs[9:]
    place = lax.axis_index("blk")
    z, x = place // PLANE, lax.rem(place // NY, NX)

    def select(lines, rows):
        count = 2 * NX * lines * 2
        out = lax.broadcasted_iota(jnp.int32, (count, rows), 0)
        column = lax.broadcasted_iota(jnp.int32, (count, rows), 1)
        half, k, line, j = out // (NX * lines * 2), out // (lines * 2) % NX, out // 2 % lines, out % 2
        offset = lax.rem(z, 2) * 16 + (x ^ k) * NY + z // 2
        wanted = line * 128 + half * 64 + j * BLOCK + offset
        return jnp.where(column == wanted, 1.0, 0.0).astype(jnp.bfloat16)

    whole, part = select(NY, 512), select(NY // 2, 256)
    picked = [jnp.dot(whole, piece[...], preferred_element_type=jnp.float32) for piece in (own, l1, l2, l3)]
    picked.append([jnp.dot(part, piece[...], preferred_element_type=jnp.float32) for piece in (r4, l4)])
    picked += [jnp.dot(whole, piece[...], preferred_element_type=jnp.float32) for piece in (r3, r2, r1)]
    for k in range(NX):
        for half in range(2):
            rows = []
            for piece in picked:
                if isinstance(piece, list):
                    at = (half * NX + k) * 4
                    rows += [piece[0][at : at + 4], piece[1][at : at + 4]]
                else:
                    at = (half * NX + k) * 8
                    rows.append(piece[at : at + 8])
            o_refs[k][:, half * HEAD : (half + 1) * HEAD] = jnp.concatenate(rows, axis=0).astype(jnp.bfloat16)


def attention_kernel(table, q_ref, kpos_ref, *refs):
    pieces, (o_ref, k_scr, kt_scr, v_scr, s_scr, stat) = refs[:9], refs[9:]
    own, r1, r2, r3, l1, l2, l3, r4, l4 = pieces
    every, first, last = range(NY), range(NY // 2), range(NY // 2, NY)
    arrange(
        table,
        [(own, 0, every), (l1, 1, every), (l2, 2, every), (l3, 3, every), (r4, 4, first), (l4, 4, last)]
        + [(r3, 5, every), (r2, 6, every), (r1, 7, every)],
        k_scr,
        kt_scr,
        v_scr,
    )
    lane = lax.broadcasted_iota(jnp.int32, (ROWS, 128), 1)
    token = lax.broadcasted_iota(jnp.int32, (BLOCK, CHUNK), 0)

    def one_group(i, carry):
        low, high = table[AT_LOW + i], table[AT_HIGH + i]
        blocks = [table[AT_ORDER + i * JOINED + u] for u in range(JOINED)]
        ids = [table[AT_ID + i * JOINED + u] for u in range(JOINED)]

        def finish(u, out, total, top):
            place = pl.ds(pl.multiple_of(blocks[u] % 2 * ROWS, ROWS), ROWS)
            o_ref[blocks[u] // 2, place, :] = out.astype(jnp.bfloat16)
            old = jnp.where(lane == blocks[u], top, stat[...])
            stat[...] = jnp.where(lane == blocks[u] + Q_BLOCKS, total, old)

        def work(n):
            q = jnp.concatenate([q_ref[blocks[u]] for u in range(JOINED)], axis=0)
            tops = [None] * (JOINED * GROUP)
            for c in range(n):
                start = pl.multiple_of((low + c) * CHUNK, CHUNK)
                s = jnp.dot(q, kt_scr[:, pl.ds(start, CHUNK)], preferred_element_type=jnp.float32)
                kpos = kpos_ref[pl.ds(low + c, 1), :]
                for u in range(JOINED):
                    distance = (ids[u] * BLOCK + token) - kpos
                    bias = jnp.where((distance >= 0) & (distance < WINDOW), 0.0, NEG)
                    for g in range(GROUP):
                        r = u * GROUP + g
                        part = s[r * BLOCK : (r + 1) * BLOCK] + bias
                        s_scr[c, r * BLOCK : (r + 1) * BLOCK, :] = part
                        wide = jnp.maximum(part[:, :128], part[:, 128:])
                        tops[r] = wide if tops[r] is None else jnp.maximum(tops[r], wide)
            top = jnp.max(jnp.concatenate(tops, axis=0), axis=1, keepdims=True) * SCALE
            top = jnp.broadcast_to(top, (JOINED * ROWS, 128))
            twice = jnp.concatenate([top, top], axis=1)
            acc = None
            for c in range(n):
                start = pl.multiple_of((low + c) * CHUNK, CHUNK)
                p = jnp.exp2(s_scr[c] * SCALE - twice).astype(jnp.bfloat16)
                part = jnp.dot(p, v_scr[pl.ds(start, CHUNK), :], preferred_element_type=jnp.float32)
                acc = part if acc is None else acc + part
            for u in range(JOINED):
                rows = slice(u * ROWS, (u + 1) * ROWS)
                finish(u, acc[rows, :HEAD] / acc[rows, HEAD:], acc[rows, HEAD:], top[rows])

        @pl.when(high <= low)
        def _():
            nothing = jnp.zeros((ROWS, 128), jnp.float32)
            for u in range(JOINED):
                finish(u, nothing, nothing, nothing + NEG)

        for n in range(1, KEYS // CHUNK + 1):
            pl.when(high - low == n)(functools.partial(work, n))
        return carry

    stat[...] = jnp.zeros((ROWS, 128), jnp.float32)
    lax.fori_loop(0, Q_BLOCKS // JOINED, one_group, 0)
    turned = stat[...].T
    for d in range(PLANE):
        value = jnp.concatenate(
            [turned[2 * d : 2 * d + 2], turned[Q_BLOCKS + 2 * d : Q_BLOCKS + 2 * d + 2]], axis=0
        )
        first = value.astype(jnp.bfloat16).astype(jnp.float32)
        second = (value - first).astype(jnp.bfloat16).astype(jnp.float32)
        third = value - first - second
        rows = jnp.concatenate([first, second, third, jnp.zeros_like(first)], axis=0)
        o_ref[d, 2 * ROWS :, :] = rows.astype(jnp.bfloat16)


def combine_kernel(heads, blocks, length, m_ref, o_ref):
    values = []
    for d in range(PLANE):
        rows = m_ref[d, 2 * ROWS :, :].astype(jnp.float32)
        values.append(rows[0:4] + rows[4:8] + rows[8:12])
    weights = [None] * PLANE
    for y in range(NY):
        sources = [x * NY + y for x in range(NX)]
        top = values[sources[0]][0:2]
        for d in sources[1:]:
            top = jnp.maximum(top, values[d][0:2])
        parts = [jnp.exp2(values[d][0:2] - top) * values[d][2:4] for d in sources]
        total = parts[0] + parts[1] + parts[2] + parts[3]
        for d, part in zip(sources, parts):
            weights[d] = part / total
    matrix = jnp.concatenate(weights + [jnp.zeros((128 - Q_BLOCKS, 128), jnp.float32)], axis=0).T
    token = lax.broadcasted_iota(jnp.int32, (ROWS, HEAD), 0) % BLOCK
    for y in range(NY):
        for j in range(2):
            out = jnp.zeros((ROWS, HEAD), jnp.float32)
            for x in range(NX):
                d = x * NY + y
                weight = matrix[:, 2 * d + j : 2 * d + j + 1]
                out += weight * m_ref[d, j * ROWS : (j + 1) * ROWS, :].astype(jnp.float32)
            out = jnp.where(blocks[j] * BLOCK + token < length[0], out, 0.0).astype(jnp.bfloat16)
            for g in range(GROUP):
                column = pl.multiple_of((heads[y] * GROUP + g) * HEAD, HEAD)
                o_ref[j * BLOCK : (j + 1) * BLOCK, pl.ds(column, HEAD)] = out[g * BLOCK : (g + 1) * BLOCK]


def ranks(ids):
    return jnp.sum(ids[..., None, :] < ids[..., :, None], axis=-1, dtype=jnp.int32)


def placed(values, rank):
    places = jnp.arange(values.shape[-1], dtype=jnp.int32)
    return jnp.sum(jnp.where(rank[..., None, :] == places[:, None], values[..., None, :], 0), axis=-1, dtype=jnp.int32)


def body(query, rotated_key_value, lengths, block_map, segment_head):
    place = lax.axis_index("blk")
    z, x, y = place // 16, (place // 4) % 4, place % 4
    y_groups = [[4 * g + i for i in range(4)] for g in range(N_BLK // 4)]
    x_groups = [[16 * a + 4 * i + c for i in range(4)] for a in range(NZ) for c in range(NY)]
    planes = [[16 * a + i for i in range(16)] for a in range(NZ)]

    def move(value, target):
        return lax.ppermute(value, "blk", [(s, target(s // 16, (s // 4) % 4, s % 4)) for s in range(N_BLK)])

    def index(zz, xx, yy):
        return (zz % NZ) * 16 + xx * 4 + yy

    def exchange(value, groups):
        return lax.all_to_all(value, "blk", 0, 0, axis_index_groups=groups, tiled=True)

    kv = pl.pallas_call(
        split_kv_kernel,
        out_shape=(jax.ShapeDtypeStruct((128, HEAD), jnp.bfloat16),) * NY,
        in_specs=[SMEM, VMEM],
        out_specs=(VMEM,) * NY,
        name="split_kv",
    )(segment_head, rotated_key_value.reshape(128, KEY_VALUE_HEADS * HEAD))
    line = [kv[0]] + [move(kv[k], lambda a, b, c, k=k: index(a, b, c ^ k)) for k in range(1, NY)]
    own = jnp.concatenate(line, axis=0)
    shift = lambda v, d: move(v, lambda a, b, c: index(a + d, b, c))
    r1, l1 = shift(own, 1), shift(own, -1)
    r2, l2 = shift(own, 2), shift(own, -2)
    q = pl.pallas_call(
        split_q_kernel,
        out_shape=jax.ShapeDtypeStruct((PLANE, 2 * ROWS, HEAD), jnp.bfloat16),
        in_specs=[SMEM, VMEM],
        out_specs=VMEM,
        name="split_q",
    )(segment_head, query.reshape(2 * BLOCK, QUERY_HEADS * HEAD))
    q, _ = lax.optimization_barrier((q, (r1, l1, r2, l2)))
    q = exchange(q, planes).reshape(Q_BLOCKS, ROWS, HEAD)
    r3, l3 = shift(r1, 2), shift(l1, -2)
    half = own.shape[0] // 2
    r4, l4 = shift(r2[:half], 2), shift(l2[half:], -2)

    ids = block_map.reshape(NZ, NX, NY, 2).transpose(1, 0, 2, 3).reshape(NX, KEY_BLOCKS)
    rank = ranks(ids)
    ordered = placed(ids, rank)
    mine = lax.dynamic_index_in_dim(ordered, x, 0, keepdims=False)
    my_rank = lax.dynamic_index_in_dim(rank, x, 0, keepdims=False)
    q_ids = lax.dynamic_slice_in_dim(block_map, z * Q_BLOCKS, Q_BLOCKS)
    q_rank = ranks(q_ids)
    q_order = placed(jnp.arange(Q_BLOCKS, dtype=jnp.int32), q_rank)
    q_sorted = placed(q_ids, q_rank)
    grouped = q_sorted.reshape(Q_BLOCKS // JOINED, JOINED)
    lows = jnp.sum(mine[None, :] < grouped[:, :1] - WINDOW // BLOCK, axis=1, dtype=jnp.int32) // CHUNK_BLOCKS
    highs = jnp.sum(mine[None, :] <= grouped[:, -1:], axis=1, dtype=jnp.int32)
    highs = (highs + CHUNK_BLOCKS - 1) // CHUNK_BLOCKS
    table = jnp.concatenate([my_rank, q_order, q_sorted, lows, highs])
    kpos = mine[:, None] * BLOCK + jnp.arange(BLOCK, dtype=jnp.int32)[None, :]
    kpos = kpos.reshape(KEYS // CHUNK, CHUNK)

    pieces = (own, r1, r2, r3, l1, l2, l3, r4, l4)
    partial = pl.pallas_call(
        attention_kernel,
        out_shape=jax.ShapeDtypeStruct((PLANE, MESSAGE, HEAD), jnp.bfloat16),
        in_specs=[SMEM] + [VMEM] * 11,
        out_specs=VMEM,
        scratch_shapes=[
            pltpu.VMEM((KEYS, HEAD), jnp.bfloat16),
            pltpu.VMEM((HEAD, KEYS), jnp.bfloat16),
            pltpu.VMEM((KEYS, 2 * HEAD), jnp.bfloat16),
            pltpu.VMEM((KEYS // CHUNK, JOINED * ROWS, CHUNK), jnp.float32),
            pltpu.VMEM((ROWS, 128), jnp.float32),
        ],
        compiler_params=PARAMS,
        cost_estimate=pl.CostEstimate(flops=3_000_000_000, bytes_accessed=4_000_000, transcendentals=5_000_000),
        name="attention",
    )(table, q, kpos, *pieces)
    out = exchange(partial, planes)

    pieces, _ = lax.optimization_barrier((pieces, partial))
    picked = pl.pallas_call(
        pick_kernel,
        out_shape=(jax.ShapeDtypeStruct((KEY_BLOCKS, 2 * HEAD), jnp.bfloat16),) * NX,
        in_specs=[VMEM] * 9,
        out_specs=(VMEM,) * NX,
        cost_estimate=pl.CostEstimate(flops=20_000_000, bytes_accessed=1_200_000, transcendentals=0),
        name="pick",
    )(*pieces)
    picked = jnp.concatenate(
        [move(picked[k], lambda a, b, c, k=k: index(2 * c + a % 2, b ^ k, a // 2)) for k in range(NX)], axis=0
    )
    blocks = jnp.arange(BLOCKS, dtype=jnp.int32)
    stored = jnp.sum(jnp.where(block_map[None, :] == blocks[:, None], blocks[None, :], 0), axis=1, dtype=jnp.int32)
    from_z, from_y = 2 * y + z % 2, z // 2
    row = ((stored // 8 % NX) ^ x) * KEY_BLOCKS + (stored // 32 - from_z) % NZ * 8
    row = row + ((stored // 2 % NY) ^ from_y) * 2 + stored % 2
    position = blocks * BLOCK + place % BLOCK
    choose = (row[:, None] == blocks[None, :]) & (position < lengths[0])[:, None]
    cache = jnp.dot(choose.astype(jnp.bfloat16), picked, preferred_element_type=jnp.float32).astype(jnp.bfloat16)
    cache = cache.reshape(BLOCKS, 2, HEAD).transpose(1, 0, 2)[None, :, None]

    my_blocks = lax.dynamic_slice_in_dim(block_map, 2 * place, 2)
    attended = pl.pallas_call(
        combine_kernel,
        out_shape=jax.ShapeDtypeStruct((2 * BLOCK, QUERY_HEADS * HEAD), jnp.bfloat16),
        in_specs=[SMEM] * 3 + [VMEM],
        out_specs=VMEM,
        name="combine",
    )(segment_head, my_blocks, lengths, out)
    return attended.reshape(1, 2 * BLOCK, QUERY_HEADS * HEAD), cache


def solution(mesh):
    return jax.shard_map(
        body,
        mesh=mesh,
        in_specs=(P("req", "blk", None), P("req", None, "blk", None), P("req"), P(), P()),
        out_specs=(P("req", "blk", None), P("req", None, "blk", None, None)),
        check_vma=False,
    )
```

```python
import functools

import jax
import jax.numpy as jnp
from jax import lax
from jax.experimental import pallas as pl
from jax.experimental.pallas import tpu as pltpu
from jax.sharding import PartitionSpec as P

QUERY_HEADS = 16
KEY_VALUE_HEADS = 4
GROUP = QUERY_HEADS // KEY_VALUE_HEADS
HEAD = 128
WINDOW = 4096
BLOCK = 32
BLOCKS = 256
NZ, NX, NY = 8, 4, 4
N_BLK = NZ * NX * NY
PLANE = NX * NY
KEY_BLOCKS = 2 * NZ * NY
Q_BLOCKS = 2 * PLANE
ROWS = GROUP * BLOCK
KEYS = KEY_BLOCKS * BLOCK
JOINED = 4
CHUNK_BLOCKS = 8
CHUNK = CHUNK_BLOCKS * BLOCK
MESSAGE = 2 * ROWS + 16
SCALE = HEAD**-0.5 * 1.4426950408889634
NEG = -1e30
AT_ORDER = KEY_BLOCKS
AT_ID = AT_ORDER + Q_BLOCKS
AT_LOW = AT_ID + Q_BLOCKS
AT_HIGH = AT_LOW + Q_BLOCKS // JOINED

SMEM = pl.BlockSpec(memory_space=pltpu.SMEM)
VMEM = pl.BlockSpec(memory_space=pltpu.VMEM)
PARAMS = pltpu.CompilerParams(vmem_limit_bytes=24 * 1024 * 1024)
SMALL = pltpu.CompilerParams(vmem_limit_bytes=8 * 1024 * 1024)


def split_kv_kernel(heads, kv_ref, *o_refs):
    y = lax.rem(lax.axis_index("blk"), NY)
    for k in range(NY):
        o_refs[k][...] = kv_ref[:, pl.ds(pl.multiple_of(heads[y ^ k] * HEAD, HEAD), HEAD)]


def split_q_kernel(heads, q_ref, o_ref):
    for y in range(NY):
        for g in range(GROUP):
            column = pl.multiple_of((heads[y] * GROUP + g) * HEAD, HEAD)
            for j in range(2):
                tile = q_ref[j * BLOCK : (j + 1) * BLOCK, pl.ds(column, HEAD)]
                for x in range(NX):
                    o_ref[x * NY + y, j * ROWS + g * BLOCK : j * ROWS + (g + 1) * BLOCK] = tile


def arrange(table, pieces, k_scr, kt_scr, v_scr):
    place = lax.axis_index("blk")
    z, y = place // PLANE, lax.rem(place, NY)
    v_scr[:, HEAD:] = jnp.ones((KEYS, HEAD), jnp.bfloat16)
    for piece, zrel, lines in pieces:
        for at, line in enumerate(lines):
            for j in range(2):
                source = (lax.rem(z + zrel, NZ) * NY + (y ^ line)) * 2 + j
                row = pl.multiple_of(table[source] * BLOCK, BLOCK)
                k_scr[pl.ds(row, BLOCK), :] = piece[at * 128 + j * BLOCK : at * 128 + (j + 1) * BLOCK, :]
                v_scr[pl.ds(row, BLOCK), :HEAD] = piece[at * 128 + 64 + j * BLOCK : at * 128 + 64 + (j + 1) * BLOCK, :]
    for t in range(KEYS // 128):
        kt_scr[:, t * 128 : (t + 1) * 128] = k_scr[t * 128 : (t + 1) * 128, :].T


def pick_kernel(*refs):
    own, r1, r2, r3, l1, l2, l3, r4, l4 = refs[:9]
    o_ref = refs[9]
    place = lax.axis_index("blk")
    z, x = place // PLANE, lax.rem(place // NY, NX)

    def select(lines, rows):
        count = 2 * NX * lines * 2
        out = lax.broadcasted_iota(jnp.int32, (count, rows), 0)
        column = lax.broadcasted_iota(jnp.int32, (count, rows), 1)
        half, k, line, j = out // (NX * lines * 2), out // (lines * 2) % NX, out // 2 % lines, out % 2
        offset = lax.rem(z, 2) * 16 + (x ^ k) * NY + z // 2
        wanted = line * 128 + half * 64 + j * BLOCK + offset
        return jnp.where(column == wanted, 1.0, 0.0).astype(jnp.bfloat16)

    whole, part = select(NY, 512), select(NY // 2, 256)
    picked = [jnp.dot(whole, piece[...], preferred_element_type=jnp.float32) for piece in (own, l1, l2, l3)]
    picked.append([jnp.dot(part, piece[...], preferred_element_type=jnp.float32) for piece in (r4, l4)])
    picked += [jnp.dot(whole, piece[...], preferred_element_type=jnp.float32) for piece in (r3, r2, r1)]
    for k in range(NX):
        for half in range(2):
            rows = []
            for piece in picked:
                if isinstance(piece, list):
                    at = (half * NX + k) * 4
                    rows += [piece[0][at : at + 4], piece[1][at : at + 4]]
                else:
                    at = (half * NX + k) * 8
                    rows.append(piece[at : at + 8])
            o_ref[k, :, half * HEAD : (half + 1) * HEAD] = jnp.concatenate(rows, axis=0).astype(jnp.bfloat16)


def attention_kernel(table, q_ref, kpos_ref, *refs):
    pieces, (o_ref, k_scr, kt_scr, v_scr, s_scr, stat) = refs[:9], refs[9:]
    own, r1, r2, r3, l1, l2, l3, r4, l4 = pieces
    every, first, last = range(NY), range(NY // 2), range(NY // 2, NY)
    arrange(
        table,
        [(own, 0, every), (l1, 1, every), (l2, 2, every), (l3, 3, every), (r4, 4, first), (l4, 4, last)]
        + [(r3, 5, every), (r2, 6, every), (r1, 7, every)],
        k_scr,
        kt_scr,
        v_scr,
    )
    lane = lax.broadcasted_iota(jnp.int32, (ROWS, 128), 1)
    token = lax.broadcasted_iota(jnp.int32, (BLOCK, CHUNK), 0)

    def one_group(i, carry):
        low, high = table[AT_LOW + i], table[AT_HIGH + i]
        blocks = [table[AT_ORDER + i * JOINED + u] for u in range(JOINED)]
        ids = [table[AT_ID + i * JOINED + u] for u in range(JOINED)]

        def finish(u, out, total, top):
            place = pl.ds(pl.multiple_of(blocks[u] % 2 * ROWS, ROWS), ROWS)
            o_ref[blocks[u] // 2, place, :] = out.astype(jnp.bfloat16)
            old = jnp.where(lane == blocks[u], top, stat[...])
            stat[...] = jnp.where(lane == blocks[u] + Q_BLOCKS, total, old)

        def work(n):
            q = jnp.concatenate([q_ref[blocks[u]] for u in range(JOINED)], axis=0)
            tops = [None] * (JOINED * GROUP)
            for c in range(n):
                start = pl.multiple_of((low + c) * CHUNK, CHUNK)
                s = jnp.dot(q, kt_scr[:, pl.ds(start, CHUNK)], preferred_element_type=jnp.float32)
                kpos = kpos_ref[pl.ds(low + c, 1), :]
                for u in range(JOINED):
                    distance = (ids[u] * BLOCK + token) - kpos
                    bias = jnp.where((distance >= 0) & (distance < WINDOW), 0.0, NEG)
                    for g in range(GROUP):
                        r = u * GROUP + g
                        part = s[r * BLOCK : (r + 1) * BLOCK] + bias
                        s_scr[c, r * BLOCK : (r + 1) * BLOCK, :] = part
                        wide = jnp.maximum(part[:, :128], part[:, 128:])
                        tops[r] = wide if tops[r] is None else jnp.maximum(tops[r], wide)
            top = jnp.max(jnp.concatenate(tops, axis=0), axis=1, keepdims=True) * SCALE
            top = jnp.broadcast_to(top, (JOINED * ROWS, 128))
            twice = jnp.concatenate([top, top], axis=1)
            acc = None
            for c in range(n):
                start = pl.multiple_of((low + c) * CHUNK, CHUNK)
                p = jnp.exp2(s_scr[c] * SCALE - twice).astype(jnp.bfloat16)
                part = jnp.dot(p, v_scr[pl.ds(start, CHUNK), :], preferred_element_type=jnp.float32)
                acc = part if acc is None else acc + part
            for u in range(JOINED):
                rows = slice(u * ROWS, (u + 1) * ROWS)
                finish(u, acc[rows, :HEAD] / acc[rows, HEAD:], acc[rows, HEAD:], top[rows])

        @pl.when(high <= low)
        def _():
            nothing = jnp.zeros((ROWS, 128), jnp.float32)
            for u in range(JOINED):
                finish(u, nothing, nothing, nothing + NEG)

        for n in range(1, KEYS // CHUNK + 1):
            pl.when(high - low == n)(functools.partial(work, n))
        return carry

    stat[...] = jnp.zeros((ROWS, 128), jnp.float32)
    lax.fori_loop(0, Q_BLOCKS // JOINED, one_group, 0)
    turned = stat[...].T
    for d in range(PLANE):
        value = jnp.concatenate(
            [turned[2 * d : 2 * d + 2], turned[Q_BLOCKS + 2 * d : Q_BLOCKS + 2 * d + 2]], axis=0
        )
        first = value.astype(jnp.bfloat16).astype(jnp.float32)
        second = (value - first).astype(jnp.bfloat16).astype(jnp.float32)
        third = value - first - second
        rows = jnp.concatenate([first, second, third, jnp.zeros_like(first)], axis=0)
        o_ref[d, 2 * ROWS :, :] = rows.astype(jnp.bfloat16)


def combine_kernel(heads, blocks, length, m_ref, o_ref):
    values = []
    for d in range(PLANE):
        rows = m_ref[d, 2 * ROWS :, :].astype(jnp.float32)
        values.append(rows[0:4] + rows[4:8] + rows[8:12])
    weights = [None] * PLANE
    for y in range(NY):
        sources = [x * NY + y for x in range(NX)]
        top = values[sources[0]][0:2]
        for d in sources[1:]:
            top = jnp.maximum(top, values[d][0:2])
        parts = [jnp.exp2(values[d][0:2] - top) * values[d][2:4] for d in sources]
        total = parts[0] + parts[1] + parts[2] + parts[3]
        for d, part in zip(sources, parts):
            weights[d] = part / total
    matrix = jnp.concatenate(weights + [jnp.zeros((128 - Q_BLOCKS, 128), jnp.float32)], axis=0).T
    token = lax.broadcasted_iota(jnp.int32, (ROWS, HEAD), 0) % BLOCK
    for y in range(NY):
        for j in range(2):
            out = jnp.zeros((ROWS, HEAD), jnp.float32)
            for x in range(NX):
                d = x * NY + y
                weight = matrix[:, 2 * d + j : 2 * d + j + 1]
                out += weight * m_ref[d, j * ROWS : (j + 1) * ROWS, :].astype(jnp.float32)
            out = jnp.where(blocks[j] * BLOCK + token < length[0], out, 0.0).astype(jnp.bfloat16)
            for g in range(GROUP):
                column = pl.multiple_of((heads[y] * GROUP + g) * HEAD, HEAD)
                o_ref[j * BLOCK : (j + 1) * BLOCK, pl.ds(column, HEAD)] = out[g * BLOCK : (g + 1) * BLOCK]


def ranks(ids):
    return jnp.sum(ids[..., None, :] < ids[..., :, None], axis=-1, dtype=jnp.int32)


def placed(values, rank):
    places = jnp.arange(values.shape[-1], dtype=jnp.int32)
    return jnp.sum(jnp.where(rank[..., None, :] == places[:, None], values[..., None, :], 0), axis=-1, dtype=jnp.int32)


def body(query, rotated_key_value, lengths, block_map, segment_head):
    place = lax.axis_index("blk")
    z, x, y = place // 16, (place // 4) % 4, place % 4
    y_groups = [[4 * g + i for i in range(4)] for g in range(N_BLK // 4)]
    x_groups = [[16 * a + 4 * i + c for i in range(4)] for a in range(NZ) for c in range(NY)]
    planes = [[16 * a + i for i in range(16)] for a in range(NZ)]

    def move(value, target):
        return lax.ppermute(value, "blk", [(s, target(s // 16, (s // 4) % 4, s % 4)) for s in range(N_BLK)])

    def index(zz, xx, yy):
        return (zz % NZ) * 16 + xx * 4 + yy

    def exchange(value, groups):
        return lax.all_to_all(value, "blk", 0, 0, axis_index_groups=groups, tiled=True)

    kv = pl.pallas_call(
        split_kv_kernel,
        out_shape=(jax.ShapeDtypeStruct((128, HEAD), jnp.bfloat16),) * NY,
        in_specs=[SMEM, VMEM],
        out_specs=(VMEM,) * NY,
        compiler_params=SMALL,
        name="split_kv",
    )(segment_head, rotated_key_value.reshape(128, KEY_VALUE_HEADS * HEAD))
    line = [kv[0]] + [move(kv[k], lambda a, b, c, k=k: index(a, b, c ^ k)) for k in range(1, NY)]
    own = jnp.concatenate(line, axis=0)
    right = lambda v: move(v, lambda a, b, c: index(a + 1, b, c))
    left = lambda v: move(v, lambda a, b, c: index(a - 1, b, c))
    r1, l1 = right(own), left(own)
    q = pl.pallas_call(
        split_q_kernel,
        out_shape=jax.ShapeDtypeStruct((PLANE, 2 * ROWS, HEAD), jnp.bfloat16),
        in_specs=[SMEM, VMEM],
        out_specs=VMEM,
        compiler_params=SMALL,
        name="split_q",
    )(segment_head, query.reshape(2 * BLOCK, QUERY_HEADS * HEAD))
    q = exchange(q, planes).reshape(Q_BLOCKS, ROWS, HEAD)
    r2, l2 = right(r1), left(l1)
    r3, l3 = right(r2), left(l2)
    half = own.shape[0] // 2
    r4, l4 = right(r3[:half]), left(l3[half:])

    ids = block_map.reshape(NZ, NX, NY, 2).transpose(1, 0, 2, 3).reshape(NX, KEY_BLOCKS)
    rank = ranks(ids)
    ordered = placed(ids, rank)
    mine = lax.dynamic_index_in_dim(ordered, x, 0, keepdims=False)
    my_rank = lax.dynamic_index_in_dim(rank, x, 0, keepdims=False)
    q_ids = lax.dynamic_slice_in_dim(block_map, z * Q_BLOCKS, Q_BLOCKS)
    q_rank = ranks(q_ids)
    q_order = placed(jnp.arange(Q_BLOCKS, dtype=jnp.int32), q_rank)
    q_sorted = placed(q_ids, q_rank)
    grouped = q_sorted.reshape(Q_BLOCKS // JOINED, JOINED)
    lows = jnp.sum(mine[None, :] < grouped[:, :1] - WINDOW // BLOCK, axis=1, dtype=jnp.int32) // CHUNK_BLOCKS
    highs = jnp.sum(mine[None, :] <= grouped[:, -1:], axis=1, dtype=jnp.int32)
    highs = (highs + CHUNK_BLOCKS - 1) // CHUNK_BLOCKS
    table = jnp.concatenate([my_rank, q_order, q_sorted, lows, highs])
    kpos = mine[:, None] * BLOCK + jnp.arange(BLOCK, dtype=jnp.int32)[None, :]
    kpos = kpos.reshape(KEYS // CHUNK, CHUNK)

    pieces = (own, r1, r2, r3, l1, l2, l3, r4, l4)
    picked = pl.pallas_call(
        pick_kernel,
        out_shape=jax.ShapeDtypeStruct((NX, KEY_BLOCKS, 2 * HEAD), jnp.bfloat16),
        in_specs=[VMEM] * 9,
        out_specs=VMEM,
        cost_estimate=pl.CostEstimate(flops=20_000_000, bytes_accessed=1_200_000, transcendentals=0),
        compiler_params=SMALL,
        name="pick",
    )(*pieces)
    picked = move(picked, lambda a, b, c: index(2 * c + a % 2, b, a // 2))
    partial = pl.pallas_call(
        attention_kernel,
        out_shape=jax.ShapeDtypeStruct((PLANE, MESSAGE, HEAD), jnp.bfloat16),
        in_specs=[SMEM] + [VMEM] * 11,
        out_specs=VMEM,
        scratch_shapes=[
            pltpu.VMEM((KEYS, HEAD), jnp.bfloat16),
            pltpu.VMEM((HEAD, KEYS), jnp.bfloat16),
            pltpu.VMEM((KEYS, 2 * HEAD), jnp.bfloat16),
            pltpu.VMEM((KEYS // CHUNK, JOINED * ROWS, CHUNK), jnp.float32),
            pltpu.VMEM((ROWS, 128), jnp.float32),
        ],
        compiler_params=PARAMS,
        cost_estimate=pl.CostEstimate(flops=3_000_000_000, bytes_accessed=4_000_000, transcendentals=5_000_000),
        name="attention",
    )(table, q, kpos, *pieces)
    partial, picked = lax.optimization_barrier((partial, picked))
    out = exchange(partial, planes)

    picked = jnp.concatenate(
        [picked[0]] + [move(picked[k], lambda a, b, c, k=k: index(a, b ^ k, c)) for k in range(1, NX)], axis=0
    )
    blocks = jnp.arange(BLOCKS, dtype=jnp.int32)
    stored = jnp.sum(jnp.where(block_map[None, :] == blocks[:, None], blocks[None, :], 0), axis=1, dtype=jnp.int32)
    from_z, from_y = 2 * y + z % 2, z // 2
    row = ((stored // 8 % NX) ^ x) * KEY_BLOCKS + (stored // 32 - from_z) % NZ * 8
    row = row + ((stored // 2 % NY) ^ from_y) * 2 + stored % 2
    position = blocks * BLOCK + place % BLOCK
    choose = (row[:, None] == blocks[None, :]) & (position < lengths[0])[:, None]
    cache = jnp.dot(choose.astype(jnp.bfloat16), picked, preferred_element_type=jnp.float32).astype(jnp.bfloat16)
    cache = cache.reshape(BLOCKS, 2, HEAD).transpose(1, 0, 2)[None, :, None]

    my_blocks = lax.dynamic_slice_in_dim(block_map, 2 * place, 2)
    attended = pl.pallas_call(
        combine_kernel,
        out_shape=jax.ShapeDtypeStruct((2 * BLOCK, QUERY_HEADS * HEAD), jnp.bfloat16),
        in_specs=[SMEM] * 3 + [VMEM],
        out_specs=VMEM,
        compiler_params=SMALL,
        name="combine",
    )(segment_head, my_blocks, lengths, out)
    return attended.reshape(1, 2 * BLOCK, QUERY_HEADS * HEAD), cache


def solution(mesh):
    return jax.shard_map(
        body,
        mesh=mesh,
        in_specs=(P("req", "blk", None), P("req", None, "blk", None), P("req"), P(), P()),
        out_specs=(P("req", "blk", None), P("req", None, "blk", None, None)),
        check_vma=False,
    )
```

```python
import functools

import jax
import jax.numpy as jnp
from jax import lax
from jax.experimental import pallas as pl
from jax.experimental.pallas import tpu as pltpu
from jax.sharding import PartitionSpec as P

QUERY_HEADS = 16
KEY_VALUE_HEADS = 4
GROUP = QUERY_HEADS // KEY_VALUE_HEADS
HEAD = 128
WINDOW = 4096
BLOCK = 32
BLOCKS = 256
NZ, NX, NY = 8, 4, 4
N_BLK = NZ * NX * NY
PLANE = NX * NY
KEY_BLOCKS = 2 * NZ * NY
Q_BLOCKS = 2 * PLANE
ROWS = GROUP * BLOCK
KEYS = KEY_BLOCKS * BLOCK
JOINED = 4
CHUNK_BLOCKS = 8
CHUNK = CHUNK_BLOCKS * BLOCK
MESSAGE = 2 * ROWS + 16
SCALE = HEAD**-0.5 * 1.4426950408889634
NEG = -1e30
AT_ORDER = KEY_BLOCKS
AT_ID = AT_ORDER + Q_BLOCKS
AT_LOW = AT_ID + Q_BLOCKS
AT_HIGH = AT_LOW + Q_BLOCKS // JOINED

SMEM = pl.BlockSpec(memory_space=pltpu.SMEM)
VMEM = pl.BlockSpec(memory_space=pltpu.VMEM)
PARAMS = pltpu.CompilerParams(vmem_limit_bytes=24 * 1024 * 1024)
SMALL = pltpu.CompilerParams(vmem_limit_bytes=8 * 1024 * 1024)


def split_kv_kernel(heads, kv_ref, *o_refs):
    y = lax.rem(lax.axis_index("blk"), NY)
    for k in range(NY):
        o_refs[k][...] = kv_ref[:, pl.ds(pl.multiple_of(heads[y ^ k] * HEAD, HEAD), HEAD)]


def split_q_kernel(heads, q_ref, *o_refs):
    y = lax.rem(lax.axis_index("blk"), NY)
    for k in range(NY):
        for g in range(GROUP):
            column = pl.multiple_of((heads[y ^ k] * GROUP + g) * HEAD, HEAD)
            for j in range(2):
                rows = slice(j * ROWS + g * BLOCK, j * ROWS + (g + 1) * BLOCK)
                o_refs[k][rows, :] = q_ref[j * BLOCK : (j + 1) * BLOCK, pl.ds(column, HEAD)]


def arrange(table, pieces, k_scr, kt_scr, v_scr):
    place = lax.axis_index("blk")
    z, y = place // PLANE, lax.rem(place, NY)
    v_scr[:, HEAD:] = jnp.ones((KEYS, HEAD), jnp.bfloat16)
    for piece, zrel, lines in pieces:
        for at, line in enumerate(lines):
            for j in range(2):
                source = (lax.rem(z + zrel, NZ) * NY + (y ^ line)) * 2 + j
                row = pl.multiple_of(table[source] * BLOCK, BLOCK)
                k_scr[pl.ds(row, BLOCK), :] = piece[at * 128 + j * BLOCK : at * 128 + (j + 1) * BLOCK, :]
                v_scr[pl.ds(row, BLOCK), :HEAD] = piece[at * 128 + 64 + j * BLOCK : at * 128 + 64 + (j + 1) * BLOCK, :]
    for t in range(KEYS // 128):
        kt_scr[:, t * 128 : (t + 1) * 128] = k_scr[t * 128 : (t + 1) * 128, :].T


def pick_kernel(*refs):
    own, r1, r2, r3, l1, l2, l3, r4, l4 = refs[:9]
    o_ref = refs[9]
    place = lax.axis_index("blk")
    z, x = place // PLANE, lax.rem(place // NY, NX)

    def select(lines, rows):
        count = 2 * NX * lines * 2
        out = lax.broadcasted_iota(jnp.int32, (count, rows), 0)
        column = lax.broadcasted_iota(jnp.int32, (count, rows), 1)
        half, k, line, j = out // (NX * lines * 2), out // (lines * 2) % NX, out // 2 % lines, out % 2
        offset = lax.rem(z, 2) * 16 + (x ^ k) * NY + z // 2
        wanted = line * 128 + half * 64 + j * BLOCK + offset
        return jnp.where(column == wanted, 1.0, 0.0).astype(jnp.bfloat16)

    whole, part = select(NY, 512), select(NY // 2, 256)
    picked = [jnp.dot(whole, piece[...], preferred_element_type=jnp.float32) for piece in (own, l1, l2, l3)]
    picked.append([jnp.dot(part, piece[...], preferred_element_type=jnp.float32) for piece in (r4, l4)])
    picked += [jnp.dot(whole, piece[...], preferred_element_type=jnp.float32) for piece in (r3, r2, r1)]
    for k in range(NX):
        for half in range(2):
            rows = []
            for piece in picked:
                if isinstance(piece, list):
                    at = (half * NX + k) * 4
                    rows += [piece[0][at : at + 4], piece[1][at : at + 4]]
                else:
                    at = (half * NX + k) * 8
                    rows.append(piece[at : at + 8])
            o_ref[k, :, half * HEAD : (half + 1) * HEAD] = jnp.concatenate(rows, axis=0).astype(jnp.bfloat16)


def attention_kernel(table, q_ref, kpos_ref, *refs):
    pieces, (o_ref, k_scr, kt_scr, v_scr, s_scr, stat) = refs[:9], refs[9:]
    own, r1, r2, r3, l1, l2, l3, r4, l4 = pieces
    every, first, last = range(NY), range(NY // 2), range(NY // 2, NY)
    arrange(
        table,
        [(own, 0, every), (l1, 1, every), (l2, 2, every), (l3, 3, every), (r4, 4, first), (l4, 4, last)]
        + [(r3, 5, every), (r2, 6, every), (r1, 7, every)],
        k_scr,
        kt_scr,
        v_scr,
    )
    mine = 2 * lax.rem(lax.axis_index("blk"), PLANE)
    lane = lax.broadcasted_iota(jnp.int32, (ROWS, 128), 1)
    token = lax.broadcasted_iota(jnp.int32, (BLOCK, CHUNK), 0)

    def one_group(i, carry):
        low, high = table[AT_LOW + i], table[AT_HIGH + i]
        blocks = [table[AT_ORDER + i * JOINED + u] for u in range(JOINED)]
        ids = [table[AT_ID + i * JOINED + u] for u in range(JOINED)]

        def finish(u, out, total, top):
            place = pl.ds(pl.multiple_of(blocks[u] % 2 * ROWS, ROWS), ROWS)
            o_ref[blocks[u] // 2, place, :] = out.astype(jnp.bfloat16)
            old = jnp.where(lane == blocks[u], top, stat[...])
            stat[...] = jnp.where(lane == blocks[u] + Q_BLOCKS, total, old)

        def work(n):
            q = jnp.concatenate([q_ref[blocks[u] ^ mine] for u in range(JOINED)], axis=0)
            tops = [None] * (JOINED * GROUP)
            for c in range(n):
                start = pl.multiple_of((low + c) * CHUNK, CHUNK)
                s = jnp.dot(q, kt_scr[:, pl.ds(start, CHUNK)], preferred_element_type=jnp.float32)
                kpos = kpos_ref[pl.ds(low + c, 1), :]
                for u in range(JOINED):
                    distance = (ids[u] * BLOCK + token) - kpos
                    bias = jnp.where((distance >= 0) & (distance < WINDOW), 0.0, NEG)
                    for g in range(GROUP):
                        r = u * GROUP + g
                        part = s[r * BLOCK : (r + 1) * BLOCK] + bias
                        s_scr[c, r * BLOCK : (r + 1) * BLOCK, :] = part
                        wide = jnp.maximum(part[:, :128], part[:, 128:])
                        tops[r] = wide if tops[r] is None else jnp.maximum(tops[r], wide)
            top = jnp.max(jnp.concatenate(tops, axis=0), axis=1, keepdims=True) * SCALE
            top = jnp.broadcast_to(top, (JOINED * ROWS, 128))
            twice = jnp.concatenate([top, top], axis=1)
            acc = None
            for c in range(n):
                start = pl.multiple_of((low + c) * CHUNK, CHUNK)
                p = jnp.exp2(s_scr[c] * SCALE - twice).astype(jnp.bfloat16)
                part = jnp.dot(p, v_scr[pl.ds(start, CHUNK), :], preferred_element_type=jnp.float32)
                acc = part if acc is None else acc + part
            for u in range(JOINED):
                rows = slice(u * ROWS, (u + 1) * ROWS)
                finish(u, acc[rows, :HEAD] / acc[rows, HEAD:], acc[rows, HEAD:], top[rows])

        @pl.when(high <= low)
        def _():
            nothing = jnp.zeros((ROWS, 128), jnp.float32)
            for u in range(JOINED):
                finish(u, nothing, nothing, nothing + NEG)

        for n in range(1, KEYS // CHUNK + 1):
            pl.when(high - low == n)(functools.partial(work, n))
        return carry

    stat[...] = jnp.zeros((ROWS, 128), jnp.float32)
    lax.fori_loop(0, Q_BLOCKS // JOINED, one_group, 0)
    turned = stat[...].T
    for d in range(PLANE):
        value = jnp.concatenate(
            [turned[2 * d : 2 * d + 2], turned[Q_BLOCKS + 2 * d : Q_BLOCKS + 2 * d + 2]], axis=0
        )
        first = value.astype(jnp.bfloat16).astype(jnp.float32)
        second = (value - first).astype(jnp.bfloat16).astype(jnp.float32)
        third = value - first - second
        rows = jnp.concatenate([first, second, third, jnp.zeros_like(first)], axis=0)
        o_ref[d, 2 * ROWS :, :] = rows.astype(jnp.bfloat16)


def combine_kernel(heads, blocks, length, m_ref, o_ref):
    values = []
    for d in range(PLANE):
        rows = m_ref[d, 2 * ROWS :, :].astype(jnp.float32)
        values.append(rows[0:4] + rows[4:8] + rows[8:12])
    weights = [None] * PLANE
    for y in range(NY):
        sources = [x * NY + y for x in range(NX)]
        top = values[sources[0]][0:2]
        for d in sources[1:]:
            top = jnp.maximum(top, values[d][0:2])
        parts = [jnp.exp2(values[d][0:2] - top) * values[d][2:4] for d in sources]
        total = parts[0] + parts[1] + parts[2] + parts[3]
        for d, part in zip(sources, parts):
            weights[d] = part / total
    matrix = jnp.concatenate(weights + [jnp.zeros((128 - Q_BLOCKS, 128), jnp.float32)], axis=0).T
    token = lax.broadcasted_iota(jnp.int32, (ROWS, HEAD), 0) % BLOCK
    for y in range(NY):
        for j in range(2):
            out = jnp.zeros((ROWS, HEAD), jnp.float32)
            for x in range(NX):
                d = x * NY + y
                weight = matrix[:, 2 * d + j : 2 * d + j + 1]
                out += weight * m_ref[d, j * ROWS : (j + 1) * ROWS, :].astype(jnp.float32)
            out = jnp.where(blocks[j] * BLOCK + token < length[0], out, 0.0).astype(jnp.bfloat16)
            for g in range(GROUP):
                column = pl.multiple_of((heads[y] * GROUP + g) * HEAD, HEAD)
                o_ref[j * BLOCK : (j + 1) * BLOCK, pl.ds(column, HEAD)] = out[g * BLOCK : (g + 1) * BLOCK]


def ranks(ids):
    return jnp.sum(ids[..., None, :] < ids[..., :, None], axis=-1, dtype=jnp.int32)


def placed(values, rank):
    places = jnp.arange(values.shape[-1], dtype=jnp.int32)
    return jnp.sum(jnp.where(rank[..., None, :] == places[:, None], values[..., None, :], 0), axis=-1, dtype=jnp.int32)


def body(query, rotated_key_value, lengths, block_map, segment_head):
    place = lax.axis_index("blk")
    z, x, y = place // 16, (place // 4) % 4, place % 4
    y_groups = [[4 * g + i for i in range(4)] for g in range(N_BLK // 4)]
    x_groups = [[16 * a + 4 * i + c for i in range(4)] for a in range(NZ) for c in range(NY)]
    planes = [[16 * a + i for i in range(16)] for a in range(NZ)]

    def move(value, target):
        return lax.ppermute(value, "blk", [(s, target(s // 16, (s // 4) % 4, s % 4)) for s in range(N_BLK)])

    def index(zz, xx, yy):
        return (zz % NZ) * 16 + xx * 4 + yy

    def exchange(value, groups):
        return lax.all_to_all(value, "blk", 0, 0, axis_index_groups=groups, tiled=True)

    kv = pl.pallas_call(
        split_kv_kernel,
        out_shape=(jax.ShapeDtypeStruct((128, HEAD), jnp.bfloat16),) * NY,
        in_specs=[SMEM, VMEM],
        out_specs=(VMEM,) * NY,
        compiler_params=SMALL,
        name="split_kv",
    )(segment_head, rotated_key_value.reshape(128, KEY_VALUE_HEADS * HEAD))
    line = [kv[0]] + [move(kv[k], lambda a, b, c, k=k: index(a, b, c ^ k)) for k in range(1, NY)]
    own = jnp.concatenate(line, axis=0)
    right = lambda v: move(v, lambda a, b, c: index(a + 1, b, c))
    left = lambda v: move(v, lambda a, b, c: index(a - 1, b, c))
    r1, l1 = right(own), left(own)
    qs = pl.pallas_call(
        split_q_kernel,
        out_shape=(jax.ShapeDtypeStruct((2 * ROWS, HEAD), jnp.bfloat16),) * NY,
        in_specs=[SMEM, VMEM],
        out_specs=(VMEM,) * NY,
        compiler_params=SMALL,
        name="split_q",
    )(segment_head, query.reshape(2 * BLOCK, QUERY_HEADS * HEAD))
    qs, _ = lax.optimization_barrier((qs, own))
    q = [qs[0]] + [move(qs[k], lambda a, b, c, k=k: index(a, b, c ^ k)) for k in range(1, NY)]
    q = jnp.concatenate(q, axis=0)
    q = [q] + [move(q, lambda a, b, c, k=k: index(a, b ^ k, c)) for k in range(1, NX)]
    q = jnp.concatenate(q, axis=0).reshape(Q_BLOCKS, ROWS, HEAD)
    r2, l2 = right(r1), left(l1)
    r3, l3 = right(r2), left(l2)
    half = own.shape[0] // 2
    r4, l4 = right(r3[:half]), left(l3[half:])

    ids = block_map.reshape(NZ, NX, NY, 2).transpose(1, 0, 2, 3).reshape(NX, KEY_BLOCKS)
    rank = ranks(ids)
    ordered = placed(ids, rank)
    mine = lax.dynamic_index_in_dim(ordered, x, 0, keepdims=False)
    my_rank = lax.dynamic_index_in_dim(rank, x, 0, keepdims=False)
    q_ids = lax.dynamic_slice_in_dim(block_map, z * Q_BLOCKS, Q_BLOCKS)
    q_rank = ranks(q_ids)
    q_order = placed(jnp.arange(Q_BLOCKS, dtype=jnp.int32), q_rank)
    q_sorted = placed(q_ids, q_rank)
    grouped = q_sorted.reshape(Q_BLOCKS // JOINED, JOINED)
    lows = jnp.sum(mine[None, :] < grouped[:, :1] - WINDOW // BLOCK, axis=1, dtype=jnp.int32) // CHUNK_BLOCKS
    highs = jnp.sum(mine[None, :] <= grouped[:, -1:], axis=1, dtype=jnp.int32)
    highs = (highs + CHUNK_BLOCKS - 1) // CHUNK_BLOCKS
    table = jnp.concatenate([my_rank, q_order, q_sorted, lows, highs])
    kpos = mine[:, None] * BLOCK + jnp.arange(BLOCK, dtype=jnp.int32)[None, :]
    kpos = kpos.reshape(KEYS // CHUNK, CHUNK)

    pieces = (own, r1, r2, r3, l1, l2, l3, r4, l4)
    picked = pl.pallas_call(
        pick_kernel,
        out_shape=jax.ShapeDtypeStruct((NX, KEY_BLOCKS, 2 * HEAD), jnp.bfloat16),
        in_specs=[VMEM] * 9,
        out_specs=VMEM,
        cost_estimate=pl.CostEstimate(flops=20_000_000, bytes_accessed=1_200_000, transcendentals=0),
        compiler_params=SMALL,
        name="pick",
    )(*pieces)
    picked = move(picked, lambda a, b, c: index(2 * c + a % 2, b, a // 2))
    partial = pl.pallas_call(
        attention_kernel,
        out_shape=jax.ShapeDtypeStruct((PLANE, MESSAGE, HEAD), jnp.bfloat16),
        in_specs=[SMEM] + [VMEM] * 11,
        out_specs=VMEM,
        scratch_shapes=[
            pltpu.VMEM((KEYS, HEAD), jnp.bfloat16),
            pltpu.VMEM((HEAD, KEYS), jnp.bfloat16),
            pltpu.VMEM((KEYS, 2 * HEAD), jnp.bfloat16),
            pltpu.VMEM((KEYS // CHUNK, JOINED * ROWS, CHUNK), jnp.float32),
            pltpu.VMEM((ROWS, 128), jnp.float32),
        ],
        compiler_params=PARAMS,
        cost_estimate=pl.CostEstimate(flops=3_000_000_000, bytes_accessed=4_000_000, transcendentals=5_000_000),
        name="attention",
    )(table, q, kpos, *pieces)
    partial, picked = lax.optimization_barrier((partial, picked))
    out = exchange(partial, planes)

    picked = jnp.concatenate(
        [picked[0]] + [move(picked[k], lambda a, b, c, k=k: index(a, b ^ k, c)) for k in range(1, NX)], axis=0
    )
    blocks = jnp.arange(BLOCKS, dtype=jnp.int32)
    stored = jnp.sum(jnp.where(block_map[None, :] == blocks[:, None], blocks[None, :], 0), axis=1, dtype=jnp.int32)
    from_z, from_y = 2 * y + z % 2, z // 2
    row = ((stored // 8 % NX) ^ x) * KEY_BLOCKS + (stored // 32 - from_z) % NZ * 8
    row = row + ((stored // 2 % NY) ^ from_y) * 2 + stored % 2
    position = blocks * BLOCK + place % BLOCK
    choose = (row[:, None] == blocks[None, :]) & (position < lengths[0])[:, None]
    cache = jnp.dot(choose.astype(jnp.bfloat16), picked, preferred_element_type=jnp.float32).astype(jnp.bfloat16)
    cache = cache.reshape(BLOCKS, 2, HEAD).transpose(1, 0, 2)[None, :, None]

    my_blocks = lax.dynamic_slice_in_dim(block_map, 2 * place, 2)
    attended = pl.pallas_call(
        combine_kernel,
        out_shape=jax.ShapeDtypeStruct((2 * BLOCK, QUERY_HEADS * HEAD), jnp.bfloat16),
        in_specs=[SMEM] * 3 + [VMEM],
        out_specs=VMEM,
        compiler_params=SMALL,
        name="combine",
    )(segment_head, my_blocks, lengths, out)
    return attended.reshape(1, 2 * BLOCK, QUERY_HEADS * HEAD), cache


def solution(mesh):
    return jax.shard_map(
        body,
        mesh=mesh,
        in_specs=(P("req", "blk", None), P("req", None, "blk", None), P("req"), P(), P()),
        out_specs=(P("req", "blk", None), P("req", None, "blk", None, None)),
        check_vma=False,
    )
```

```python
import functools

import jax
import jax.numpy as jnp
from jax import lax
from jax.experimental import pallas as pl
from jax.experimental.pallas import tpu as pltpu
from jax.sharding import PartitionSpec as P

QUERY_HEADS = 16
KEY_VALUE_HEADS = 4
GROUP = QUERY_HEADS // KEY_VALUE_HEADS
HEAD = 128
WINDOW = 4096
BLOCK = 32
BLOCKS = 256
NZ, NX, NY = 8, 4, 4
N_BLK = NZ * NX * NY
PLANE = NX * NY
KEY_BLOCKS = 2 * NZ * NY
Q_BLOCKS = 2 * PLANE
ROWS = GROUP * BLOCK
KEYS = KEY_BLOCKS * BLOCK
JOINED = 4
CHUNK_BLOCKS = 8
CHUNK = CHUNK_BLOCKS * BLOCK
MESSAGE = 2 * ROWS + 16
SCALE = HEAD**-0.5 * 1.4426950408889634
NEG = -1e30
AT_ORDER = KEY_BLOCKS
AT_ID = AT_ORDER + Q_BLOCKS
AT_LOW = AT_ID + Q_BLOCKS
AT_HIGH = AT_LOW + Q_BLOCKS // JOINED

SMEM = pl.BlockSpec(memory_space=pltpu.SMEM)
VMEM = pl.BlockSpec(memory_space=pltpu.VMEM)
PARAMS = pltpu.CompilerParams(vmem_limit_bytes=24 * 1024 * 1024)
SMALL = pltpu.CompilerParams(vmem_limit_bytes=8 * 1024 * 1024)


def split_kv_kernel(heads, kv_ref, *o_refs):
    y = lax.rem(lax.axis_index("blk"), NY)
    for k in range(NY):
        o_refs[k][...] = kv_ref[:, pl.ds(pl.multiple_of(heads[y ^ k] * HEAD, HEAD), HEAD)]


def split_q_kernel(heads, q_ref, o_ref):
    for y in range(NY):
        for g in range(GROUP):
            column = pl.multiple_of((heads[y] * GROUP + g) * HEAD, HEAD)
            for j in range(2):
                tile = q_ref[j * BLOCK : (j + 1) * BLOCK, pl.ds(column, HEAD)]
                for x in range(NX):
                    o_ref[x * NY + y, j * ROWS + g * BLOCK : j * ROWS + (g + 1) * BLOCK] = tile


def arrange(table, pieces, k_scr, kt_scr, v_scr):
    place = lax.axis_index("blk")
    z, y = place // PLANE, lax.rem(place, NY)
    v_scr[:, HEAD:] = jnp.ones((KEYS, HEAD), jnp.bfloat16)
    for piece, zrel, lines in pieces:
        for at, line in enumerate(lines):
            for j in range(2):
                source = (lax.rem(z + zrel, NZ) * NY + (y ^ line)) * 2 + j
                row = pl.multiple_of(table[source] * BLOCK, BLOCK)
                k_scr[pl.ds(row, BLOCK), :] = piece[at * 128 + j * BLOCK : at * 128 + (j + 1) * BLOCK, :]
                v_scr[pl.ds(row, BLOCK), :HEAD] = piece[at * 128 + 64 + j * BLOCK : at * 128 + 64 + (j + 1) * BLOCK, :]
    for t in range(KEYS // 128):
        kt_scr[:, t * 128 : (t + 1) * 128] = k_scr[t * 128 : (t + 1) * 128, :].T


def pick_kernel(own, r1, r2, r3, l1, l2, l3, r4, l4, *o_refs):
    place = lax.axis_index("blk")
    z, x, y = place // PLANE, lax.rem(place // NY, NX), lax.rem(place, NY)

    def select(lines, rows):
        blocks = 2 * lines
        out = lax.broadcasted_iota(jnp.int32, (NY * NX * 2 * blocks, rows), 0)
        column = lax.broadcasted_iota(jnp.int32, (NY * NX * 2 * blocks, rows), 1)
        m, k, half, line, j = (
            out // (NX * 2 * blocks),
            out // (2 * blocks) % NX,
            out // blocks % 2,
            out // 2 % lines,
            out % 2,
        )
        offset = lax.rem(z, 2) * 16 + (x ^ k) * NY + (y ^ m)
        wanted = line * 128 + half * 64 + j * BLOCK + offset
        return jnp.where(column == wanted, 1.0, 0.0).astype(jnp.bfloat16)

    whole, part = select(NY, 512), select(NY // 2, 256)
    take = lambda matrix, piece: jnp.dot(matrix, piece[...], preferred_element_type=jnp.float32)
    picked = [take(whole, piece) for piece in (own, l1, l2, l3)]
    picked.append([take(part, piece) for piece in (r4, l4)])
    picked += [take(whole, piece) for piece in (r3, r2, r1)]
    for m in range(NY):
        for k in range(NX):
            for half in range(2):
                rows = []
                for piece in picked:
                    if isinstance(piece, list):
                        at = ((m * NX + k) * 2 + half) * 4
                        rows += [piece[0][at : at + 4], piece[1][at : at + 4]]
                    else:
                        at = ((m * NX + k) * 2 + half) * 8
                        rows.append(piece[at : at + 8])
                rows = jnp.concatenate(rows, axis=0).astype(jnp.bfloat16)
                o_refs[m][k, :, half * HEAD : (half + 1) * HEAD] = rows


def attention_kernel(table, q_ref, kpos_ref, *refs):
    pieces, (o_ref, k_scr, kt_scr, v_scr, s_scr, stat) = refs[:9], refs[9:]
    own, r1, r2, r3, l1, l2, l3, r4, l4 = pieces
    every, first, last = range(NY), range(NY // 2), range(NY // 2, NY)
    arrange(
        table,
        [(own, 0, every), (l1, 1, every), (l2, 2, every), (l3, 3, every), (r4, 4, first), (l4, 4, last)]
        + [(r3, 5, every), (r2, 6, every), (r1, 7, every)],
        k_scr,
        kt_scr,
        v_scr,
    )
    lane = lax.broadcasted_iota(jnp.int32, (ROWS, 128), 1)
    token = lax.broadcasted_iota(jnp.int32, (BLOCK, CHUNK), 0)

    def one_group(i, carry):
        low, high = table[AT_LOW + i], table[AT_HIGH + i]
        blocks = [table[AT_ORDER + i * JOINED + u] for u in range(JOINED)]
        ids = [table[AT_ID + i * JOINED + u] for u in range(JOINED)]

        def finish(u, out, total, top):
            place = pl.ds(pl.multiple_of(blocks[u] % 2 * ROWS, ROWS), ROWS)
            o_ref[blocks[u] // 2, place, :] = out.astype(jnp.bfloat16)
            old = jnp.where(lane == blocks[u], top, stat[...])
            stat[...] = jnp.where(lane == blocks[u] + Q_BLOCKS, total, old)

        def work(n):
            q = jnp.concatenate([q_ref[blocks[u]] for u in range(JOINED)], axis=0)
            tops = [None] * (JOINED * GROUP)
            for c in range(n):
                start = pl.multiple_of((low + c) * CHUNK, CHUNK)
                s = jnp.dot(q, kt_scr[:, pl.ds(start, CHUNK)], preferred_element_type=jnp.float32)
                kpos = kpos_ref[pl.ds(low + c, 1), :]
                for u in range(JOINED):
                    distance = (ids[u] * BLOCK + token) - kpos
                    bias = jnp.where((distance >= 0) & (distance < WINDOW), 0.0, NEG)
                    for g in range(GROUP):
                        r = u * GROUP + g
                        part = s[r * BLOCK : (r + 1) * BLOCK] + bias
                        s_scr[c, r * BLOCK : (r + 1) * BLOCK, :] = part
                        wide = jnp.maximum(part[:, :128], part[:, 128:])
                        tops[r] = wide if tops[r] is None else jnp.maximum(tops[r], wide)
            top = jnp.max(jnp.concatenate(tops, axis=0), axis=1, keepdims=True) * SCALE
            top = jnp.broadcast_to(top, (JOINED * ROWS, 128))
            twice = jnp.concatenate([top, top], axis=1)
            acc = None
            for c in range(n):
                start = pl.multiple_of((low + c) * CHUNK, CHUNK)
                p = jnp.exp2(s_scr[c] * SCALE - twice).astype(jnp.bfloat16)
                part = jnp.dot(p, v_scr[pl.ds(start, CHUNK), :], preferred_element_type=jnp.float32)
                acc = part if acc is None else acc + part
            for u in range(JOINED):
                rows = slice(u * ROWS, (u + 1) * ROWS)
                finish(u, acc[rows, :HEAD] / acc[rows, HEAD:], acc[rows, HEAD:], top[rows])

        @pl.when(high <= low)
        def _():
            nothing = jnp.zeros((ROWS, 128), jnp.float32)
            for u in range(JOINED):
                finish(u, nothing, nothing, nothing + NEG)

        for n in range(1, KEYS // CHUNK + 1):
            pl.when(high - low == n)(functools.partial(work, n))
        return carry

    stat[...] = jnp.zeros((ROWS, 128), jnp.float32)
    lax.fori_loop(0, Q_BLOCKS // JOINED, one_group, 0)
    turned = stat[...].T
    for d in range(PLANE):
        value = jnp.concatenate(
            [turned[2 * d : 2 * d + 2], turned[Q_BLOCKS + 2 * d : Q_BLOCKS + 2 * d + 2]], axis=0
        )
        first = value.astype(jnp.bfloat16).astype(jnp.float32)
        second = (value - first).astype(jnp.bfloat16).astype(jnp.float32)
        third = value - first - second
        rows = jnp.concatenate([first, second, third, jnp.zeros_like(first)], axis=0)
        o_ref[d, 2 * ROWS :, :] = rows.astype(jnp.bfloat16)


def combine_kernel(heads, blocks, length, m_ref, o_ref):
    values = []
    for d in range(PLANE):
        rows = m_ref[d, 2 * ROWS :, :].astype(jnp.float32)
        values.append(rows[0:4] + rows[4:8] + rows[8:12])
    weights = [None] * PLANE
    for y in range(NY):
        sources = [x * NY + y for x in range(NX)]
        top = values[sources[0]][0:2]
        for d in sources[1:]:
            top = jnp.maximum(top, values[d][0:2])
        parts = [jnp.exp2(values[d][0:2] - top) * values[d][2:4] for d in sources]
        total = parts[0] + parts[1] + parts[2] + parts[3]
        for d, part in zip(sources, parts):
            weights[d] = part / total
    matrix = jnp.concatenate(weights + [jnp.zeros((128 - Q_BLOCKS, 128), jnp.float32)], axis=0).T
    token = lax.broadcasted_iota(jnp.int32, (ROWS, HEAD), 0) % BLOCK
    for y in range(NY):
        for j in range(2):
            out = jnp.zeros((ROWS, HEAD), jnp.float32)
            for x in range(NX):
                d = x * NY + y
                weight = matrix[:, 2 * d + j : 2 * d + j + 1]
                out += weight * m_ref[d, j * ROWS : (j + 1) * ROWS, :].astype(jnp.float32)
            out = jnp.where(blocks[j] * BLOCK + token < length[0], out, 0.0).astype(jnp.bfloat16)
            for g in range(GROUP):
                column = pl.multiple_of((heads[y] * GROUP + g) * HEAD, HEAD)
                o_ref[j * BLOCK : (j + 1) * BLOCK, pl.ds(column, HEAD)] = out[g * BLOCK : (g + 1) * BLOCK]


def ranks(ids):
    return jnp.sum(ids[..., None, :] < ids[..., :, None], axis=-1, dtype=jnp.int32)


def placed(values, rank):
    places = jnp.arange(values.shape[-1], dtype=jnp.int32)
    return jnp.sum(jnp.where(rank[..., None, :] == places[:, None], values[..., None, :], 0), axis=-1, dtype=jnp.int32)


def body(query, rotated_key_value, lengths, block_map, segment_head):
    place = lax.axis_index("blk")
    z, x, y = place // 16, (place // 4) % 4, place % 4
    y_groups = [[4 * g + i for i in range(4)] for g in range(N_BLK // 4)]
    x_groups = [[16 * a + 4 * i + c for i in range(4)] for a in range(NZ) for c in range(NY)]
    planes = [[16 * a + i for i in range(16)] for a in range(NZ)]

    def move(value, target):
        return lax.ppermute(value, "blk", [(s, target(s // 16, (s // 4) % 4, s % 4)) for s in range(N_BLK)])

    def index(zz, xx, yy):
        return (zz % NZ) * 16 + xx * 4 + yy

    def exchange(value, groups):
        return lax.all_to_all(value, "blk", 0, 0, axis_index_groups=groups, tiled=True)

    kv = pl.pallas_call(
        split_kv_kernel,
        out_shape=(jax.ShapeDtypeStruct((128, HEAD), jnp.bfloat16),) * NY,
        in_specs=[SMEM, VMEM],
        out_specs=(VMEM,) * NY,
        compiler_params=SMALL,
        name="split_kv",
    )(segment_head, rotated_key_value.reshape(128, KEY_VALUE_HEADS * HEAD))
    line = [kv[0]] + [move(kv[k], lambda a, b, c, k=k: index(a, b, c ^ k)) for k in range(1, NY)]
    own = jnp.concatenate(line, axis=0)
    right = lambda v: move(v, lambda a, b, c: index(a + 1, b, c))
    left = lambda v: move(v, lambda a, b, c: index(a - 1, b, c))
    r1, l1 = right(own), left(own)
    q = pl.pallas_call(
        split_q_kernel,
        out_shape=jax.ShapeDtypeStruct((PLANE, 2 * ROWS, HEAD), jnp.bfloat16),
        in_specs=[SMEM, VMEM],
        out_specs=VMEM,
        compiler_params=SMALL,
        name="split_q",
    )(segment_head, query.reshape(2 * BLOCK, QUERY_HEADS * HEAD))
    q = exchange(q, planes).reshape(Q_BLOCKS, ROWS, HEAD)
    r2, l2 = right(r1), left(l1)
    r3, l3 = right(r2), left(l2)
    half = own.shape[0] // 2
    r4, l4 = right(r3[:half]), left(l3[half:])

    ids = block_map.reshape(NZ, NX, NY, 2).transpose(1, 0, 2, 3).reshape(NX, KEY_BLOCKS)
    rank = ranks(ids)
    ordered = placed(ids, rank)
    mine = lax.dynamic_index_in_dim(ordered, x, 0, keepdims=False)
    my_rank = lax.dynamic_index_in_dim(rank, x, 0, keepdims=False)
    q_ids = lax.dynamic_slice_in_dim(block_map, z * Q_BLOCKS, Q_BLOCKS)
    q_rank = ranks(q_ids)
    q_order = placed(jnp.arange(Q_BLOCKS, dtype=jnp.int32), q_rank)
    q_sorted = placed(q_ids, q_rank)
    grouped = q_sorted.reshape(Q_BLOCKS // JOINED, JOINED)
    lows = jnp.sum(mine[None, :] < grouped[:, :1] - WINDOW // BLOCK, axis=1, dtype=jnp.int32) // CHUNK_BLOCKS
    highs = jnp.sum(mine[None, :] <= grouped[:, -1:], axis=1, dtype=jnp.int32)
    highs = (highs + CHUNK_BLOCKS - 1) // CHUNK_BLOCKS
    table = jnp.concatenate([my_rank, q_order, q_sorted, lows, highs])
    kpos = mine[:, None] * BLOCK + jnp.arange(BLOCK, dtype=jnp.int32)[None, :]
    kpos = kpos.reshape(KEYS // CHUNK, CHUNK)

    pieces = (own, r1, r2, r3, l1, l2, l3, r4, l4)
    picked = pl.pallas_call(
        pick_kernel,
        out_shape=(jax.ShapeDtypeStruct((NX, KEY_BLOCKS, 2 * HEAD), jnp.bfloat16),) * NY,
        in_specs=[VMEM] * 9,
        out_specs=(VMEM,) * NY,
        cost_estimate=pl.CostEstimate(flops=80_000_000, bytes_accessed=1_500_000, transcendentals=0),
        compiler_params=SMALL,
        name="pick",
    )(*pieces)
    kept = [picked[0]]
    for m in range(1, NY):
        pairs = [(index(a, b, a // 2), index(a, b, a // 2 ^ m)) for a in range(NZ) for b in range(NX)]
        kept.append(lax.ppermute(picked[m], "blk", pairs))
    partial = pl.pallas_call(
        attention_kernel,
        out_shape=jax.ShapeDtypeStruct((PLANE, MESSAGE, HEAD), jnp.bfloat16),
        in_specs=[SMEM] + [VMEM] * 11,
        out_specs=VMEM,
        scratch_shapes=[
            pltpu.VMEM((KEYS, HEAD), jnp.bfloat16),
            pltpu.VMEM((HEAD, KEYS), jnp.bfloat16),
            pltpu.VMEM((KEYS, 2 * HEAD), jnp.bfloat16),
            pltpu.VMEM((KEYS // CHUNK, JOINED * ROWS, CHUNK), jnp.float32),
            pltpu.VMEM((ROWS, 128), jnp.float32),
        ],
        compiler_params=PARAMS,
        cost_estimate=pl.CostEstimate(flops=3_000_000_000, bytes_accessed=4_000_000, transcendentals=5_000_000),
        name="attention",
    )(table, q, kpos, *pieces)
    partial, kept = lax.optimization_barrier((partial, kept))
    out = exchange(partial, planes)

    hops = y ^ (z // 2)
    kept = jnp.where(hops == 0, kept[0], jnp.where(hops == 1, kept[1], jnp.where(hops == 2, kept[2], kept[3])))
    kept = jnp.concatenate(
        [kept[0]] + [move(kept[k], lambda a, b, c, k=k: index(a, b ^ k, c)) for k in range(1, NX)], axis=0
    )
    blocks = jnp.arange(BLOCKS, dtype=jnp.int32)
    stored = jnp.sum(jnp.where(block_map[None, :] == blocks[:, None], blocks[None, :], 0), axis=1, dtype=jnp.int32)
    row = ((stored // 8 % NX) ^ x) * KEY_BLOCKS + (stored // 32 - z) % NZ * 8
    row = row + ((stored // 2 % NY) ^ (z // 2)) * 2 + stored % 2
    position = blocks * BLOCK + place % BLOCK
    choose = (row[:, None] == blocks[None, :]) & (position < lengths[0])[:, None]
    cache = jnp.dot(choose.astype(jnp.bfloat16), kept, preferred_element_type=jnp.float32).astype(jnp.bfloat16)
    cache = cache.reshape(BLOCKS, 2, HEAD).transpose(1, 0, 2)[None, :, None]

    my_blocks = lax.dynamic_slice_in_dim(block_map, 2 * place, 2)
    attended = pl.pallas_call(
        combine_kernel,
        out_shape=jax.ShapeDtypeStruct((2 * BLOCK, QUERY_HEADS * HEAD), jnp.bfloat16),
        in_specs=[SMEM] * 3 + [VMEM],
        out_specs=VMEM,
        compiler_params=SMALL,
        name="combine",
    )(segment_head, my_blocks, lengths, out)
    return attended.reshape(1, 2 * BLOCK, QUERY_HEADS * HEAD), cache


def solution(mesh):
    return jax.shard_map(
        body,
        mesh=mesh,
        in_specs=(P("req", "blk", None), P("req", None, "blk", None), P("req"), P(), P()),
        out_specs=(P("req", "blk", None), P("req", None, "blk", None, None)),
        check_vma=False,
    )
```

```python
import functools

import jax
import jax.numpy as jnp
from jax import lax
from jax.experimental import pallas as pl
from jax.experimental.pallas import tpu as pltpu
from jax.sharding import PartitionSpec as P

QUERY_HEADS = 16
KEY_VALUE_HEADS = 4
GROUP = QUERY_HEADS // KEY_VALUE_HEADS
HEAD = 128
WINDOW = 4096
BLOCK = 32
BLOCKS = 256
NZ, NX, NY = 8, 4, 4
N_BLK = NZ * NX * NY
PLANE = NX * NY
KEY_BLOCKS = 2 * NZ * NY
Q_BLOCKS = 2 * PLANE
ROWS = GROUP * BLOCK
KEYS = KEY_BLOCKS * BLOCK
JOINED = 4
CHUNK_BLOCKS = 8
CHUNK = CHUNK_BLOCKS * BLOCK
MESSAGE = 2 * ROWS + 16
SCALE = HEAD**-0.5 * 1.4426950408889634
NEG = -1e30
AT_ORDER = KEY_BLOCKS
AT_ID = AT_ORDER + Q_BLOCKS
AT_LOW = AT_ID + Q_BLOCKS
AT_HIGH = AT_LOW + Q_BLOCKS // JOINED

SMEM = pl.BlockSpec(memory_space=pltpu.SMEM)
VMEM = pl.BlockSpec(memory_space=pltpu.VMEM)
PARAMS = pltpu.CompilerParams(vmem_limit_bytes=24 * 1024 * 1024)
SMALL = pltpu.CompilerParams(vmem_limit_bytes=8 * 1024 * 1024)


def split_kv_kernel(heads, kv_ref, *o_refs):
    y = lax.rem(lax.axis_index("blk"), NY)
    for k in range(NY):
        o_refs[k][...] = kv_ref[:, pl.ds(pl.multiple_of(heads[y ^ k] * HEAD, HEAD), HEAD)]


def split_q_kernel(heads, q_ref, *o_refs):
    y = lax.rem(lax.axis_index("blk"), NY)
    for k in range(NY):
        for g in range(GROUP):
            column = pl.multiple_of((heads[y ^ k] * GROUP + g) * HEAD, HEAD)
            for j in range(2):
                rows = slice(j * ROWS + g * BLOCK, j * ROWS + (g + 1) * BLOCK)
                o_refs[k][rows, :] = q_ref[j * BLOCK : (j + 1) * BLOCK, pl.ds(column, HEAD)]


def arrange(table, pieces, k_scr, kt_scr, v_scr):
    place = lax.axis_index("blk")
    z, y = place // PLANE, lax.rem(place, NY)
    v_scr[:, HEAD:] = jnp.ones((KEYS, HEAD), jnp.bfloat16)
    for piece, zrel, lines in pieces:
        for at, line in enumerate(lines):
            for j in range(2):
                source = (lax.rem(z + zrel, NZ) * NY + (y ^ line)) * 2 + j
                row = pl.multiple_of(table[source] * BLOCK, BLOCK)
                k_scr[pl.ds(row, BLOCK), :] = piece[at * 128 + j * BLOCK : at * 128 + (j + 1) * BLOCK, :]
                v_scr[pl.ds(row, BLOCK), :HEAD] = piece[at * 128 + 64 + j * BLOCK : at * 128 + 64 + (j + 1) * BLOCK, :]
    for t in range(KEYS // 128):
        kt_scr[:, t * 128 : (t + 1) * 128] = k_scr[t * 128 : (t + 1) * 128, :].T


def pick_kernel(own, r1, r2, r3, l1, l2, l3, r4, l4, *o_refs):
    place = lax.axis_index("blk")
    z, x, y = place // PLANE, lax.rem(place // NY, NX), lax.rem(place, NY)

    def select(lines, rows):
        blocks = 2 * lines
        out = lax.broadcasted_iota(jnp.int32, (NY * NX * 2 * blocks, rows), 0)
        column = lax.broadcasted_iota(jnp.int32, (NY * NX * 2 * blocks, rows), 1)
        m, k, half, line, j = (
            out // (NX * 2 * blocks),
            out // (2 * blocks) % NX,
            out // blocks % 2,
            out // 2 % lines,
            out % 2,
        )
        offset = lax.rem(z, 2) * 16 + (x ^ k) * NY + (y ^ m)
        wanted = line * 128 + half * 64 + j * BLOCK + offset
        return jnp.where(column == wanted, 1.0, 0.0).astype(jnp.bfloat16)

    whole, part = select(NY, 512), select(NY // 2, 256)
    take = lambda matrix, piece: jnp.dot(matrix, piece[...], preferred_element_type=jnp.float32)
    picked = [take(whole, piece) for piece in (own, l1, l2, l3)]
    picked.append([take(part, piece) for piece in (r4, l4)])
    picked += [take(whole, piece) for piece in (r3, r2, r1)]
    for m in range(NY):
        for k in range(NX):
            for half in range(2):
                rows = []
                for piece in picked:
                    if isinstance(piece, list):
                        at = ((m * NX + k) * 2 + half) * 4
                        rows += [piece[0][at : at + 4], piece[1][at : at + 4]]
                    else:
                        at = ((m * NX + k) * 2 + half) * 8
                        rows.append(piece[at : at + 8])
                rows = jnp.concatenate(rows, axis=0).astype(jnp.bfloat16)
                o_refs[m][k, :, half * HEAD : (half + 1) * HEAD] = rows


def attention_kernel(table, q_ref, kpos_ref, *refs):
    pieces, (o_ref, k_scr, kt_scr, v_scr, s_scr, stat) = refs[:9], refs[9:]
    own, r1, r2, r3, l1, l2, l3, r4, l4 = pieces
    every, first, last = range(NY), range(NY // 2), range(NY // 2, NY)
    arrange(
        table,
        [(own, 0, every), (l1, 1, every), (l2, 2, every), (l3, 3, every), (r4, 4, first), (l4, 4, last)]
        + [(r3, 5, every), (r2, 6, every), (r1, 7, every)],
        k_scr,
        kt_scr,
        v_scr,
    )
    mine = 2 * lax.rem(lax.axis_index("blk"), PLANE)
    lane = lax.broadcasted_iota(jnp.int32, (ROWS, 128), 1)
    token = lax.broadcasted_iota(jnp.int32, (BLOCK, CHUNK), 0)

    def one_group(i, carry):
        low, high = table[AT_LOW + i], table[AT_HIGH + i]
        blocks = [table[AT_ORDER + i * JOINED + u] for u in range(JOINED)]
        ids = [table[AT_ID + i * JOINED + u] for u in range(JOINED)]

        def finish(u, out, total, top):
            place = pl.ds(pl.multiple_of(blocks[u] % 2 * ROWS, ROWS), ROWS)
            o_ref[blocks[u] // 2, place, :] = out.astype(jnp.bfloat16)
            old = jnp.where(lane == blocks[u], top, stat[...])
            stat[...] = jnp.where(lane == blocks[u] + Q_BLOCKS, total, old)

        def work(n):
            q = jnp.concatenate([q_ref[blocks[u] ^ mine] for u in range(JOINED)], axis=0)
            tops = [None] * (JOINED * GROUP)
            for c in range(n):
                start = pl.multiple_of((low + c) * CHUNK, CHUNK)
                s = jnp.dot(q, kt_scr[:, pl.ds(start, CHUNK)], preferred_element_type=jnp.float32)
                kpos = kpos_ref[pl.ds(low + c, 1), :]
                for u in range(JOINED):
                    distance = (ids[u] * BLOCK + token) - kpos
                    bias = jnp.where((distance >= 0) & (distance < WINDOW), 0.0, NEG)
                    for g in range(GROUP):
                        r = u * GROUP + g
                        part = s[r * BLOCK : (r + 1) * BLOCK] + bias
                        s_scr[c, r * BLOCK : (r + 1) * BLOCK, :] = part
                        wide = jnp.maximum(part[:, :128], part[:, 128:])
                        tops[r] = wide if tops[r] is None else jnp.maximum(tops[r], wide)
            top = jnp.max(jnp.concatenate(tops, axis=0), axis=1, keepdims=True) * SCALE
            top = jnp.broadcast_to(top, (JOINED * ROWS, 128))
            twice = jnp.concatenate([top, top], axis=1)
            acc = None
            for c in range(n):
                start = pl.multiple_of((low + c) * CHUNK, CHUNK)
                p = jnp.exp2(s_scr[c] * SCALE - twice).astype(jnp.bfloat16)
                part = jnp.dot(p, v_scr[pl.ds(start, CHUNK), :], preferred_element_type=jnp.float32)
                acc = part if acc is None else acc + part
            for u in range(JOINED):
                rows = slice(u * ROWS, (u + 1) * ROWS)
                finish(u, acc[rows, :HEAD] / acc[rows, HEAD:], acc[rows, HEAD:], top[rows])

        @pl.when(high <= low)
        def _():
            nothing = jnp.zeros((ROWS, 128), jnp.float32)
            for u in range(JOINED):
                finish(u, nothing, nothing, nothing + NEG)

        for n in range(1, KEYS // CHUNK + 1):
            pl.when(high - low == n)(functools.partial(work, n))
        return carry

    stat[...] = jnp.zeros((ROWS, 128), jnp.float32)
    lax.fori_loop(0, Q_BLOCKS // JOINED, one_group, 0)
    turned = stat[...].T
    for d in range(PLANE):
        value = jnp.concatenate(
            [turned[2 * d : 2 * d + 2], turned[Q_BLOCKS + 2 * d : Q_BLOCKS + 2 * d + 2]], axis=0
        )
        first = value.astype(jnp.bfloat16).astype(jnp.float32)
        second = (value - first).astype(jnp.bfloat16).astype(jnp.float32)
        third = value - first - second
        rows = jnp.concatenate([first, second, third, jnp.zeros_like(first)], axis=0)
        o_ref[d, 2 * ROWS :, :] = rows.astype(jnp.bfloat16)


def combine_kernel(heads, blocks, length, m_ref, o_ref):
    values = []
    for d in range(PLANE):
        rows = m_ref[d, 2 * ROWS :, :].astype(jnp.float32)
        values.append(rows[0:4] + rows[4:8] + rows[8:12])
    weights = [None] * PLANE
    for y in range(NY):
        sources = [x * NY + y for x in range(NX)]
        top = values[sources[0]][0:2]
        for d in sources[1:]:
            top = jnp.maximum(top, values[d][0:2])
        parts = [jnp.exp2(values[d][0:2] - top) * values[d][2:4] for d in sources]
        total = parts[0] + parts[1] + parts[2] + parts[3]
        for d, part in zip(sources, parts):
            weights[d] = part / total
    matrix = jnp.concatenate(weights + [jnp.zeros((128 - Q_BLOCKS, 128), jnp.float32)], axis=0).T
    token = lax.broadcasted_iota(jnp.int32, (ROWS, HEAD), 0) % BLOCK
    for y in range(NY):
        for j in range(2):
            out = jnp.zeros((ROWS, HEAD), jnp.float32)
            for x in range(NX):
                d = x * NY + y
                weight = matrix[:, 2 * d + j : 2 * d + j + 1]
                out += weight * m_ref[d, j * ROWS : (j + 1) * ROWS, :].astype(jnp.float32)
            out = jnp.where(blocks[j] * BLOCK + token < length[0], out, 0.0).astype(jnp.bfloat16)
            for g in range(GROUP):
                column = pl.multiple_of((heads[y] * GROUP + g) * HEAD, HEAD)
                o_ref[j * BLOCK : (j + 1) * BLOCK, pl.ds(column, HEAD)] = out[g * BLOCK : (g + 1) * BLOCK]


def ranks(ids):
    return jnp.sum(ids[..., None, :] < ids[..., :, None], axis=-1, dtype=jnp.int32)


def placed(values, rank):
    places = jnp.arange(values.shape[-1], dtype=jnp.int32)
    return jnp.sum(jnp.where(rank[..., None, :] == places[:, None], values[..., None, :], 0), axis=-1, dtype=jnp.int32)


def body(query, rotated_key_value, lengths, block_map, segment_head):
    place = lax.axis_index("blk")
    z, x, y = place // 16, (place // 4) % 4, place % 4
    y_groups = [[4 * g + i for i in range(4)] for g in range(N_BLK // 4)]
    x_groups = [[16 * a + 4 * i + c for i in range(4)] for a in range(NZ) for c in range(NY)]
    planes = [[16 * a + i for i in range(16)] for a in range(NZ)]

    def move(value, target):
        return lax.ppermute(value, "blk", [(s, target(s // 16, (s // 4) % 4, s % 4)) for s in range(N_BLK)])

    def index(zz, xx, yy):
        return (zz % NZ) * 16 + xx * 4 + yy

    def exchange(value, groups):
        return lax.all_to_all(value, "blk", 0, 0, axis_index_groups=groups, tiled=True)

    kv = pl.pallas_call(
        split_kv_kernel,
        out_shape=(jax.ShapeDtypeStruct((128, HEAD), jnp.bfloat16),) * NY,
        in_specs=[SMEM, VMEM],
        out_specs=(VMEM,) * NY,
        compiler_params=SMALL,
        name="split_kv",
    )(segment_head, rotated_key_value.reshape(128, KEY_VALUE_HEADS * HEAD))
    line = [kv[0]] + [move(kv[k], lambda a, b, c, k=k: index(a, b, c ^ k)) for k in range(1, NY)]
    own = jnp.concatenate(line, axis=0)
    right = lambda v: move(v, lambda a, b, c: index(a + 1, b, c))
    left = lambda v: move(v, lambda a, b, c: index(a - 1, b, c))
    r1, l1 = right(own), left(own)
    qs = pl.pallas_call(
        split_q_kernel,
        out_shape=(jax.ShapeDtypeStruct((2 * ROWS, HEAD), jnp.bfloat16),) * NY,
        in_specs=[SMEM, VMEM],
        out_specs=(VMEM,) * NY,
        compiler_params=SMALL,
        name="split_q",
    )(segment_head, query.reshape(2 * BLOCK, QUERY_HEADS * HEAD))
    qs, _ = lax.optimization_barrier((qs, own))
    q = [qs[0]] + [move(qs[k], lambda a, b, c, k=k: index(a, b, c ^ k)) for k in range(1, NY)]
    r2, l2 = right(r1), left(l1)
    q = jnp.concatenate(q, axis=0)
    q, _ = lax.optimization_barrier((q, l2))
    q = [q] + [move(q, lambda a, b, c, k=k: index(a, b ^ k, c)) for k in range(1, NX)]
    q = jnp.concatenate(q, axis=0).reshape(Q_BLOCKS, ROWS, HEAD)
    r3, l3 = right(r2), left(l2)
    half = own.shape[0] // 2
    r4, l4 = right(r3[:half]), left(l3[half:])

    ids = block_map.reshape(NZ, NX, NY, 2).transpose(1, 0, 2, 3).reshape(NX, KEY_BLOCKS)
    rank = ranks(ids)
    ordered = placed(ids, rank)
    mine = lax.dynamic_index_in_dim(ordered, x, 0, keepdims=False)
    my_rank = lax.dynamic_index_in_dim(rank, x, 0, keepdims=False)
    q_ids = lax.dynamic_slice_in_dim(block_map, z * Q_BLOCKS, Q_BLOCKS)
    q_rank = ranks(q_ids)
    q_order = placed(jnp.arange(Q_BLOCKS, dtype=jnp.int32), q_rank)
    q_sorted = placed(q_ids, q_rank)
    grouped = q_sorted.reshape(Q_BLOCKS // JOINED, JOINED)
    lows = jnp.sum(mine[None, :] < grouped[:, :1] - WINDOW // BLOCK, axis=1, dtype=jnp.int32) // CHUNK_BLOCKS
    highs = jnp.sum(mine[None, :] <= grouped[:, -1:], axis=1, dtype=jnp.int32)
    highs = (highs + CHUNK_BLOCKS - 1) // CHUNK_BLOCKS
    table = jnp.concatenate([my_rank, q_order, q_sorted, lows, highs])
    kpos = mine[:, None] * BLOCK + jnp.arange(BLOCK, dtype=jnp.int32)[None, :]
    kpos = kpos.reshape(KEYS // CHUNK, CHUNK)

    pieces = (own, r1, r2, r3, l1, l2, l3, r4, l4)
    picked = pl.pallas_call(
        pick_kernel,
        out_shape=(jax.ShapeDtypeStruct((NX, KEY_BLOCKS, 2 * HEAD), jnp.bfloat16),) * NY,
        in_specs=[VMEM] * 9,
        out_specs=(VMEM,) * NY,
        cost_estimate=pl.CostEstimate(flops=80_000_000, bytes_accessed=1_500_000, transcendentals=0),
        compiler_params=SMALL,
        name="pick",
    )(*pieces)
    kept = [picked[0]]
    for m in range(1, NY):
        pairs = [(index(a, b, a // 2), index(a, b, a // 2 ^ m)) for a in range(NZ) for b in range(NX)]
        kept.append(lax.ppermute(picked[m], "blk", pairs))
    partial = pl.pallas_call(
        attention_kernel,
        out_shape=jax.ShapeDtypeStruct((PLANE, MESSAGE, HEAD), jnp.bfloat16),
        in_specs=[SMEM] + [VMEM] * 11,
        out_specs=VMEM,
        scratch_shapes=[
            pltpu.VMEM((KEYS, HEAD), jnp.bfloat16),
            pltpu.VMEM((HEAD, KEYS), jnp.bfloat16),
            pltpu.VMEM((KEYS, 2 * HEAD), jnp.bfloat16),
            pltpu.VMEM((KEYS // CHUNK, JOINED * ROWS, CHUNK), jnp.float32),
            pltpu.VMEM((ROWS, 128), jnp.float32),
        ],
        compiler_params=PARAMS,
        cost_estimate=pl.CostEstimate(flops=3_000_000_000, bytes_accessed=4_000_000, transcendentals=5_000_000),
        name="attention",
    )(table, q, kpos, *pieces)
    partial, kept = lax.optimization_barrier((partial, kept))
    out = exchange(partial, planes)

    hops = y ^ (z // 2)
    kept = jnp.where(hops == 0, kept[0], jnp.where(hops == 1, kept[1], jnp.where(hops == 2, kept[2], kept[3])))
    kept = jnp.concatenate(
        [kept[0]] + [move(kept[k], lambda a, b, c, k=k: index(a, b ^ k, c)) for k in range(1, NX)], axis=0
    )
    blocks = jnp.arange(BLOCKS, dtype=jnp.int32)
    stored = jnp.sum(jnp.where(block_map[None, :] == blocks[:, None], blocks[None, :], 0), axis=1, dtype=jnp.int32)
    row = ((stored // 8 % NX) ^ x) * KEY_BLOCKS + (stored // 32 - z) % NZ * 8
    row = row + ((stored // 2 % NY) ^ (z // 2)) * 2 + stored % 2
    position = blocks * BLOCK + place % BLOCK
    choose = (row[:, None] == blocks[None, :]) & (position < lengths[0])[:, None]
    cache = jnp.dot(choose.astype(jnp.bfloat16), kept, preferred_element_type=jnp.float32).astype(jnp.bfloat16)
    cache = cache.reshape(BLOCKS, 2, HEAD).transpose(1, 0, 2)[None, :, None]

    my_blocks = lax.dynamic_slice_in_dim(block_map, 2 * place, 2)
    attended = pl.pallas_call(
        combine_kernel,
        out_shape=jax.ShapeDtypeStruct((2 * BLOCK, QUERY_HEADS * HEAD), jnp.bfloat16),
        in_specs=[SMEM] * 3 + [VMEM],
        out_specs=VMEM,
        compiler_params=SMALL,
        name="combine",
    )(segment_head, my_blocks, lengths, out)
    return attended.reshape(1, 2 * BLOCK, QUERY_HEADS * HEAD), cache


def solution(mesh):
    return jax.shard_map(
        body,
        mesh=mesh,
        in_specs=(P("req", "blk", None), P("req", None, "blk", None), P("req"), P(), P()),
        out_specs=(P("req", "blk", None), P("req", None, "blk", None, None)),
        check_vma=False,
    )
```

```python
import functools

import jax
import jax.numpy as jnp
from jax import lax
from jax.experimental import pallas as pl
from jax.experimental.pallas import tpu as pltpu
from jax.sharding import PartitionSpec as P

QUERY_HEADS = 16
KEY_VALUE_HEADS = 4
GROUP = QUERY_HEADS // KEY_VALUE_HEADS
HEAD = 128
WINDOW = 4096
BLOCK = 32
BLOCKS = 256
NZ, NX, NY = 8, 4, 4
N_BLK = NZ * NX * NY
PLANE = NX * NY
KEY_BLOCKS = 2 * NZ * NY
Q_BLOCKS = 2 * PLANE
ROWS = GROUP * BLOCK
KEYS = KEY_BLOCKS * BLOCK
JOINED = 4
CHUNK_BLOCKS = 8
CHUNK = CHUNK_BLOCKS * BLOCK
PARTIAL = 2 * ROWS + 16
MESSAGE = PARTIAL + 2 * KEY_BLOCKS
SCALE = HEAD**-0.5 * 1.4426950408889634
NEG = -1e30
AT_ORDER = KEY_BLOCKS
AT_ID = AT_ORDER + Q_BLOCKS
AT_LOW = AT_ID + Q_BLOCKS
AT_HIGH = AT_LOW + Q_BLOCKS // JOINED

SMEM = pl.BlockSpec(memory_space=pltpu.SMEM)
VMEM = pl.BlockSpec(memory_space=pltpu.VMEM)
PARAMS = pltpu.CompilerParams(vmem_limit_bytes=24 * 1024 * 1024)
SMALL = pltpu.CompilerParams(vmem_limit_bytes=8 * 1024 * 1024)


def split_kv_kernel(heads, kv_ref, *o_refs):
    y = lax.rem(lax.axis_index("blk"), NY)
    for k in range(NY):
        o_refs[k][...] = kv_ref[:, pl.ds(pl.multiple_of(heads[y ^ k] * HEAD, HEAD), HEAD)]


def split_q_kernel(heads, q_ref, o_ref):
    for y in range(NY):
        for g in range(GROUP):
            column = pl.multiple_of((heads[y] * GROUP + g) * HEAD, HEAD)
            for j in range(2):
                tile = q_ref[j * BLOCK : (j + 1) * BLOCK, pl.ds(column, HEAD)]
                for x in range(NX):
                    o_ref[x * NY + y, j * ROWS + g * BLOCK : j * ROWS + (g + 1) * BLOCK] = tile


def arrange(table, pieces, k_scr, kt_scr, v_scr):
    place = lax.axis_index("blk")
    z, y = place // PLANE, lax.rem(place, NY)
    v_scr[:, HEAD:] = jnp.ones((KEYS, HEAD), jnp.bfloat16)
    for piece, zrel, lines in pieces:
        for at, line in enumerate(lines):
            for j in range(2):
                source = (lax.rem(z + zrel, NZ) * NY + (y ^ line)) * 2 + j
                row = pl.multiple_of(table[source] * BLOCK, BLOCK)
                k_scr[pl.ds(row, BLOCK), :] = piece[at * 128 + j * BLOCK : at * 128 + (j + 1) * BLOCK, :]
                v_scr[pl.ds(row, BLOCK), :HEAD] = piece[at * 128 + 64 + j * BLOCK : at * 128 + 64 + (j + 1) * BLOCK, :]
    for t in range(KEYS // 128):
        kt_scr[:, t * 128 : (t + 1) * 128] = k_scr[t * 128 : (t + 1) * 128, :].T


def pick(k_scr, v_scr, o_ref):
    place = lax.axis_index("blk")
    z, y = place // PLANE, lax.rem(place, NY)
    some = 16

    @pl.when(y == z // 2)
    def _():
        line = lax.broadcasted_iota(jnp.int32, (PLANE * some, some * BLOCK), 0)
        column = lax.broadcasted_iota(jnp.int32, (PLANE * some, some * BLOCK), 1)
        wanted = (line % some) * BLOCK + lax.rem(z, 2) * PLANE + line // some
        select = jnp.where(column == wanted, 1.0, 0.0).astype(jnp.bfloat16)
        for c in range(KEY_BLOCKS // some):
            rows = slice(c * some * BLOCK, (c + 1) * some * BLOCK)
            for at, scr in ((PARTIAL, k_scr), (PARTIAL + KEY_BLOCKS, v_scr)):
                values = jnp.dot(select, scr[rows, :HEAD], preferred_element_type=jnp.float32).astype(jnp.bfloat16)
                for d in range(PLANE):
                    o_ref[d, at + c * some : at + (c + 1) * some, :] = values[d * some : (d + 1) * some]

    @pl.when(y != z // 2)
    def _():
        for d in range(PLANE):
            o_ref[d, PARTIAL:, :] = jnp.zeros((2 * KEY_BLOCKS, HEAD), jnp.bfloat16)


def attention_kernel(table, q_ref, kpos_ref, *refs):
    pieces, (o_ref, k_scr, kt_scr, v_scr, s_scr, stat) = refs[:9], refs[9:]
    own, r1, r2, r3, l1, l2, l3, r4, l4 = pieces
    every, first, last = range(NY), range(NY // 2), range(NY // 2, NY)
    arrange(
        table,
        [(own, 0, every), (l1, 1, every), (l2, 2, every), (l3, 3, every), (r4, 4, first), (l4, 4, last)]
        + [(r3, 5, every), (r2, 6, every), (r1, 7, every)],
        k_scr,
        kt_scr,
        v_scr,
    )
    pick(k_scr, v_scr, o_ref)
    lane = lax.broadcasted_iota(jnp.int32, (ROWS, 128), 1)
    token = lax.broadcasted_iota(jnp.int32, (BLOCK, CHUNK), 0)

    def one_group(i, carry):
        low, high = table[AT_LOW + i], table[AT_HIGH + i]
        blocks = [table[AT_ORDER + i * JOINED + u] for u in range(JOINED)]
        ids = [table[AT_ID + i * JOINED + u] for u in range(JOINED)]

        def finish(u, out, total, top):
            place = pl.ds(pl.multiple_of(blocks[u] % 2 * ROWS, ROWS), ROWS)
            o_ref[blocks[u] // 2, place, :] = out.astype(jnp.bfloat16)
            old = jnp.where(lane == blocks[u], top, stat[...])
            stat[...] = jnp.where(lane == blocks[u] + Q_BLOCKS, total, old)

        def work(n):
            q = jnp.concatenate([q_ref[blocks[u]] for u in range(JOINED)], axis=0)
            tops = [None] * (JOINED * GROUP)
            for c in range(n):
                start = pl.multiple_of((low + c) * CHUNK, CHUNK)
                s = jnp.dot(q, kt_scr[:, pl.ds(start, CHUNK)], preferred_element_type=jnp.float32)
                kpos = kpos_ref[pl.ds(low + c, 1), :]
                for u in range(JOINED):
                    distance = (ids[u] * BLOCK + token) - kpos
                    bias = jnp.where((distance >= 0) & (distance < WINDOW), 0.0, NEG)
                    for g in range(GROUP):
                        r = u * GROUP + g
                        part = s[r * BLOCK : (r + 1) * BLOCK] + bias
                        s_scr[c, r * BLOCK : (r + 1) * BLOCK, :] = part
                        wide = jnp.maximum(part[:, :128], part[:, 128:])
                        tops[r] = wide if tops[r] is None else jnp.maximum(tops[r], wide)
            top = jnp.max(jnp.concatenate(tops, axis=0), axis=1, keepdims=True) * SCALE
            top = jnp.broadcast_to(top, (JOINED * ROWS, 128))
            twice = jnp.concatenate([top, top], axis=1)
            acc = None
            for c in range(n):
                start = pl.multiple_of((low + c) * CHUNK, CHUNK)
                p = jnp.exp2(s_scr[c] * SCALE - twice).astype(jnp.bfloat16)
                part = jnp.dot(p, v_scr[pl.ds(start, CHUNK), :], preferred_element_type=jnp.float32)
                acc = part if acc is None else acc + part
            for u in range(JOINED):
                rows = slice(u * ROWS, (u + 1) * ROWS)
                finish(u, acc[rows, :HEAD] / acc[rows, HEAD:], acc[rows, HEAD:], top[rows])

        @pl.when(high <= low)
        def _():
            nothing = jnp.zeros((ROWS, 128), jnp.float32)
            for u in range(JOINED):
                finish(u, nothing, nothing, nothing + NEG)

        for n in range(1, KEYS // CHUNK + 1):
            pl.when(high - low == n)(functools.partial(work, n))
        return carry

    stat[...] = jnp.zeros((ROWS, 128), jnp.float32)
    lax.fori_loop(0, Q_BLOCKS // JOINED, one_group, 0)
    turned = stat[...].T
    for d in range(PLANE):
        value = jnp.concatenate(
            [turned[2 * d : 2 * d + 2], turned[Q_BLOCKS + 2 * d : Q_BLOCKS + 2 * d + 2]], axis=0
        )
        first = value.astype(jnp.bfloat16).astype(jnp.float32)
        second = (value - first).astype(jnp.bfloat16).astype(jnp.float32)
        third = value - first - second
        rows = jnp.concatenate([first, second, third, jnp.zeros_like(first)], axis=0)
        o_ref[d, 2 * ROWS : PARTIAL, :] = rows.astype(jnp.bfloat16)


def combine_kernel(heads, blocks, length, choose_ref, m_ref, o_ref, cache_ref):
    keeper = lax.axis_index("blk") // (2 * PLANE)
    for half in range(2):
        rows = slice(PARTIAL + half * KEY_BLOCKS, PARTIAL + (half + 1) * KEY_BLOCKS)
        found = jnp.concatenate([m_ref[x * NY + keeper, rows, :] for x in range(NX)], axis=0)
        cache = jnp.dot(choose_ref[...], found, preferred_element_type=jnp.float32)
        cache_ref[half] = cache.astype(jnp.bfloat16)
    values = []
    for d in range(PLANE):
        rows = m_ref[d, 2 * ROWS : PARTIAL, :].astype(jnp.float32)
        values.append(rows[0:4] + rows[4:8] + rows[8:12])
    weights = [None] * PLANE
    for y in range(NY):
        sources = [x * NY + y for x in range(NX)]
        top = values[sources[0]][0:2]
        for d in sources[1:]:
            top = jnp.maximum(top, values[d][0:2])
        parts = [jnp.exp2(values[d][0:2] - top) * values[d][2:4] for d in sources]
        total = parts[0] + parts[1] + parts[2] + parts[3]
        for d, part in zip(sources, parts):
            weights[d] = part / total
    matrix = jnp.concatenate(weights + [jnp.zeros((128 - Q_BLOCKS, 128), jnp.float32)], axis=0).T
    token = lax.broadcasted_iota(jnp.int32, (ROWS, HEAD), 0) % BLOCK
    for y in range(NY):
        for j in range(2):
            out = jnp.zeros((ROWS, HEAD), jnp.float32)
            for x in range(NX):
                d = x * NY + y
                weight = matrix[:, 2 * d + j : 2 * d + j + 1]
                out += weight * m_ref[d, j * ROWS : (j + 1) * ROWS, :].astype(jnp.float32)
            out = jnp.where(blocks[j] * BLOCK + token < length[0], out, 0.0).astype(jnp.bfloat16)
            for g in range(GROUP):
                column = pl.multiple_of((heads[y] * GROUP + g) * HEAD, HEAD)
                o_ref[j * BLOCK : (j + 1) * BLOCK, pl.ds(column, HEAD)] = out[g * BLOCK : (g + 1) * BLOCK]


def ranks(ids):
    return jnp.sum(ids[..., None, :] < ids[..., :, None], axis=-1, dtype=jnp.int32)


def placed(values, rank):
    places = jnp.arange(values.shape[-1], dtype=jnp.int32)
    return jnp.sum(jnp.where(rank[..., None, :] == places[:, None], values[..., None, :], 0), axis=-1, dtype=jnp.int32)


def body(query, rotated_key_value, lengths, block_map, segment_head):
    place = lax.axis_index("blk")
    z, x, y = place // 16, (place // 4) % 4, place % 4
    y_groups = [[4 * g + i for i in range(4)] for g in range(N_BLK // 4)]
    x_groups = [[16 * a + 4 * i + c for i in range(4)] for a in range(NZ) for c in range(NY)]
    planes = [[16 * a + i for i in range(16)] for a in range(NZ)]

    def move(value, target):
        return lax.ppermute(value, "blk", [(s, target(s // 16, (s // 4) % 4, s % 4)) for s in range(N_BLK)])

    def index(zz, xx, yy):
        return (zz % NZ) * 16 + xx * 4 + yy

    def exchange(value, groups):
        return lax.all_to_all(value, "blk", 0, 0, axis_index_groups=groups, tiled=True)

    kv = pl.pallas_call(
        split_kv_kernel,
        out_shape=(jax.ShapeDtypeStruct((128, HEAD), jnp.bfloat16),) * NY,
        in_specs=[SMEM, VMEM],
        out_specs=(VMEM,) * NY,
        compiler_params=SMALL,
        name="split_kv",
    )(segment_head, rotated_key_value.reshape(128, KEY_VALUE_HEADS * HEAD))
    line = [kv[0]] + [move(kv[k], lambda a, b, c, k=k: index(a, b, c ^ k)) for k in range(1, NY)]
    own = jnp.concatenate(line, axis=0)
    right = lambda v: move(v, lambda a, b, c: index(a + 1, b, c))
    left = lambda v: move(v, lambda a, b, c: index(a - 1, b, c))
    r1, l1 = right(own), left(own)
    q = pl.pallas_call(
        split_q_kernel,
        out_shape=jax.ShapeDtypeStruct((PLANE, 2 * ROWS, HEAD), jnp.bfloat16),
        in_specs=[SMEM, VMEM],
        out_specs=VMEM,
        compiler_params=SMALL,
        name="split_q",
    )(segment_head, query.reshape(2 * BLOCK, QUERY_HEADS * HEAD))
    q = exchange(q, planes).reshape(Q_BLOCKS, ROWS, HEAD)
    r2, l2 = right(r1), left(l1)
    r3, l3 = right(r2), left(l2)
    half = own.shape[0] // 2
    r4 = move(r2[:half], lambda a, b, c: index(a + 2, b, c))
    l4 = move(l2[half:], lambda a, b, c: index(a - 2, b, c))

    ids = block_map.reshape(NZ, NX, NY, 2).transpose(1, 0, 2, 3).reshape(NX, KEY_BLOCKS)
    rank = ranks(ids)
    ordered = placed(ids, rank)
    mine = lax.dynamic_index_in_dim(ordered, x, 0, keepdims=False)
    my_rank = lax.dynamic_index_in_dim(rank, x, 0, keepdims=False)
    q_ids = lax.dynamic_slice_in_dim(block_map, z * Q_BLOCKS, Q_BLOCKS)
    q_rank = ranks(q_ids)
    q_order = placed(jnp.arange(Q_BLOCKS, dtype=jnp.int32), q_rank)
    q_sorted = placed(q_ids, q_rank)
    grouped = q_sorted.reshape(Q_BLOCKS // JOINED, JOINED)
    lows = jnp.sum(mine[None, :] < grouped[:, :1] - WINDOW // BLOCK, axis=1, dtype=jnp.int32) // CHUNK_BLOCKS
    highs = jnp.sum(mine[None, :] <= grouped[:, -1:], axis=1, dtype=jnp.int32)
    highs = (highs + CHUNK_BLOCKS - 1) // CHUNK_BLOCKS
    table = jnp.concatenate([my_rank, q_order, q_sorted, lows, highs])
    kpos = mine[:, None] * BLOCK + jnp.arange(BLOCK, dtype=jnp.int32)[None, :]
    kpos = kpos.reshape(KEYS // CHUNK, CHUNK)

    pieces = (own, r1, r2, r3, l1, l2, l3, r4, l4)
    partial = pl.pallas_call(
        attention_kernel,
        out_shape=jax.ShapeDtypeStruct((PLANE, MESSAGE, HEAD), jnp.bfloat16),
        in_specs=[SMEM] + [VMEM] * 11,
        out_specs=VMEM,
        scratch_shapes=[
            pltpu.VMEM((KEYS, HEAD), jnp.bfloat16),
            pltpu.VMEM((HEAD, KEYS), jnp.bfloat16),
            pltpu.VMEM((KEYS, 2 * HEAD), jnp.bfloat16),
            pltpu.VMEM((KEYS // CHUNK, JOINED * ROWS, CHUNK), jnp.float32),
            pltpu.VMEM((ROWS, 128), jnp.float32),
        ],
        compiler_params=PARAMS,
        cost_estimate=pl.CostEstimate(flops=3_000_000_000, bytes_accessed=4_000_000, transcendentals=5_000_000),
        name="attention",
    )(table, q, kpos, *pieces)
    out = exchange(partial, planes)

    blocks = jnp.arange(BLOCKS, dtype=jnp.int32)
    position = blocks * BLOCK + place % BLOCK
    choose = (ordered.reshape(1, BLOCKS) == blocks[:, None]) & (position < lengths[0])[:, None]
    choose = choose.astype(jnp.bfloat16)
    my_blocks = lax.dynamic_slice_in_dim(block_map, 2 * place, 2)
    attended, cache = pl.pallas_call(
        combine_kernel,
        out_shape=(
            jax.ShapeDtypeStruct((2 * BLOCK, QUERY_HEADS * HEAD), jnp.bfloat16),
            jax.ShapeDtypeStruct((2, BLOCKS, HEAD), jnp.bfloat16),
        ),
        in_specs=[SMEM] * 3 + [VMEM] * 2,
        out_specs=(VMEM, VMEM),
        compiler_params=SMALL,
        name="combine",
    )(segment_head, my_blocks, lengths, choose, out)
    return attended.reshape(1, 2 * BLOCK, QUERY_HEADS * HEAD), cache[None, :, None]


def solution(mesh):
    return jax.shard_map(
        body,
        mesh=mesh,
        in_specs=(P("req", "blk", None), P("req", None, "blk", None), P("req"), P(), P()),
        out_specs=(P("req", "blk", None), P("req", None, "blk", None, None)),
        check_vma=False,
    )
```

```python
import functools

import jax
import jax.numpy as jnp
from jax import lax
from jax.experimental import pallas as pl
from jax.experimental.pallas import tpu as pltpu
from jax.sharding import PartitionSpec as P

QUERY_HEADS = 16
KEY_VALUE_HEADS = 4
GROUP = QUERY_HEADS // KEY_VALUE_HEADS
HEAD = 128
WINDOW = 4096
BLOCK = 32
BLOCKS = 256
NZ, NX, NY = 8, 4, 4
N_BLK = NZ * NX * NY
PLANE = NX * NY
KEY_BLOCKS = 2 * NZ * NY
Q_BLOCKS = 2 * PLANE
ROWS = GROUP * BLOCK
KEYS = KEY_BLOCKS * BLOCK
JOINED = 4
CHUNK_BLOCKS = 8
CHUNK = CHUNK_BLOCKS * BLOCK
HALF = Q_BLOCKS // 2
PARTIAL = ROWS + 16
MESSAGE = PARTIAL + 2 * KEY_BLOCKS
SCALE = HEAD**-0.5 * 1.4426950408889634
NEG = -1e30
AT_ORDER = KEY_BLOCKS
AT_ID = AT_ORDER + Q_BLOCKS
AT_LOW = AT_ID + Q_BLOCKS
AT_HIGH = AT_LOW + Q_BLOCKS // JOINED

SMEM = pl.BlockSpec(memory_space=pltpu.SMEM)
VMEM = pl.BlockSpec(memory_space=pltpu.VMEM)
PARAMS = pltpu.CompilerParams(vmem_limit_bytes=24 * 1024 * 1024)
SMALL = pltpu.CompilerParams(vmem_limit_bytes=8 * 1024 * 1024)


def split_kv_kernel(heads, kv_ref, *o_refs):
    y = lax.rem(lax.axis_index("blk"), NY)
    for k in range(NY):
        o_refs[k][...] = kv_ref[:, pl.ds(pl.multiple_of(heads[y ^ k] * HEAD, HEAD), HEAD)]


def split_q_kernel(heads, q_ref, o_ref):
    for y in range(NY):
        for g in range(GROUP):
            column = pl.multiple_of((heads[y] * GROUP + g) * HEAD, HEAD)
            for j in range(2):
                tile = q_ref[j * BLOCK : (j + 1) * BLOCK, pl.ds(column, HEAD)]
                for x in range(NX):
                    o_ref[x * NY + y, j * ROWS + g * BLOCK : j * ROWS + (g + 1) * BLOCK] = tile


def arrange(table, pieces, k_scr, kt_scr, v_scr):
    place = lax.axis_index("blk")
    z, y = place // PLANE, lax.rem(place, NY)
    v_scr[:, HEAD:] = jnp.ones((KEYS, HEAD), jnp.bfloat16)
    for piece, zrel, lines in pieces:
        for at, line in enumerate(lines):
            for j in range(2):
                source = (lax.rem(z + zrel, NZ) * NY + (y ^ line)) * 2 + j
                row = pl.multiple_of(table[source] * BLOCK, BLOCK)
                k_scr[pl.ds(row, BLOCK), :] = piece[at * 128 + j * BLOCK : at * 128 + (j + 1) * BLOCK, :]
                v_scr[pl.ds(row, BLOCK), :HEAD] = piece[at * 128 + 64 + j * BLOCK : at * 128 + 64 + (j + 1) * BLOCK, :]
    for t in range(KEYS // 128):
        kt_scr[:, t * 128 : (t + 1) * 128] = k_scr[t * 128 : (t + 1) * 128, :].T


def pick(k_scr, v_scr, o_ref):
    place = lax.axis_index("blk")
    z, y = place // PLANE, lax.rem(place, NY)
    some = 16

    @pl.when(y == z // 2)
    def _():
        line = lax.broadcasted_iota(jnp.int32, (PLANE * some, some * BLOCK), 0)
        column = lax.broadcasted_iota(jnp.int32, (PLANE * some, some * BLOCK), 1)
        wanted = (line % some) * BLOCK + lax.rem(z, 2) * PLANE + line // some
        select = jnp.where(column == wanted, 1.0, 0.0).astype(jnp.bfloat16)
        for c in range(KEY_BLOCKS // some):
            rows = slice(c * some * BLOCK, (c + 1) * some * BLOCK)
            for at, scr in ((PARTIAL, k_scr), (PARTIAL + KEY_BLOCKS, v_scr)):
                values = jnp.dot(select, scr[rows, :HEAD], preferred_element_type=jnp.float32).astype(jnp.bfloat16)
                for d in range(PLANE):
                    o_ref[d, at + c * some : at + (c + 1) * some, :] = values[d * some : (d + 1) * some]

    @pl.when(y != z // 2)
    def _():
        for d in range(PLANE):
            o_ref[d, PARTIAL:, :] = jnp.zeros((2 * KEY_BLOCKS, HEAD), jnp.bfloat16)


def low_kernel(table, q_ref, kpos_ref, *refs):
    pieces, (o_ref, kt_ref, v_ref, k_scr, s_scr, stat) = refs[:9], refs[9:]
    own, r1, r2, r3, l1, l2, l3, r4, l4 = pieces
    every, first, last = range(NY), range(NY // 2), range(NY // 2, NY)
    arrange(
        table,
        [(own, 0, every), (l1, 1, every), (l2, 2, every), (l3, 3, every), (r4, 4, first), (l4, 4, last)]
        + [(r3, 5, every), (r2, 6, every), (r1, 7, every)],
        k_scr,
        kt_ref,
        v_ref,
    )
    pick(k_scr, v_ref, o_ref)
    attend(0, KEYS // CHUNK // 2, table, q_ref, kpos_ref, kt_ref, v_ref, o_ref, s_scr, stat)


def high_kernel(table, q_ref, kpos_ref, kt_ref, v_ref, o_ref, s_scr, stat):
    attend(HALF // JOINED, KEYS // CHUNK, table, q_ref, kpos_ref, kt_ref, v_ref, o_ref, s_scr, stat)


def attend(first_group, most, table, q_ref, kpos_ref, kt_ref, v_ref, o_ref, s_scr, stat):
    lane = lax.broadcasted_iota(jnp.int32, (ROWS, 128), 1)
    token = lax.broadcasted_iota(jnp.int32, (BLOCK, CHUNK), 0)

    def one_group(i, carry):
        low, high = table[AT_LOW + i], table[AT_HIGH + i]
        blocks = [table[AT_ORDER + i * JOINED + u] for u in range(JOINED)]
        ids = [table[AT_ID + i * JOINED + u] for u in range(JOINED)]

        def finish(u, out, total, top):
            target = blocks[u] // 2
            o_ref[target, :ROWS, :] = out.astype(jnp.bfloat16)
            old = jnp.where(lane == target, top, stat[...])
            stat[...] = jnp.where(lane == target + PLANE, total, old)

        def work(n):
            q = jnp.concatenate([q_ref[blocks[u]] for u in range(JOINED)], axis=0)
            tops = [None] * (JOINED * GROUP)
            for c in range(n):
                start = pl.multiple_of((low + c) * CHUNK, CHUNK)
                s = jnp.dot(q, kt_ref[:, pl.ds(start, CHUNK)], preferred_element_type=jnp.float32)
                kpos = kpos_ref[pl.ds(low + c, 1), :]
                for u in range(JOINED):
                    distance = (ids[u] * BLOCK + token) - kpos
                    bias = jnp.where((distance >= 0) & (distance < WINDOW), 0.0, NEG)
                    for g in range(GROUP):
                        r = u * GROUP + g
                        part = s[r * BLOCK : (r + 1) * BLOCK] + bias
                        s_scr[c, r * BLOCK : (r + 1) * BLOCK, :] = part
                        wide = jnp.maximum(part[:, :128], part[:, 128:])
                        tops[r] = wide if tops[r] is None else jnp.maximum(tops[r], wide)
            top = jnp.max(jnp.concatenate(tops, axis=0), axis=1, keepdims=True) * SCALE
            top = jnp.broadcast_to(top, (JOINED * ROWS, 128))
            twice = jnp.concatenate([top, top], axis=1)
            acc = None
            for c in range(n):
                start = pl.multiple_of((low + c) * CHUNK, CHUNK)
                p = jnp.exp2(s_scr[c] * SCALE - twice).astype(jnp.bfloat16)
                part = jnp.dot(p, v_ref[pl.ds(start, CHUNK), :], preferred_element_type=jnp.float32)
                acc = part if acc is None else acc + part
            for u in range(JOINED):
                rows = slice(u * ROWS, (u + 1) * ROWS)
                finish(u, acc[rows, :HEAD] / acc[rows, HEAD:], acc[rows, HEAD:], top[rows])

        @pl.when(high <= low)
        def _():
            nothing = jnp.zeros((ROWS, 128), jnp.float32)
            for u in range(JOINED):
                finish(u, nothing, nothing, nothing + NEG)

        for n in range(1, most + 1):
            pl.when(high - low == n)(functools.partial(work, n))
        return carry

    stat[...] = jnp.zeros((ROWS, 128), jnp.float32)
    lax.fori_loop(first_group, first_group + HALF // JOINED, one_group, 0)
    turned = stat[...].T
    for d in range(PLANE):
        value = jnp.concatenate([turned[d : d + 1], turned[PLANE + d : PLANE + d + 1]], axis=0)
        first = value.astype(jnp.bfloat16).astype(jnp.float32)
        second = (value - first).astype(jnp.bfloat16).astype(jnp.float32)
        third = value - first - second
        rows = jnp.concatenate([first, second, third, jnp.zeros((10, 128), jnp.float32)], axis=0)
        o_ref[d, ROWS:PARTIAL, :] = rows.astype(jnp.bfloat16)


def merge(heads, block, length, m_ref, store):
    values = []
    for d in range(PLANE):
        rows = m_ref[d, ROWS:PARTIAL, :].astype(jnp.float32)
        values.append(rows[0:2] + rows[2:4] + rows[4:6])
    weights = [None] * PLANE
    for y in range(NY):
        sources = [x * NY + y for x in range(NX)]
        top = values[sources[0]][0:1]
        for d in sources[1:]:
            top = jnp.maximum(top, values[d][0:1])
        parts = [jnp.exp2(values[d][0:1] - top) * values[d][1:2] for d in sources]
        total = parts[0] + parts[1] + parts[2] + parts[3]
        for d, part in zip(sources, parts):
            weights[d] = part / total
    matrix = jnp.concatenate(weights + [jnp.zeros((128 - PLANE, 128), jnp.float32)], axis=0).T
    token = lax.broadcasted_iota(jnp.int32, (ROWS, HEAD), 0) % BLOCK
    for y in range(NY):
        out = jnp.zeros((ROWS, HEAD), jnp.float32)
        for x in range(NX):
            d = x * NY + y
            out += matrix[:, d : d + 1] * m_ref[d, :ROWS, :].astype(jnp.float32)
        out = jnp.where(block * BLOCK + token < length[0], out, 0.0).astype(jnp.bfloat16)
        for g in range(GROUP):
            column = pl.multiple_of((heads[y] * GROUP + g) * HEAD, HEAD)
            store(pl.ds(column, HEAD), out[g * BLOCK : (g + 1) * BLOCK])


def combine_low_kernel(heads, blocks, length, choose_ref, m_ref, o_ref, cache_ref):
    keeper = lax.axis_index("blk") // (2 * PLANE)
    for half in range(2):
        rows = slice(PARTIAL + half * KEY_BLOCKS, PARTIAL + (half + 1) * KEY_BLOCKS)
        found = jnp.concatenate([m_ref[x * NY + keeper, rows, :] for x in range(NX)], axis=0)
        cache = jnp.dot(choose_ref[...], found, preferred_element_type=jnp.float32)
        cache_ref[half] = cache.astype(jnp.bfloat16)

    def store(columns, value):
        o_ref[:, columns] = value

    merge(heads, jnp.minimum(blocks[0], blocks[1]), length, m_ref, store)


def combine_high_kernel(heads, blocks, length, low_ref, m_ref, o_ref):
    second = jnp.where(blocks[0] < blocks[1], 1, 0)
    rows = pl.ds(pl.multiple_of(second * BLOCK, BLOCK), BLOCK)
    o_ref[pl.ds(pl.multiple_of((1 - second) * BLOCK, BLOCK), BLOCK), :] = low_ref[...]

    def store(columns, value):
        o_ref[rows, columns] = value

    merge(heads, jnp.maximum(blocks[0], blocks[1]), length, m_ref, store)


def ranks(ids):
    return jnp.sum(ids[..., None, :] < ids[..., :, None], axis=-1, dtype=jnp.int32)


def placed(values, rank):
    places = jnp.arange(values.shape[-1], dtype=jnp.int32)
    return jnp.sum(jnp.where(rank[..., None, :] == places[:, None], values[..., None, :], 0), axis=-1, dtype=jnp.int32)


def body(query, rotated_key_value, lengths, block_map, segment_head):
    place = lax.axis_index("blk")
    z, x, y = place // 16, (place // 4) % 4, place % 4
    y_groups = [[4 * g + i for i in range(4)] for g in range(N_BLK // 4)]
    x_groups = [[16 * a + 4 * i + c for i in range(4)] for a in range(NZ) for c in range(NY)]
    planes = [[16 * a + i for i in range(16)] for a in range(NZ)]

    def move(value, target):
        return lax.ppermute(value, "blk", [(s, target(s // 16, (s // 4) % 4, s % 4)) for s in range(N_BLK)])

    def index(zz, xx, yy):
        return (zz % NZ) * 16 + xx * 4 + yy

    def exchange(value, groups):
        return lax.all_to_all(value, "blk", 0, 0, axis_index_groups=groups, tiled=True)

    kv = pl.pallas_call(
        split_kv_kernel,
        out_shape=(jax.ShapeDtypeStruct((128, HEAD), jnp.bfloat16),) * NY,
        in_specs=[SMEM, VMEM],
        out_specs=(VMEM,) * NY,
        compiler_params=SMALL,
        name="split_kv",
    )(segment_head, rotated_key_value.reshape(128, KEY_VALUE_HEADS * HEAD))
    line = [kv[0]] + [move(kv[k], lambda a, b, c, k=k: index(a, b, c ^ k)) for k in range(1, NY)]
    own = jnp.concatenate(line, axis=0)
    right = lambda v: move(v, lambda a, b, c: index(a + 1, b, c))
    left = lambda v: move(v, lambda a, b, c: index(a - 1, b, c))
    r1, l1 = right(own), left(own)
    q = pl.pallas_call(
        split_q_kernel,
        out_shape=jax.ShapeDtypeStruct((PLANE, 2 * ROWS, HEAD), jnp.bfloat16),
        in_specs=[SMEM, VMEM],
        out_specs=VMEM,
        compiler_params=SMALL,
        name="split_q",
    )(segment_head, query.reshape(2 * BLOCK, QUERY_HEADS * HEAD))
    q = exchange(q, planes).reshape(Q_BLOCKS, ROWS, HEAD)
    r2, l2 = right(r1), left(l1)
    r3, l3 = right(r2), left(l2)
    half = own.shape[0] // 2
    r4 = move(r2[:half], lambda a, b, c: index(a + 2, b, c))
    l4 = move(l2[half:], lambda a, b, c: index(a - 2, b, c))

    ids = block_map.reshape(NZ, NX, NY, 2).transpose(1, 0, 2, 3).reshape(NX, KEY_BLOCKS)
    rank = ranks(ids)
    ordered = placed(ids, rank)
    mine = lax.dynamic_index_in_dim(ordered, x, 0, keepdims=False)
    my_rank = lax.dynamic_index_in_dim(rank, x, 0, keepdims=False)
    q_ids = lax.dynamic_slice_in_dim(block_map, z * Q_BLOCKS, Q_BLOCKS)
    q_rank = ranks(q_ids)
    q_order = placed(jnp.arange(Q_BLOCKS, dtype=jnp.int32), q_rank)
    q_sorted = placed(q_ids, q_rank)
    grouped = q_sorted.reshape(Q_BLOCKS // JOINED, JOINED)
    lows = jnp.sum(mine[None, :] < grouped[:, :1] - WINDOW // BLOCK, axis=1, dtype=jnp.int32) // CHUNK_BLOCKS
    highs = jnp.sum(mine[None, :] <= grouped[:, -1:], axis=1, dtype=jnp.int32)
    highs = (highs + CHUNK_BLOCKS - 1) // CHUNK_BLOCKS
    table = jnp.concatenate([my_rank, q_order, q_sorted, lows, highs])
    kpos = mine[:, None] * BLOCK + jnp.arange(BLOCK, dtype=jnp.int32)[None, :]
    kpos = kpos.reshape(KEYS // CHUNK, CHUNK)

    pieces = (own, r1, r2, r3, l1, l2, l3, r4, l4)
    low, kt, v = pl.pallas_call(
        low_kernel,
        out_shape=(
            jax.ShapeDtypeStruct((PLANE, MESSAGE, HEAD), jnp.bfloat16),
            jax.ShapeDtypeStruct((HEAD, KEYS), jnp.bfloat16),
            jax.ShapeDtypeStruct((KEYS, 2 * HEAD), jnp.bfloat16),
        ),
        in_specs=[SMEM] + [VMEM] * 11,
        out_specs=(VMEM,) * 3,
        scratch_shapes=[
            pltpu.VMEM((KEYS, HEAD), jnp.bfloat16),
            pltpu.VMEM((KEYS // CHUNK // 2, JOINED * ROWS, CHUNK), jnp.float32),
            pltpu.VMEM((ROWS, 128), jnp.float32),
        ],
        compiler_params=PARAMS,
        cost_estimate=pl.CostEstimate(flops=1_000_000_000, bytes_accessed=4_000_000, transcendentals=2_000_000),
        name="low",
    )(table, q, kpos, *pieces)
    low = exchange(low, planes)
    high = pl.pallas_call(
        high_kernel,
        out_shape=jax.ShapeDtypeStruct((PLANE, PARTIAL, HEAD), jnp.bfloat16),
        in_specs=[SMEM] + [VMEM] * 4,
        out_specs=VMEM,
        scratch_shapes=[
            pltpu.VMEM((KEYS // CHUNK, JOINED * ROWS, CHUNK), jnp.float32),
            pltpu.VMEM((ROWS, 128), jnp.float32),
        ],
        compiler_params=PARAMS,
        cost_estimate=pl.CostEstimate(flops=2_000_000_000, bytes_accessed=3_000_000, transcendentals=3_000_000),
        name="high",
    )(table, q, kpos, kt, v)
    high = exchange(high, planes)

    blocks = jnp.arange(BLOCKS, dtype=jnp.int32)
    position = blocks * BLOCK + place % BLOCK
    choose = (ordered.reshape(1, BLOCKS) == blocks[:, None]) & (position < lengths[0])[:, None]
    choose = choose.astype(jnp.bfloat16)
    my_blocks = lax.dynamic_slice_in_dim(block_map, 2 * place, 2)
    low, cache = pl.pallas_call(
        combine_low_kernel,
        out_shape=(
            jax.ShapeDtypeStruct((BLOCK, QUERY_HEADS * HEAD), jnp.bfloat16),
            jax.ShapeDtypeStruct((2, BLOCKS, HEAD), jnp.bfloat16),
        ),
        in_specs=[SMEM] * 3 + [VMEM] * 2,
        out_specs=(VMEM, VMEM),
        compiler_params=SMALL,
        name="combine_low",
    )(segment_head, my_blocks, lengths, choose, low)
    attended = pl.pallas_call(
        combine_high_kernel,
        out_shape=jax.ShapeDtypeStruct((2 * BLOCK, QUERY_HEADS * HEAD), jnp.bfloat16),
        in_specs=[SMEM] * 3 + [VMEM] * 2,
        out_specs=VMEM,
        compiler_params=SMALL,
        name="combine_high",
    )(segment_head, my_blocks, lengths, low, high)
    return attended.reshape(1, 2 * BLOCK, QUERY_HEADS * HEAD), cache[None, :, None]


def solution(mesh):
    return jax.shard_map(
        body,
        mesh=mesh,
        in_specs=(P("req", "blk", None), P("req", None, "blk", None), P("req"), P(), P()),
        out_specs=(P("req", "blk", None), P("req", None, "blk", None, None)),
        check_vma=False,
    )
```

```python
import functools

import jax
import jax.numpy as jnp
from jax import lax
from jax.experimental import pallas as pl
from jax.experimental.pallas import tpu as pltpu
from jax.sharding import PartitionSpec as P

QUERY_HEADS = 16
KEY_VALUE_HEADS = 4
GROUP = QUERY_HEADS // KEY_VALUE_HEADS
HEAD = 128
WINDOW = 4096
BLOCK = 32
BLOCKS = 256
NZ, NX, NY = 8, 4, 4
N_BLK = NZ * NX * NY
PLANE = NX * NY
KEY_BLOCKS = 2 * NZ * NY
Q_BLOCKS = 2 * PLANE
ROWS = GROUP * BLOCK
KEYS = KEY_BLOCKS * BLOCK
JOINED = 4
CHUNK_BLOCKS = 8
CHUNK = CHUNK_BLOCKS * BLOCK
MESSAGE = 2 * ROWS + 16
SCALE = HEAD**-0.5 * 1.4426950408889634
NEG = -1e30
AT_ORDER = KEY_BLOCKS
AT_ID = AT_ORDER + Q_BLOCKS
AT_LOW = AT_ID + Q_BLOCKS
AT_HIGH = AT_LOW + Q_BLOCKS // JOINED

SMEM = pl.BlockSpec(memory_space=pltpu.SMEM)
VMEM = pl.BlockSpec(memory_space=pltpu.VMEM)
PARAMS = pltpu.CompilerParams(vmem_limit_bytes=24 * 1024 * 1024)
SMALL = pltpu.CompilerParams(vmem_limit_bytes=8 * 1024 * 1024)


def split_kv_kernel(heads, kv_ref, *o_refs):
    y = lax.rem(lax.axis_index("blk"), NY)
    for k in range(NY):
        o_refs[k][...] = kv_ref[:, pl.ds(pl.multiple_of(heads[y ^ k] * HEAD, HEAD), HEAD)]


def split_q_kernel(heads, q_ref, o_ref):
    for y in range(NY):
        for g in range(GROUP):
            column = pl.multiple_of((heads[y] * GROUP + g) * HEAD, HEAD)
            for j in range(2):
                tile = q_ref[j * BLOCK : (j + 1) * BLOCK, pl.ds(column, HEAD)]
                for x in range(NX):
                    o_ref[x * NY + y, j * ROWS + g * BLOCK : j * ROWS + (g + 1) * BLOCK] = tile


def arrange(table, pieces, k_scr, kt_scr, v_scr):
    place = lax.axis_index("blk")
    z, y = place // PLANE, lax.rem(place, NY)
    v_scr[:, HEAD:] = jnp.ones((KEYS, HEAD), jnp.bfloat16)
    for piece, zrel, lines in pieces:
        for at, line in enumerate(lines):
            for j in range(2):
                source = (lax.rem(z + zrel, NZ) * NY + (y ^ line)) * 2 + j
                row = pl.multiple_of(table[source] * BLOCK, BLOCK)
                k_scr[pl.ds(row, BLOCK), :] = piece[at * 128 + j * BLOCK : at * 128 + (j + 1) * BLOCK, :]
                v_scr[pl.ds(row, BLOCK), :HEAD] = piece[at * 128 + 64 + j * BLOCK : at * 128 + 64 + (j + 1) * BLOCK, :]
    for t in range(KEYS // 128):
        kt_scr[:, t * 128 : (t + 1) * 128] = k_scr[t * 128 : (t + 1) * 128, :].T


def pick_kernel(*refs):
    own, r1, r2, r3, l1, l2, l3, r4, l4 = refs[:9]
    o_ref = refs[9]
    place = lax.axis_index("blk")
    z, x = place // PLANE, lax.rem(place // NY, NX)

    def select(lines, rows):
        count = 2 * NX * lines * 2
        out = lax.broadcasted_iota(jnp.int32, (count, rows), 0)
        column = lax.broadcasted_iota(jnp.int32, (count, rows), 1)
        half, k, line, j = out // (NX * lines * 2), out // (lines * 2) % NX, out // 2 % lines, out % 2
        offset = lax.rem(z, 2) * 16 + (x ^ k) * NY + z // 2
        wanted = line * 128 + half * 64 + j * BLOCK + offset
        return jnp.where(column == wanted, 1.0, 0.0).astype(jnp.bfloat16)

    whole, part = select(NY, 512), select(NY // 2, 256)
    picked = [jnp.dot(whole, piece[...], preferred_element_type=jnp.float32) for piece in (own, l1, l2, l3)]
    picked.append([jnp.dot(part, piece[...], preferred_element_type=jnp.float32) for piece in (r4, l4)])
    picked += [jnp.dot(whole, piece[...], preferred_element_type=jnp.float32) for piece in (r3, r2, r1)]
    for k in range(NX):
        for half in range(2):
            rows = []
            for piece in picked:
                if isinstance(piece, list):
                    at = (half * NX + k) * 4
                    rows += [piece[0][at : at + 4], piece[1][at : at + 4]]
                else:
                    at = (half * NX + k) * 8
                    rows.append(piece[at : at + 8])
            o_ref[k, :, half * HEAD : (half + 1) * HEAD] = jnp.concatenate(rows, axis=0).astype(jnp.bfloat16)


def attention_kernel(table, q_ref, kpos_ref, *refs):
    pieces, (o_ref, k_scr, kt_scr, v_scr, s_scr, stat) = refs[:9], refs[9:]
    own, r1, r2, r3, l1, l2, l3, r4, l4 = pieces
    every, first, last = range(NY), range(NY // 2), range(NY // 2, NY)
    arrange(
        table,
        [(own, 0, every), (l1, 1, every), (l2, 2, every), (l3, 3, every), (r4, 4, first), (l4, 4, last)]
        + [(r3, 5, every), (r2, 6, every), (r1, 7, every)],
        k_scr,
        kt_scr,
        v_scr,
    )
    lane = lax.broadcasted_iota(jnp.int32, (ROWS, 128), 1)
    token = lax.broadcasted_iota(jnp.int32, (BLOCK, CHUNK), 0)

    def one_group(i, carry):
        low, high = table[AT_LOW + i], table[AT_HIGH + i]
        blocks = [table[AT_ORDER + i * JOINED + u] for u in range(JOINED)]
        ids = [table[AT_ID + i * JOINED + u] for u in range(JOINED)]

        def finish(u, out, total, top):
            place = pl.ds(pl.multiple_of(blocks[u] % 2 * ROWS, ROWS), ROWS)
            o_ref[blocks[u] // 2, place, :] = out.astype(jnp.bfloat16)
            old = jnp.where(lane == blocks[u], top, stat[...])
            stat[...] = jnp.where(lane == blocks[u] + Q_BLOCKS, total, old)

        def work(n):
            q = jnp.concatenate([q_ref[blocks[u]] for u in range(JOINED)], axis=0)
            tops = [None] * (JOINED * GROUP)
            for c in range(n):
                start = pl.multiple_of((low + c) * CHUNK, CHUNK)
                s = jnp.dot(q, kt_scr[:, pl.ds(start, CHUNK)], preferred_element_type=jnp.float32)
                kpos = kpos_ref[pl.ds(low + c, 1), :]
                for u in range(JOINED):
                    distance = (ids[u] * BLOCK + token) - kpos
                    bias = jnp.where((distance >= 0) & (distance < WINDOW), 0.0, NEG)
                    for g in range(GROUP):
                        r = u * GROUP + g
                        part = s[r * BLOCK : (r + 1) * BLOCK] + bias
                        s_scr[c, r * BLOCK : (r + 1) * BLOCK, :] = part
                        wide = jnp.maximum(part[:, :128], part[:, 128:])
                        tops[r] = wide if tops[r] is None else jnp.maximum(tops[r], wide)
            top = jnp.max(jnp.concatenate(tops, axis=0), axis=1, keepdims=True) * SCALE
            top = jnp.broadcast_to(top, (JOINED * ROWS, 128))
            twice = jnp.concatenate([top, top], axis=1)
            acc = None
            for c in range(n):
                start = pl.multiple_of((low + c) * CHUNK, CHUNK)
                p = jnp.exp2(s_scr[c] * SCALE - twice).astype(jnp.bfloat16)
                part = jnp.dot(p, v_scr[pl.ds(start, CHUNK), :], preferred_element_type=jnp.float32)
                acc = part if acc is None else acc + part
            for u in range(JOINED):
                rows = slice(u * ROWS, (u + 1) * ROWS)
                finish(u, acc[rows, :HEAD] / acc[rows, HEAD:], acc[rows, HEAD:], top[rows])

        @pl.when(high <= low)
        def _():
            nothing = jnp.zeros((ROWS, 128), jnp.float32)
            for u in range(JOINED):
                finish(u, nothing, nothing, nothing + NEG)

        for n in range(1, KEYS // CHUNK + 1):
            pl.when(high - low == n)(functools.partial(work, n))
        return carry

    stat[...] = jnp.zeros((ROWS, 128), jnp.float32)
    lax.fori_loop(0, Q_BLOCKS // JOINED, one_group, 0)
    turned = stat[...].T
    for d in range(PLANE):
        value = jnp.concatenate(
            [turned[2 * d : 2 * d + 2], turned[Q_BLOCKS + 2 * d : Q_BLOCKS + 2 * d + 2]], axis=0
        )
        first = value.astype(jnp.bfloat16).astype(jnp.float32)
        second = (value - first).astype(jnp.bfloat16).astype(jnp.float32)
        third = value - first - second
        rows = jnp.concatenate([first, second, third, jnp.zeros_like(first)], axis=0)
        o_ref[d, 2 * ROWS :, :] = rows.astype(jnp.bfloat16)


def combine_kernel(heads, blocks, length, m_ref, o_ref):
    values = []
    for d in range(PLANE):
        rows = m_ref[d, 2 * ROWS :, :].astype(jnp.float32)
        values.append(rows[0:4] + rows[4:8] + rows[8:12])
    weights = [None] * PLANE
    for y in range(NY):
        sources = [x * NY + y for x in range(NX)]
        top = values[sources[0]][0:2]
        for d in sources[1:]:
            top = jnp.maximum(top, values[d][0:2])
        parts = [jnp.exp2(values[d][0:2] - top) * values[d][2:4] for d in sources]
        total = parts[0] + parts[1] + parts[2] + parts[3]
        for d, part in zip(sources, parts):
            weights[d] = part / total
    matrix = jnp.concatenate(weights + [jnp.zeros((128 - Q_BLOCKS, 128), jnp.float32)], axis=0).T
    token = lax.broadcasted_iota(jnp.int32, (ROWS, HEAD), 0) % BLOCK
    for y in range(NY):
        for j in range(2):
            out = jnp.zeros((ROWS, HEAD), jnp.float32)
            for x in range(NX):
                d = x * NY + y
                weight = matrix[:, 2 * d + j : 2 * d + j + 1]
                out += weight * m_ref[d, j * ROWS : (j + 1) * ROWS, :].astype(jnp.float32)
            out = jnp.where(blocks[j] * BLOCK + token < length[0], out, 0.0).astype(jnp.bfloat16)
            for g in range(GROUP):
                column = pl.multiple_of((heads[y] * GROUP + g) * HEAD, HEAD)
                o_ref[j * BLOCK : (j + 1) * BLOCK, pl.ds(column, HEAD)] = out[g * BLOCK : (g + 1) * BLOCK]


def ranks(ids):
    return jnp.sum(ids[..., None, :] < ids[..., :, None], axis=-1, dtype=jnp.int32)


def placed(values, rank):
    places = jnp.arange(values.shape[-1], dtype=jnp.int32)
    return jnp.sum(jnp.where(rank[..., None, :] == places[:, None], values[..., None, :], 0), axis=-1, dtype=jnp.int32)


def body(query, rotated_key_value, lengths, block_map, segment_head):
    place = lax.axis_index("blk")
    z, x, y = place // 16, (place // 4) % 4, place % 4
    y_groups = [[4 * g + i for i in range(4)] for g in range(N_BLK // 4)]
    x_groups = [[16 * a + 4 * i + c for i in range(4)] for a in range(NZ) for c in range(NY)]
    planes = [[16 * a + i for i in range(16)] for a in range(NZ)]

    def move(value, target):
        return lax.ppermute(value, "blk", [(s, target(s // 16, (s // 4) % 4, s % 4)) for s in range(N_BLK)])

    def index(zz, xx, yy):
        return (zz % NZ) * 16 + xx * 4 + yy

    def exchange(value, groups):
        return lax.all_to_all(value, "blk", 0, 0, axis_index_groups=groups, tiled=True)

    kv = pl.pallas_call(
        split_kv_kernel,
        out_shape=(jax.ShapeDtypeStruct((128, HEAD), jnp.bfloat16),) * NY,
        in_specs=[SMEM, VMEM],
        out_specs=(VMEM,) * NY,
        name="split_kv",
    )(segment_head, rotated_key_value.reshape(128, KEY_VALUE_HEADS * HEAD))
    line = [kv[0]] + [move(kv[k], lambda a, b, c, k=k: index(a, b, c ^ k)) for k in range(1, NY)]
    own = jnp.concatenate(line, axis=0)
    right = lambda v: move(v, lambda a, b, c: index(a + 1, b, c))
    left = lambda v: move(v, lambda a, b, c: index(a - 1, b, c))
    r1, l1 = right(own), left(own)
    q = pl.pallas_call(
        split_q_kernel,
        out_shape=jax.ShapeDtypeStruct((PLANE, 2 * ROWS, HEAD), jnp.bfloat16),
        in_specs=[SMEM, VMEM],
        out_specs=VMEM,
        compiler_params=SMALL,
        name="split_q",
    )(segment_head, query.reshape(2 * BLOCK, QUERY_HEADS * HEAD))
    q = exchange(q, planes).reshape(Q_BLOCKS, ROWS, HEAD)
    r2, l2 = right(r1), left(l1)
    r3, l3 = right(r2), left(l2)
    half = own.shape[0] // 2
    r4 = move(r2[:half], lambda a, b, c: index(a + 2, b, c))
    l4 = move(l2[half:], lambda a, b, c: index(a - 2, b, c))

    ids = block_map.reshape(NZ, NX, NY, 2).transpose(1, 0, 2, 3).reshape(NX, KEY_BLOCKS)
    rank = ranks(ids)
    ordered = placed(ids, rank)
    mine = lax.dynamic_index_in_dim(ordered, x, 0, keepdims=False)
    my_rank = lax.dynamic_index_in_dim(rank, x, 0, keepdims=False)
    q_ids = lax.dynamic_slice_in_dim(block_map, z * Q_BLOCKS, Q_BLOCKS)
    q_rank = ranks(q_ids)
    q_order = placed(jnp.arange(Q_BLOCKS, dtype=jnp.int32), q_rank)
    q_sorted = placed(q_ids, q_rank)
    grouped = q_sorted.reshape(Q_BLOCKS // JOINED, JOINED)
    lows = jnp.sum(mine[None, :] < grouped[:, :1] - WINDOW // BLOCK, axis=1, dtype=jnp.int32) // CHUNK_BLOCKS
    highs = jnp.sum(mine[None, :] <= grouped[:, -1:], axis=1, dtype=jnp.int32)
    highs = (highs + CHUNK_BLOCKS - 1) // CHUNK_BLOCKS
    table = jnp.concatenate([my_rank, q_order, q_sorted, lows, highs])
    kpos = mine[:, None] * BLOCK + jnp.arange(BLOCK, dtype=jnp.int32)[None, :]
    kpos = kpos.reshape(KEYS // CHUNK, CHUNK)

    pieces = (own, r1, r2, r3, l1, l2, l3, r4, l4)
    picked = pl.pallas_call(
        pick_kernel,
        out_shape=jax.ShapeDtypeStruct((NX, KEY_BLOCKS, 2 * HEAD), jnp.bfloat16),
        in_specs=[VMEM] * 9,
        out_specs=VMEM,
        cost_estimate=pl.CostEstimate(flops=20_000_000, bytes_accessed=1_200_000, transcendentals=0),
        compiler_params=SMALL,
        name="pick",
    )(*pieces)
    picked = move(picked, lambda a, b, c: index(2 * c + a % 2, b, a // 2))
    partial = pl.pallas_call(
        attention_kernel,
        out_shape=jax.ShapeDtypeStruct((PLANE, MESSAGE, HEAD), jnp.bfloat16),
        in_specs=[SMEM] + [VMEM] * 11,
        out_specs=VMEM,
        scratch_shapes=[
            pltpu.VMEM((KEYS, HEAD), jnp.bfloat16),
            pltpu.VMEM((HEAD, KEYS), jnp.bfloat16),
            pltpu.VMEM((KEYS, 2 * HEAD), jnp.bfloat16),
            pltpu.VMEM((KEYS // CHUNK, JOINED * ROWS, CHUNK), jnp.float32),
            pltpu.VMEM((ROWS, 128), jnp.float32),
        ],
        compiler_params=PARAMS,
        cost_estimate=pl.CostEstimate(flops=3_000_000_000, bytes_accessed=4_000_000, transcendentals=5_000_000),
        name="attention",
    )(table, q, kpos, *pieces)
    partial, picked = lax.optimization_barrier((partial, picked))
    out = exchange(partial, planes)

    picked = jnp.concatenate(
        [picked[0]] + [move(picked[k], lambda a, b, c, k=k: index(a, b ^ k, c)) for k in range(1, NX)], axis=0
    )
    blocks = jnp.arange(BLOCKS, dtype=jnp.int32)
    stored = jnp.sum(jnp.where(block_map[None, :] == blocks[:, None], blocks[None, :], 0), axis=1, dtype=jnp.int32)
    from_z, from_y = 2 * y + z % 2, z // 2
    row = ((stored // 8 % NX) ^ x) * KEY_BLOCKS + (stored // 32 - from_z) % NZ * 8
    row = row + ((stored // 2 % NY) ^ from_y) * 2 + stored % 2
    position = blocks * BLOCK + place % BLOCK
    choose = (row[:, None] == blocks[None, :]) & (position < lengths[0])[:, None]
    cache = jnp.dot(choose.astype(jnp.bfloat16), picked, preferred_element_type=jnp.float32).astype(jnp.bfloat16)
    cache = cache.reshape(BLOCKS, 2, HEAD).transpose(1, 0, 2)[None, :, None]

    my_blocks = lax.dynamic_slice_in_dim(block_map, 2 * place, 2)
    attended = pl.pallas_call(
        combine_kernel,
        out_shape=jax.ShapeDtypeStruct((2 * BLOCK, QUERY_HEADS * HEAD), jnp.bfloat16),
        in_specs=[SMEM] * 3 + [VMEM],
        out_specs=VMEM,
        compiler_params=SMALL,
        name="combine",
    )(segment_head, my_blocks, lengths, out)
    return attended.reshape(1, 2 * BLOCK, QUERY_HEADS * HEAD), cache


def solution(mesh):
    return jax.shard_map(
        body,
        mesh=mesh,
        in_specs=(P("req", "blk", None), P("req", None, "blk", None), P("req"), P(), P()),
        out_specs=(P("req", "blk", None), P("req", None, "blk", None, None)),
        check_vma=False,
    )
```

```python
import functools

import jax
import jax.numpy as jnp
from jax import lax
from jax.experimental import pallas as pl
from jax.experimental.pallas import tpu as pltpu
from jax.sharding import PartitionSpec as P

QUERY_HEADS = 16
KEY_VALUE_HEADS = 4
GROUP = QUERY_HEADS // KEY_VALUE_HEADS
HEAD = 128
WINDOW = 4096
BLOCK = 32
BLOCKS = 256
NZ, NX, NY = 8, 4, 4
N_BLK = NZ * NX * NY
PLANE = NX * NY
KEY_BLOCKS = 2 * NZ * NY
Q_BLOCKS = 2 * PLANE
ROWS = GROUP * BLOCK
KEYS = KEY_BLOCKS * BLOCK
JOINED = 4
CHUNK_BLOCKS = 8
CHUNK = CHUNK_BLOCKS * BLOCK
MESSAGE = 2 * ROWS + 16
SCALE = HEAD**-0.5 * 1.4426950408889634
NEG = -1e30
AT_ORDER = KEY_BLOCKS
AT_ID = AT_ORDER + Q_BLOCKS
AT_LOW = AT_ID + Q_BLOCKS
AT_HIGH = AT_LOW + Q_BLOCKS // JOINED

SMEM = pl.BlockSpec(memory_space=pltpu.SMEM)
VMEM = pl.BlockSpec(memory_space=pltpu.VMEM)
PARAMS = pltpu.CompilerParams(vmem_limit_bytes=24 * 1024 * 1024)
SMALL = pltpu.CompilerParams(vmem_limit_bytes=8 * 1024 * 1024)


def split_kv_kernel(heads, kv_ref, *o_refs):
    y = lax.rem(lax.axis_index("blk"), NY)
    for k in range(NY):
        o_refs[k][...] = kv_ref[:, pl.ds(pl.multiple_of(heads[y ^ k] * HEAD, HEAD), HEAD)]


def split_q_kernel(heads, q_ref, o_ref):
    for y in range(NY):
        for g in range(GROUP):
            column = pl.multiple_of((heads[y] * GROUP + g) * HEAD, HEAD)
            for j in range(2):
                tile = q_ref[j * BLOCK : (j + 1) * BLOCK, pl.ds(column, HEAD)]
                for x in range(NX):
                    o_ref[x * NY + y, j * ROWS + g * BLOCK : j * ROWS + (g + 1) * BLOCK] = tile


def arrange(table, pieces, k_scr, kt_scr, v_scr):
    place = lax.axis_index("blk")
    z, y = place // PLANE, lax.rem(place, NY)
    v_scr[:, HEAD:] = jnp.ones((KEYS, HEAD), jnp.bfloat16)
    for piece, zrel, lines in pieces:
        for at, line in enumerate(lines):
            for j in range(2):
                source = (lax.rem(z + zrel, NZ) * NY + (y ^ line)) * 2 + j
                row = pl.multiple_of(table[source] * BLOCK, BLOCK)
                k_scr[pl.ds(row, BLOCK), :] = piece[at * 128 + j * BLOCK : at * 128 + (j + 1) * BLOCK, :]
                v_scr[pl.ds(row, BLOCK), :HEAD] = piece[at * 128 + 64 + j * BLOCK : at * 128 + 64 + (j + 1) * BLOCK, :]
    for t in range(KEYS // 128):
        kt_scr[:, t * 128 : (t + 1) * 128] = k_scr[t * 128 : (t + 1) * 128, :].T


def pick_kernel(*refs):
    own, r1, r2, r3, l1, l2, l3, r4, l4 = refs[:9]
    o_ref = refs[9]
    place = lax.axis_index("blk")
    z, x = place // PLANE, lax.rem(place // NY, NX)

    def select(lines, rows):
        count = 2 * NX * lines * 2
        out = lax.broadcasted_iota(jnp.int32, (count, rows), 0)
        column = lax.broadcasted_iota(jnp.int32, (count, rows), 1)
        half, k, line, j = out // (NX * lines * 2), out // (lines * 2) % NX, out // 2 % lines, out % 2
        offset = lax.rem(z, 2) * 16 + (x ^ k) * NY + z // 2
        wanted = line * 128 + half * 64 + j * BLOCK + offset
        return jnp.where(column == wanted, 1.0, 0.0).astype(jnp.bfloat16)

    whole, part = select(NY, 512), select(NY // 2, 256)
    picked = [jnp.dot(whole, piece[...], preferred_element_type=jnp.float32) for piece in (own, l1, l2, l3)]
    picked.append([jnp.dot(part, piece[...], preferred_element_type=jnp.float32) for piece in (r4, l4)])
    picked += [jnp.dot(whole, piece[...], preferred_element_type=jnp.float32) for piece in (r3, r2, r1)]
    for k in range(NX):
        for half in range(2):
            rows = []
            for piece in picked:
                if isinstance(piece, list):
                    at = (half * NX + k) * 4
                    rows += [piece[0][at : at + 4], piece[1][at : at + 4]]
                else:
                    at = (half * NX + k) * 8
                    rows.append(piece[at : at + 8])
            o_ref[k, :, half * HEAD : (half + 1) * HEAD] = jnp.concatenate(rows, axis=0).astype(jnp.bfloat16)


def attention_kernel(table, q_ref, kpos_ref, *refs):
    pieces, (o_ref, k_scr, kt_scr, v_scr, s_scr, stat) = refs[:9], refs[9:]
    own, r1, r2, r3, l1, l2, l3, r4, l4 = pieces
    every, first, last = range(NY), range(NY // 2), range(NY // 2, NY)
    arrange(
        table,
        [(own, 0, every), (l1, 1, every), (l2, 2, every), (l3, 3, every), (r4, 4, first), (l4, 4, last)]
        + [(r3, 5, every), (r2, 6, every), (r1, 7, every)],
        k_scr,
        kt_scr,
        v_scr,
    )
    lane = lax.broadcasted_iota(jnp.int32, (ROWS, 128), 1)
    token = lax.broadcasted_iota(jnp.int32, (BLOCK, CHUNK), 0)

    def one_group(i, carry):
        low, high = table[AT_LOW + i], table[AT_HIGH + i]
        blocks = [table[AT_ORDER + i * JOINED + u] for u in range(JOINED)]
        ids = [table[AT_ID + i * JOINED + u] for u in range(JOINED)]

        def finish(u, out, total, top):
            place = pl.ds(pl.multiple_of(blocks[u] % 2 * ROWS, ROWS), ROWS)
            o_ref[blocks[u] // 2, place, :] = out.astype(jnp.bfloat16)
            old = jnp.where(lane == blocks[u], top, stat[...])
            stat[...] = jnp.where(lane == blocks[u] + Q_BLOCKS, total, old)

        def work(n):
            q = jnp.concatenate([q_ref[blocks[u]] for u in range(JOINED)], axis=0)
            tops = [None] * (JOINED * GROUP)
            for c in range(n):
                start = pl.multiple_of((low + c) * CHUNK, CHUNK)
                s = jnp.dot(q, kt_scr[:, pl.ds(start, CHUNK)], preferred_element_type=jnp.float32)
                kpos = kpos_ref[pl.ds(low + c, 1), :]
                for u in range(JOINED):
                    distance = (ids[u] * BLOCK + token) - kpos
                    bias = jnp.where((distance >= 0) & (distance < WINDOW), 0.0, NEG)
                    for g in range(GROUP):
                        r = u * GROUP + g
                        part = s[r * BLOCK : (r + 1) * BLOCK] + bias
                        s_scr[c, r * BLOCK : (r + 1) * BLOCK, :] = part
                        wide = jnp.maximum(part[:, :128], part[:, 128:])
                        tops[r] = wide if tops[r] is None else jnp.maximum(tops[r], wide)
            top = jnp.max(jnp.concatenate(tops, axis=0), axis=1, keepdims=True) * SCALE
            top = jnp.broadcast_to(top, (JOINED * ROWS, 128))
            twice = jnp.concatenate([top, top], axis=1)
            acc = None
            for c in range(n):
                start = pl.multiple_of((low + c) * CHUNK, CHUNK)
                p = jnp.exp2(s_scr[c] * SCALE - twice).astype(jnp.bfloat16)
                part = jnp.dot(p, v_scr[pl.ds(start, CHUNK), :], preferred_element_type=jnp.float32)
                acc = part if acc is None else acc + part
            for u in range(JOINED):
                rows = slice(u * ROWS, (u + 1) * ROWS)
                finish(u, acc[rows, :HEAD] / acc[rows, HEAD:], acc[rows, HEAD:], top[rows])

        @pl.when(high <= low)
        def _():
            nothing = jnp.zeros((ROWS, 128), jnp.float32)
            for u in range(JOINED):
                finish(u, nothing, nothing, nothing + NEG)

        for n in range(1, KEYS // CHUNK + 1):
            pl.when(high - low == n)(functools.partial(work, n))
        return carry

    stat[...] = jnp.zeros((ROWS, 128), jnp.float32)
    lax.fori_loop(0, Q_BLOCKS // JOINED, one_group, 0)
    turned = stat[...].T
    for d in range(PLANE):
        value = jnp.concatenate(
            [turned[2 * d : 2 * d + 2], turned[Q_BLOCKS + 2 * d : Q_BLOCKS + 2 * d + 2]], axis=0
        )
        first = value.astype(jnp.bfloat16).astype(jnp.float32)
        second = (value - first).astype(jnp.bfloat16).astype(jnp.float32)
        third = value - first - second
        rows = jnp.concatenate([first, second, third, jnp.zeros_like(first)], axis=0)
        o_ref[d, 2 * ROWS :, :] = rows.astype(jnp.bfloat16)


def combine_kernel(heads, blocks, length, choose_ref, k0_ref, k1_ref, k2_ref, k3_ref, m_ref, o_ref, cache_ref):
    found = jnp.concatenate([k0_ref[0], k1_ref[...], k2_ref[...], k3_ref[...]], axis=0)
    for half in range(2):
        cache = jnp.dot(choose_ref[...], found[:, half * HEAD : (half + 1) * HEAD], preferred_element_type=jnp.float32)
        cache_ref[half] = cache.astype(jnp.bfloat16)
    values = []
    for d in range(PLANE):
        rows = m_ref[d, 2 * ROWS :, :].astype(jnp.float32)
        values.append(rows[0:4] + rows[4:8] + rows[8:12])
    weights = [None] * PLANE
    for y in range(NY):
        sources = [x * NY + y for x in range(NX)]
        top = values[sources[0]][0:2]
        for d in sources[1:]:
            top = jnp.maximum(top, values[d][0:2])
        parts = [jnp.exp2(values[d][0:2] - top) * values[d][2:4] for d in sources]
        total = parts[0] + parts[1] + parts[2] + parts[3]
        for d, part in zip(sources, parts):
            weights[d] = part / total
    matrix = jnp.concatenate(weights + [jnp.zeros((128 - Q_BLOCKS, 128), jnp.float32)], axis=0).T
    token = lax.broadcasted_iota(jnp.int32, (ROWS, HEAD), 0) % BLOCK
    for y in range(NY):
        for j in range(2):
            out = jnp.zeros((ROWS, HEAD), jnp.float32)
            for x in range(NX):
                d = x * NY + y
                weight = matrix[:, 2 * d + j : 2 * d + j + 1]
                out += weight * m_ref[d, j * ROWS : (j + 1) * ROWS, :].astype(jnp.float32)
            out = jnp.where(blocks[j] * BLOCK + token < length[0], out, 0.0).astype(jnp.bfloat16)
            for g in range(GROUP):
                column = pl.multiple_of((heads[y] * GROUP + g) * HEAD, HEAD)
                o_ref[j * BLOCK : (j + 1) * BLOCK, pl.ds(column, HEAD)] = out[g * BLOCK : (g + 1) * BLOCK]


def ranks(ids):
    return jnp.sum(ids[..., None, :] < ids[..., :, None], axis=-1, dtype=jnp.int32)


def placed(values, rank):
    places = jnp.arange(values.shape[-1], dtype=jnp.int32)
    return jnp.sum(jnp.where(rank[..., None, :] == places[:, None], values[..., None, :], 0), axis=-1, dtype=jnp.int32)


def body(query, rotated_key_value, lengths, block_map, segment_head):
    place = lax.axis_index("blk")
    z, x, y = place // 16, (place // 4) % 4, place % 4
    y_groups = [[4 * g + i for i in range(4)] for g in range(N_BLK // 4)]
    x_groups = [[16 * a + 4 * i + c for i in range(4)] for a in range(NZ) for c in range(NY)]
    planes = [[16 * a + i for i in range(16)] for a in range(NZ)]

    def move(value, target):
        return lax.ppermute(value, "blk", [(s, target(s // 16, (s // 4) % 4, s % 4)) for s in range(N_BLK)])

    def index(zz, xx, yy):
        return (zz % NZ) * 16 + xx * 4 + yy

    def exchange(value, groups):
        return lax.all_to_all(value, "blk", 0, 0, axis_index_groups=groups, tiled=True)

    kv = pl.pallas_call(
        split_kv_kernel,
        out_shape=(jax.ShapeDtypeStruct((128, HEAD), jnp.bfloat16),) * NY,
        in_specs=[SMEM, VMEM],
        out_specs=(VMEM,) * NY,
        name="split_kv",
    )(segment_head, rotated_key_value.reshape(128, KEY_VALUE_HEADS * HEAD))
    line = [kv[0]] + [move(kv[k], lambda a, b, c, k=k: index(a, b, c ^ k)) for k in range(1, NY)]
    own = jnp.concatenate(line, axis=0)
    right = lambda v: move(v, lambda a, b, c: index(a + 1, b, c))
    left = lambda v: move(v, lambda a, b, c: index(a - 1, b, c))
    r1, l1 = right(own), left(own)
    q = pl.pallas_call(
        split_q_kernel,
        out_shape=jax.ShapeDtypeStruct((PLANE, 2 * ROWS, HEAD), jnp.bfloat16),
        in_specs=[SMEM, VMEM],
        out_specs=VMEM,
        compiler_params=SMALL,
        name="split_q",
    )(segment_head, query.reshape(2 * BLOCK, QUERY_HEADS * HEAD))
    q = exchange(q, planes).reshape(Q_BLOCKS, ROWS, HEAD)
    r2, l2 = right(r1), left(l1)
    r3, l3 = right(r2), left(l2)
    half = own.shape[0] // 2
    r4 = move(r2[:half], lambda a, b, c: index(a + 2, b, c))
    l4 = move(l2[half:], lambda a, b, c: index(a - 2, b, c))

    ids = block_map.reshape(NZ, NX, NY, 2).transpose(1, 0, 2, 3).reshape(NX, KEY_BLOCKS)
    rank = ranks(ids)
    ordered = placed(ids, rank)
    mine = lax.dynamic_index_in_dim(ordered, x, 0, keepdims=False)
    my_rank = lax.dynamic_index_in_dim(rank, x, 0, keepdims=False)
    q_ids = lax.dynamic_slice_in_dim(block_map, z * Q_BLOCKS, Q_BLOCKS)
    q_rank = ranks(q_ids)
    q_order = placed(jnp.arange(Q_BLOCKS, dtype=jnp.int32), q_rank)
    q_sorted = placed(q_ids, q_rank)
    grouped = q_sorted.reshape(Q_BLOCKS // JOINED, JOINED)
    lows = jnp.sum(mine[None, :] < grouped[:, :1] - WINDOW // BLOCK, axis=1, dtype=jnp.int32) // CHUNK_BLOCKS
    highs = jnp.sum(mine[None, :] <= grouped[:, -1:], axis=1, dtype=jnp.int32)
    highs = (highs + CHUNK_BLOCKS - 1) // CHUNK_BLOCKS
    table = jnp.concatenate([my_rank, q_order, q_sorted, lows, highs])
    kpos = mine[:, None] * BLOCK + jnp.arange(BLOCK, dtype=jnp.int32)[None, :]
    kpos = kpos.reshape(KEYS // CHUNK, CHUNK)

    pieces = (own, r1, r2, r3, l1, l2, l3, r4, l4)
    picked = pl.pallas_call(
        pick_kernel,
        out_shape=jax.ShapeDtypeStruct((NX, KEY_BLOCKS, 2 * HEAD), jnp.bfloat16),
        in_specs=[VMEM] * 9,
        out_specs=VMEM,
        cost_estimate=pl.CostEstimate(flops=20_000_000, bytes_accessed=1_200_000, transcendentals=0),
        compiler_params=SMALL,
        name="pick",
    )(*pieces)
    picked = move(picked, lambda a, b, c: index(2 * c + a % 2, b, a // 2))
    partial = pl.pallas_call(
        attention_kernel,
        out_shape=jax.ShapeDtypeStruct((PLANE, MESSAGE, HEAD), jnp.bfloat16),
        in_specs=[SMEM] + [VMEM] * 11,
        out_specs=VMEM,
        scratch_shapes=[
            pltpu.VMEM((KEYS, HEAD), jnp.bfloat16),
            pltpu.VMEM((HEAD, KEYS), jnp.bfloat16),
            pltpu.VMEM((KEYS, 2 * HEAD), jnp.bfloat16),
            pltpu.VMEM((KEYS // CHUNK, JOINED * ROWS, CHUNK), jnp.float32),
            pltpu.VMEM((ROWS, 128), jnp.float32),
        ],
        compiler_params=PARAMS,
        cost_estimate=pl.CostEstimate(flops=3_000_000_000, bytes_accessed=4_000_000, transcendentals=5_000_000),
        name="attention",
    )(table, q, kpos, *pieces)
    partial, picked = lax.optimization_barrier((partial, picked))
    out = exchange(partial, planes)

    kept = [move(picked[k], lambda a, b, c, k=k: index(a, b ^ k, c)) for k in range(1, NX)]
    blocks = jnp.arange(BLOCKS, dtype=jnp.int32)
    stored = jnp.sum(jnp.where(block_map[None, :] == blocks[:, None], blocks[None, :], 0), axis=1, dtype=jnp.int32)
    from_z, from_y = 2 * y + z % 2, z // 2
    row = ((stored // 8 % NX) ^ x) * KEY_BLOCKS + (stored // 32 - from_z) % NZ * 8
    row = row + ((stored // 2 % NY) ^ from_y) * 2 + stored % 2
    position = blocks * BLOCK + place % BLOCK
    choose = (row[:, None] == blocks[None, :]) & (position < lengths[0])[:, None]
    choose = choose.astype(jnp.bfloat16)
    my_blocks = lax.dynamic_slice_in_dim(block_map, 2 * place, 2)
    attended, cache = pl.pallas_call(
        combine_kernel,
        out_shape=(
            jax.ShapeDtypeStruct((2 * BLOCK, QUERY_HEADS * HEAD), jnp.bfloat16),
            jax.ShapeDtypeStruct((2, BLOCKS, HEAD), jnp.bfloat16),
        ),
        in_specs=[SMEM] * 3 + [VMEM] * 6,
        out_specs=(VMEM, VMEM),
        compiler_params=SMALL,
        name="combine",
    )(segment_head, my_blocks, lengths, choose, picked, *kept, out)
    return attended.reshape(1, 2 * BLOCK, QUERY_HEADS * HEAD), cache[None, :, None]


def solution(mesh):
    return jax.shard_map(
        body,
        mesh=mesh,
        in_specs=(P("req", "blk", None), P("req", None, "blk", None), P("req"), P(), P()),
        out_specs=(P("req", "blk", None), P("req", None, "blk", None, None)),
        check_vma=False,
    )
```

```python
import functools

import jax
import jax.numpy as jnp
from jax import lax
from jax.experimental import pallas as pl
from jax.experimental.pallas import tpu as pltpu
from jax.sharding import PartitionSpec as P

QUERY_HEADS = 16
KEY_VALUE_HEADS = 4
GROUP = QUERY_HEADS // KEY_VALUE_HEADS
HEAD = 128
WINDOW = 4096
BLOCK = 32
BLOCKS = 256
NZ, NX, NY = 8, 4, 4
N_BLK = NZ * NX * NY
PLANE = NX * NY
KEY_BLOCKS = 2 * NZ * NY
Q_BLOCKS = 2 * PLANE
ROWS = GROUP * BLOCK
KEYS = KEY_BLOCKS * BLOCK
JOINED = 4
CHUNK_BLOCKS = 8
CHUNK = CHUNK_BLOCKS * BLOCK
MESSAGE = 2 * ROWS + 16
SCALE = HEAD**-0.5 * 1.4426950408889634
NEG = -1e30
AT_ORDER = KEY_BLOCKS
AT_ID = AT_ORDER + Q_BLOCKS
AT_LOW = AT_ID + Q_BLOCKS
AT_HIGH = AT_LOW + Q_BLOCKS // JOINED

SMEM = pl.BlockSpec(memory_space=pltpu.SMEM)
VMEM = pl.BlockSpec(memory_space=pltpu.VMEM)
PARAMS = pltpu.CompilerParams(vmem_limit_bytes=24 * 1024 * 1024)
SMALL = pltpu.CompilerParams(vmem_limit_bytes=8 * 1024 * 1024)


def split_kv_kernel(heads, kv_ref, *o_refs):
    y = lax.rem(lax.axis_index("blk"), NY)
    for k in range(NY):
        o_refs[k][...] = kv_ref[:, pl.ds(pl.multiple_of(heads[y ^ k] * HEAD, HEAD), HEAD)]


def split_q_kernel(heads, q_ref, o_ref):
    for y in range(NY):
        for g in range(GROUP):
            column = pl.multiple_of((heads[y] * GROUP + g) * HEAD, HEAD)
            for j in range(2):
                tile = q_ref[j * BLOCK : (j + 1) * BLOCK, pl.ds(column, HEAD)]
                for x in range(NX):
                    o_ref[x * NY + y, j * ROWS + g * BLOCK : j * ROWS + (g + 1) * BLOCK] = tile


def arrange(table, pieces, k_scr, kt_scr, v_scr):
    place = lax.axis_index("blk")
    z, y = place // PLANE, lax.rem(place, NY)
    v_scr[:, HEAD:] = jnp.ones((KEYS, HEAD), jnp.bfloat16)
    for piece, zrel, lines in pieces:
        for at, line in enumerate(lines):
            for j in range(2):
                source = (lax.rem(z + zrel, NZ) * NY + (y ^ line)) * 2 + j
                row = pl.multiple_of(table[source] * BLOCK, BLOCK)
                k_scr[pl.ds(row, BLOCK), :] = piece[at * 128 + j * BLOCK : at * 128 + (j + 1) * BLOCK, :]
                v_scr[pl.ds(row, BLOCK), :HEAD] = piece[at * 128 + 64 + j * BLOCK : at * 128 + 64 + (j + 1) * BLOCK, :]
    for t in range(KEYS // 128):
        kt_scr[:, t * 128 : (t + 1) * 128] = k_scr[t * 128 : (t + 1) * 128, :].T


def pick_kernel(*refs):
    own, r1, r2, r3, l1, l2, l3, r4, l4 = refs[:9]
    o_ref = refs[9]
    place = lax.axis_index("blk")
    z, x = place // PLANE, lax.rem(place // NY, NX)

    def select(lines, rows):
        count = 2 * NX * lines * 2
        out = lax.broadcasted_iota(jnp.int32, (count, rows), 0)
        column = lax.broadcasted_iota(jnp.int32, (count, rows), 1)
        half, k, line, j = out // (NX * lines * 2), out // (lines * 2) % NX, out // 2 % lines, out % 2
        offset = lax.rem(z, 2) * 16 + (x ^ k) * NY + z // 2
        wanted = line * 128 + half * 64 + j * BLOCK + offset
        return jnp.where(column == wanted, 1.0, 0.0).astype(jnp.bfloat16)

    whole, part = select(NY, 512), select(NY // 2, 256)
    picked = [jnp.dot(whole, piece[...], preferred_element_type=jnp.float32) for piece in (own, l1, l2, l3)]
    picked.append([jnp.dot(part, piece[...], preferred_element_type=jnp.float32) for piece in (r4, l4)])
    picked += [jnp.dot(whole, piece[...], preferred_element_type=jnp.float32) for piece in (r3, r2, r1)]
    for k in range(NX):
        for half in range(2):
            rows = []
            for piece in picked:
                if isinstance(piece, list):
                    at = (half * NX + k) * 4
                    rows += [piece[0][at : at + 4], piece[1][at : at + 4]]
                else:
                    at = (half * NX + k) * 8
                    rows.append(piece[at : at + 8])
            o_ref[k, :, half * HEAD : (half + 1) * HEAD] = jnp.concatenate(rows, axis=0).astype(jnp.bfloat16)


def attention_kernel(table, q_ref, kpos_ref, *refs):
    pieces, (o_ref, k_scr, kt_scr, v_scr, s_scr, stat) = refs[:9], refs[9:]
    own, r1, r2, r3, l1, l2, l3, r4, l4 = pieces
    every, first, last = range(NY), range(NY // 2), range(NY // 2, NY)
    arrange(
        table,
        [(own, 0, every), (l1, 1, every), (l2, 2, every), (l3, 3, every), (r4, 4, first), (l4, 4, last)]
        + [(r3, 5, every), (r2, 6, every), (r1, 7, every)],
        k_scr,
        kt_scr,
        v_scr,
    )
    lane = lax.broadcasted_iota(jnp.int32, (ROWS, 128), 1)
    token = lax.broadcasted_iota(jnp.int32, (BLOCK, CHUNK), 0)

    def one_group(i, carry):
        low, high = table[AT_LOW + i], table[AT_HIGH + i]
        blocks = [table[AT_ORDER + i * JOINED + u] for u in range(JOINED)]
        ids = [table[AT_ID + i * JOINED + u] for u in range(JOINED)]

        def finish(u, out, total, top):
            place = pl.ds(pl.multiple_of(blocks[u] % 2 * ROWS, ROWS), ROWS)
            o_ref[blocks[u] // 2, place, :] = out.astype(jnp.bfloat16)
            old = jnp.where(lane == blocks[u], top, stat[...])
            stat[...] = jnp.where(lane == blocks[u] + Q_BLOCKS, total, old)

        def work(n):
            q = jnp.concatenate([q_ref[blocks[u]] for u in range(JOINED)], axis=0)
            tops = [None] * (JOINED * GROUP)
            for c in range(n):
                start = pl.multiple_of((low + c) * CHUNK, CHUNK)
                s = jnp.dot(q, kt_scr[:, pl.ds(start, CHUNK)], preferred_element_type=jnp.float32)
                kpos = kpos_ref[pl.ds(low + c, 1), :]
                for u in range(JOINED):
                    distance = (ids[u] * BLOCK + token) - kpos
                    bias = jnp.where((distance >= 0) & (distance < WINDOW), 0.0, NEG)
                    for g in range(GROUP):
                        r = u * GROUP + g
                        part = s[r * BLOCK : (r + 1) * BLOCK] + bias
                        s_scr[c, r * BLOCK : (r + 1) * BLOCK, :] = part
                        wide = jnp.maximum(part[:, :128], part[:, 128:])
                        tops[r] = wide if tops[r] is None else jnp.maximum(tops[r], wide)
            top = jnp.max(jnp.concatenate(tops, axis=0), axis=1, keepdims=True) * SCALE
            top = jnp.broadcast_to(top, (JOINED * ROWS, 128))
            twice = jnp.concatenate([top, top], axis=1)
            acc = None
            for c in range(n):
                start = pl.multiple_of((low + c) * CHUNK, CHUNK)
                p = jnp.exp2(s_scr[c] * SCALE - twice).astype(jnp.bfloat16)
                part = jnp.dot(p, v_scr[pl.ds(start, CHUNK), :], preferred_element_type=jnp.float32)
                acc = part if acc is None else acc + part
            for u in range(JOINED):
                rows = slice(u * ROWS, (u + 1) * ROWS)
                finish(u, acc[rows, :HEAD] / acc[rows, HEAD:], acc[rows, HEAD:], top[rows])

        @pl.when(high <= low)
        def _():
            nothing = jnp.zeros((ROWS, 128), jnp.float32)
            for u in range(JOINED):
                finish(u, nothing, nothing, nothing + NEG)

        for n in range(1, KEYS // CHUNK + 1):
            pl.when(high - low == n)(functools.partial(work, n))
        return carry

    stat[...] = jnp.zeros((ROWS, 128), jnp.float32)
    lax.fori_loop(0, Q_BLOCKS // JOINED, one_group, 0)
    turned = stat[...].T
    for d in range(PLANE):
        value = jnp.concatenate(
            [turned[2 * d : 2 * d + 2], turned[Q_BLOCKS + 2 * d : Q_BLOCKS + 2 * d + 2]], axis=0
        )
        first = value.astype(jnp.bfloat16).astype(jnp.float32)
        second = (value - first).astype(jnp.bfloat16).astype(jnp.float32)
        third = value - first - second
        rows = jnp.concatenate([first, second, third, jnp.zeros_like(first)], axis=0)
        o_ref[d, 2 * ROWS :, :] = rows.astype(jnp.bfloat16)


def combine_kernel(heads, blocks, length, choose_ref, k0_ref, k1_ref, k2_ref, k3_ref, m_ref, o_ref, cache_ref):
    found = jnp.concatenate([k0_ref[0], k1_ref[...], k2_ref[...], k3_ref[...]], axis=0)
    for half in range(2):
        cache = jnp.dot(choose_ref[...], found[:, half * HEAD : (half + 1) * HEAD], preferred_element_type=jnp.float32)
        cache_ref[half] = cache.astype(jnp.bfloat16)
    values = []
    for d in range(PLANE):
        rows = m_ref[d, 2 * ROWS :, :].astype(jnp.float32)
        values.append(rows[0:4] + rows[4:8] + rows[8:12])
    weights = [None] * PLANE
    for y in range(NY):
        sources = [x * NY + y for x in range(NX)]
        top = values[sources[0]][0:2]
        for d in sources[1:]:
            top = jnp.maximum(top, values[d][0:2])
        parts = [jnp.exp2(values[d][0:2] - top) * values[d][2:4] for d in sources]
        total = parts[0] + parts[1] + parts[2] + parts[3]
        for d, part in zip(sources, parts):
            weights[d] = part / total
    matrix = jnp.concatenate(weights + [jnp.zeros((128 - Q_BLOCKS, 128), jnp.float32)], axis=0).T
    token = lax.broadcasted_iota(jnp.int32, (ROWS, HEAD), 0) % BLOCK
    for y in range(NY):
        for j in range(2):
            out = jnp.zeros((ROWS, HEAD), jnp.float32)
            for x in range(NX):
                d = x * NY + y
                weight = matrix[:, 2 * d + j : 2 * d + j + 1]
                out += weight * m_ref[d, j * ROWS : (j + 1) * ROWS, :].astype(jnp.float32)
            out = jnp.where(blocks[j] * BLOCK + token < length[0], out, 0.0).astype(jnp.bfloat16)
            for g in range(GROUP):
                column = pl.multiple_of((heads[y] * GROUP + g) * HEAD, HEAD)
                o_ref[j * BLOCK : (j + 1) * BLOCK, pl.ds(column, HEAD)] = out[g * BLOCK : (g + 1) * BLOCK]


def ranks(ids):
    return jnp.sum(ids[..., None, :] < ids[..., :, None], axis=-1, dtype=jnp.int32)


def placed(values, rank):
    places = jnp.arange(values.shape[-1], dtype=jnp.int32)
    return jnp.sum(jnp.where(rank[..., None, :] == places[:, None], values[..., None, :], 0), axis=-1, dtype=jnp.int32)


def body(query, rotated_key_value, lengths, block_map, segment_head):
    place = lax.axis_index("blk")
    z, x, y = place // 16, (place // 4) % 4, place % 4
    y_groups = [[4 * g + i for i in range(4)] for g in range(N_BLK // 4)]
    x_groups = [[16 * a + 4 * i + c for i in range(4)] for a in range(NZ) for c in range(NY)]
    planes = [[16 * a + i for i in range(16)] for a in range(NZ)]

    def move(value, target):
        return lax.ppermute(value, "blk", [(s, target(s // 16, (s // 4) % 4, s % 4)) for s in range(N_BLK)])

    def index(zz, xx, yy):
        return (zz % NZ) * 16 + xx * 4 + yy

    def exchange(value, groups):
        return lax.all_to_all(value, "blk", 0, 0, axis_index_groups=groups, tiled=True)

    kv = pl.pallas_call(
        split_kv_kernel,
        out_shape=(jax.ShapeDtypeStruct((128, HEAD), jnp.bfloat16),) * NY,
        in_specs=[SMEM, VMEM],
        out_specs=(VMEM,) * NY,
        name="split_kv",
    )(segment_head, rotated_key_value.reshape(128, KEY_VALUE_HEADS * HEAD))
    line = [kv[0]] + [move(kv[k], lambda a, b, c, k=k: index(a, b, c ^ k)) for k in range(1, NY)]
    own = jnp.concatenate(line, axis=0)
    right = lambda v: move(v, lambda a, b, c: index(a + 1, b, c))
    left = lambda v: move(v, lambda a, b, c: index(a - 1, b, c))
    r1, l1 = right(own), left(own)
    q = pl.pallas_call(
        split_q_kernel,
        out_shape=jax.ShapeDtypeStruct((PLANE, 2 * ROWS, HEAD), jnp.bfloat16),
        in_specs=[SMEM, VMEM],
        out_specs=VMEM,
        compiler_params=SMALL,
        name="split_q",
    )(segment_head, query.reshape(2 * BLOCK, QUERY_HEADS * HEAD))
    q = exchange(q, planes).reshape(Q_BLOCKS, ROWS, HEAD)
    r2, l2 = right(r1), left(l1)
    r3, l3 = right(r2), left(l2)
    half = own.shape[0] // 2
    r4 = move(r2[:half], lambda a, b, c: index(a + 2, b, c))
    l4 = move(l2[half:], lambda a, b, c: index(a - 2, b, c))

    block_map, _ = lax.optimization_barrier((block_map, l1))

    ids = block_map.reshape(NZ, NX, NY, 2).transpose(1, 0, 2, 3).reshape(NX, KEY_BLOCKS)
    rank = ranks(ids)
    ordered = placed(ids, rank)
    mine = lax.dynamic_index_in_dim(ordered, x, 0, keepdims=False)
    my_rank = lax.dynamic_index_in_dim(rank, x, 0, keepdims=False)
    q_ids = lax.dynamic_slice_in_dim(block_map, z * Q_BLOCKS, Q_BLOCKS)
    q_rank = ranks(q_ids)
    q_order = placed(jnp.arange(Q_BLOCKS, dtype=jnp.int32), q_rank)
    q_sorted = placed(q_ids, q_rank)
    grouped = q_sorted.reshape(Q_BLOCKS // JOINED, JOINED)
    lows = jnp.sum(mine[None, :] < grouped[:, :1] - WINDOW // BLOCK, axis=1, dtype=jnp.int32) // CHUNK_BLOCKS
    highs = jnp.sum(mine[None, :] <= grouped[:, -1:], axis=1, dtype=jnp.int32)
    highs = (highs + CHUNK_BLOCKS - 1) // CHUNK_BLOCKS
    table = jnp.concatenate([my_rank, q_order, q_sorted, lows, highs])
    kpos = mine[:, None] * BLOCK + jnp.arange(BLOCK, dtype=jnp.int32)[None, :]
    kpos = kpos.reshape(KEYS // CHUNK, CHUNK)

    pieces = (own, r1, r2, r3, l1, l2, l3, r4, l4)
    picked = pl.pallas_call(
        pick_kernel,
        out_shape=jax.ShapeDtypeStruct((NX, KEY_BLOCKS, 2 * HEAD), jnp.bfloat16),
        in_specs=[VMEM] * 9,
        out_specs=VMEM,
        cost_estimate=pl.CostEstimate(flops=20_000_000, bytes_accessed=1_200_000, transcendentals=0),
        compiler_params=SMALL,
        name="pick",
    )(*pieces)
    picked = move(picked, lambda a, b, c: index(2 * c + a % 2, b, a // 2))
    partial = pl.pallas_call(
        attention_kernel,
        out_shape=jax.ShapeDtypeStruct((PLANE, MESSAGE, HEAD), jnp.bfloat16),
        in_specs=[SMEM] + [VMEM] * 11,
        out_specs=VMEM,
        scratch_shapes=[
            pltpu.VMEM((KEYS, HEAD), jnp.bfloat16),
            pltpu.VMEM((HEAD, KEYS), jnp.bfloat16),
            pltpu.VMEM((KEYS, 2 * HEAD), jnp.bfloat16),
            pltpu.VMEM((KEYS // CHUNK, JOINED * ROWS, CHUNK), jnp.float32),
            pltpu.VMEM((ROWS, 128), jnp.float32),
        ],
        compiler_params=PARAMS,
        cost_estimate=pl.CostEstimate(flops=3_000_000_000, bytes_accessed=4_000_000, transcendentals=5_000_000),
        name="attention",
    )(table, q, kpos, *pieces)
    partial, picked = lax.optimization_barrier((partial, picked))
    out = exchange(partial, planes)

    kept = [move(picked[k], lambda a, b, c, k=k: index(a, b ^ k, c)) for k in range(1, NX)]
    blocks = jnp.arange(BLOCKS, dtype=jnp.int32)
    stored = jnp.sum(jnp.where(block_map[None, :] == blocks[:, None], blocks[None, :], 0), axis=1, dtype=jnp.int32)
    from_z, from_y = 2 * y + z % 2, z // 2
    row = ((stored // 8 % NX) ^ x) * KEY_BLOCKS + (stored // 32 - from_z) % NZ * 8
    row = row + ((stored // 2 % NY) ^ from_y) * 2 + stored % 2
    position = blocks * BLOCK + place % BLOCK
    choose = (row[:, None] == blocks[None, :]) & (position < lengths[0])[:, None]
    choose = choose.astype(jnp.bfloat16)
    my_blocks = lax.dynamic_slice_in_dim(block_map, 2 * place, 2)
    attended, cache = pl.pallas_call(
        combine_kernel,
        out_shape=(
            jax.ShapeDtypeStruct((2 * BLOCK, QUERY_HEADS * HEAD), jnp.bfloat16),
            jax.ShapeDtypeStruct((2, BLOCKS, HEAD), jnp.bfloat16),
        ),
        in_specs=[SMEM] * 3 + [VMEM] * 6,
        out_specs=(VMEM, VMEM),
        compiler_params=SMALL,
        name="combine",
    )(segment_head, my_blocks, lengths, choose, picked, *kept, out)
    return attended.reshape(1, 2 * BLOCK, QUERY_HEADS * HEAD), cache[None, :, None]


def solution(mesh):
    return jax.shard_map(
        body,
        mesh=mesh,
        in_specs=(P("req", "blk", None), P("req", None, "blk", None), P("req"), P(), P()),
        out_specs=(P("req", "blk", None), P("req", None, "blk", None, None)),
        check_vma=False,
    )
```

```python
import functools

import jax
import jax.numpy as jnp
from jax import lax
from jax.experimental import pallas as pl
from jax.experimental.pallas import tpu as pltpu
from jax.sharding import PartitionSpec as P

QUERY_HEADS = 16
KEY_VALUE_HEADS = 4
GROUP = QUERY_HEADS // KEY_VALUE_HEADS
HEAD = 128
WINDOW = 4096
BLOCK = 32
BLOCKS = 256
NZ, NX, NY = 8, 4, 4
N_BLK = NZ * NX * NY
PLANE = NX * NY
KEY_BLOCKS = 2 * NZ * NY
Q_BLOCKS = 2 * PLANE
ROWS = GROUP * BLOCK
KEYS = KEY_BLOCKS * BLOCK
JOINED = 4
CHUNK_BLOCKS = 8
CHUNK = CHUNK_BLOCKS * BLOCK
MESSAGE = 2 * ROWS + 16
SCALE = HEAD**-0.5 * 1.4426950408889634
NEG = -1e30
AT_ORDER = KEY_BLOCKS
AT_ID = AT_ORDER + Q_BLOCKS
AT_LOW = AT_ID + Q_BLOCKS
AT_HIGH = AT_LOW + Q_BLOCKS // JOINED

SMEM = pl.BlockSpec(memory_space=pltpu.SMEM)
VMEM = pl.BlockSpec(memory_space=pltpu.VMEM)
PARAMS = pltpu.CompilerParams(vmem_limit_bytes=24 * 1024 * 1024)
SMALL = pltpu.CompilerParams(vmem_limit_bytes=8 * 1024 * 1024)


def split_kv_kernel(heads, kv_ref, *o_refs):
    y = lax.rem(lax.axis_index("blk"), NY)
    for k in range(NY):
        o_refs[k][...] = kv_ref[:, pl.ds(pl.multiple_of(heads[y ^ k] * HEAD, HEAD), HEAD)]


def split_q_kernel(heads, q_ref, o_ref):
    for y in range(NY):
        for g in range(GROUP):
            column = pl.multiple_of((heads[y] * GROUP + g) * HEAD, HEAD)
            for j in range(2):
                tile = q_ref[j * BLOCK : (j + 1) * BLOCK, pl.ds(column, HEAD)]
                for x in range(NX):
                    o_ref[x * NY + y, j * ROWS + g * BLOCK : j * ROWS + (g + 1) * BLOCK] = tile


def arrange(table, pieces, k_scr, kt_scr, v_scr):
    place = lax.axis_index("blk")
    z, y = place // PLANE, lax.rem(place, NY)
    v_scr[:, HEAD:] = jnp.ones((KEYS, HEAD), jnp.bfloat16)
    for piece, zrel, lines in pieces:
        for at, line in enumerate(lines):
            for j in range(2):
                source = (lax.rem(z + zrel, NZ) * NY + (y ^ line)) * 2 + j
                row = pl.multiple_of(table[source] * BLOCK, BLOCK)
                k_scr[pl.ds(row, BLOCK), :] = piece[at * 128 + j * BLOCK : at * 128 + (j + 1) * BLOCK, :]
                v_scr[pl.ds(row, BLOCK), :HEAD] = piece[at * 128 + 64 + j * BLOCK : at * 128 + 64 + (j + 1) * BLOCK, :]
    for t in range(KEYS // 128):
        kt_scr[:, t * 128 : (t + 1) * 128] = k_scr[t * 128 : (t + 1) * 128, :].T


def pick_kernel(*refs):
    own, r1, r2, r3, l1, l2, l3, r4, l4 = refs[:9]
    o_ref = refs[9]
    place = lax.axis_index("blk")
    z, x = place // PLANE, lax.rem(place // NY, NX)

    def select(lines, rows):
        count = 2 * NX * lines * 2
        out = lax.broadcasted_iota(jnp.int32, (count, rows), 0)
        column = lax.broadcasted_iota(jnp.int32, (count, rows), 1)
        half, k, line, j = out // (NX * lines * 2), out // (lines * 2) % NX, out // 2 % lines, out % 2
        offset = lax.rem(z, 2) * 16 + (x ^ k) * NY + z // 2
        wanted = line * 128 + half * 64 + j * BLOCK + offset
        return jnp.where(column == wanted, 1.0, 0.0).astype(jnp.bfloat16)

    whole, part = select(NY, 512), select(NY // 2, 256)
    picked = [jnp.dot(whole, piece[...], preferred_element_type=jnp.float32) for piece in (own, l1, l2, l3)]
    picked.append([jnp.dot(part, piece[...], preferred_element_type=jnp.float32) for piece in (r4, l4)])
    picked += [jnp.dot(whole, piece[...], preferred_element_type=jnp.float32) for piece in (r3, r2, r1)]
    for k in range(NX):
        for half in range(2):
            rows = []
            for piece in picked:
                if isinstance(piece, list):
                    at = (half * NX + k) * 4
                    rows += [piece[0][at : at + 4], piece[1][at : at + 4]]
                else:
                    at = (half * NX + k) * 8
                    rows.append(piece[at : at + 8])
            o_ref[k, :, half * HEAD : (half + 1) * HEAD] = jnp.concatenate(rows, axis=0).astype(jnp.bfloat16)


def attention_kernel(table, q_ref, kpos_ref, *refs):
    pieces, (o_ref, k_scr, kt_scr, v_scr, s_scr, stat) = refs[:9], refs[9:]
    own, r1, r2, r3, l1, l2, l3, r4, l4 = pieces
    every, first, last = range(NY), range(NY // 2), range(NY // 2, NY)
    arrange(
        table,
        [(own, 0, every), (l1, 1, every), (l2, 2, every), (l3, 3, every), (r4, 4, first), (l4, 4, last)]
        + [(r3, 5, every), (r2, 6, every), (r1, 7, every)],
        k_scr,
        kt_scr,
        v_scr,
    )
    lane = lax.broadcasted_iota(jnp.int32, (ROWS, 128), 1)
    token = lax.broadcasted_iota(jnp.int32, (BLOCK, CHUNK), 0)

    def one_group(i, carry):
        low, high = table[AT_LOW + i], table[AT_HIGH + i]
        blocks = [table[AT_ORDER + i * JOINED + u] for u in range(JOINED)]
        ids = [table[AT_ID + i * JOINED + u] for u in range(JOINED)]

        def finish(u, out, total, top):
            place = pl.ds(pl.multiple_of(blocks[u] % 2 * ROWS, ROWS), ROWS)
            o_ref[blocks[u] // 2, place, :] = out.astype(jnp.bfloat16)
            old = jnp.where(lane == blocks[u], top, stat[...])
            stat[...] = jnp.where(lane == blocks[u] + Q_BLOCKS, total, old)

        def work(n):
            q = jnp.concatenate([q_ref[blocks[u]] for u in range(JOINED)], axis=0)
            tops = [None] * (JOINED * GROUP)
            for c in range(n):
                start = pl.multiple_of((low + c) * CHUNK, CHUNK)
                s = jnp.dot(q, kt_scr[:, pl.ds(start, CHUNK)], preferred_element_type=jnp.float32)
                kpos = kpos_ref[pl.ds(low + c, 1), :]
                for u in range(JOINED):
                    distance = (ids[u] * BLOCK + token) - kpos
                    bias = jnp.where((distance >= 0) & (distance < WINDOW), 0.0, NEG)
                    for g in range(GROUP):
                        r = u * GROUP + g
                        part = s[r * BLOCK : (r + 1) * BLOCK] + bias
                        s_scr[c, r * BLOCK : (r + 1) * BLOCK, :] = part
                        wide = jnp.maximum(part[:, :128], part[:, 128:])
                        tops[r] = wide if tops[r] is None else jnp.maximum(tops[r], wide)
            top = jnp.max(jnp.concatenate(tops, axis=0), axis=1, keepdims=True) * SCALE
            top = jnp.broadcast_to(top, (JOINED * ROWS, 128))
            twice = jnp.concatenate([top, top], axis=1)
            acc = None
            for c in range(n):
                start = pl.multiple_of((low + c) * CHUNK, CHUNK)
                p = jnp.exp2(s_scr[c] * SCALE - twice).astype(jnp.bfloat16)
                part = jnp.dot(p, v_scr[pl.ds(start, CHUNK), :], preferred_element_type=jnp.float32)
                acc = part if acc is None else acc + part
            for u in range(JOINED):
                rows = slice(u * ROWS, (u + 1) * ROWS)
                finish(u, acc[rows, :HEAD] / acc[rows, HEAD:], acc[rows, HEAD:], top[rows])

        @pl.when(high <= low)
        def _():
            nothing = jnp.zeros((ROWS, 128), jnp.float32)
            for u in range(JOINED):
                finish(u, nothing, nothing, nothing + NEG)

        for n in range(1, KEYS // CHUNK + 1):
            pl.when(high - low == n)(functools.partial(work, n))
        return carry

    stat[...] = jnp.zeros((ROWS, 128), jnp.float32)
    lax.fori_loop(0, Q_BLOCKS // JOINED, one_group, 0)
    turned = stat[...].T
    for d in range(PLANE):
        value = jnp.concatenate(
            [turned[2 * d : 2 * d + 2], turned[Q_BLOCKS + 2 * d : Q_BLOCKS + 2 * d + 2]], axis=0
        )
        first = value.astype(jnp.bfloat16).astype(jnp.float32)
        second = (value - first).astype(jnp.bfloat16).astype(jnp.float32)
        third = value - first - second
        rows = jnp.concatenate([first, second, third, jnp.zeros_like(first)], axis=0)
        o_ref[d, 2 * ROWS :, :] = rows.astype(jnp.bfloat16)


def combine_kernel(heads, blocks, length, choose_ref, k0_ref, k1_ref, k2_ref, k3_ref, m_ref, o_ref, cache_ref):
    found = jnp.concatenate([k0_ref[0], k1_ref[...], k2_ref[...], k3_ref[...]], axis=0)
    for half in range(2):
        cache = jnp.dot(choose_ref[...], found[:, half * HEAD : (half + 1) * HEAD], preferred_element_type=jnp.float32)
        cache_ref[half] = cache.astype(jnp.bfloat16)
    values = []
    for d in range(PLANE):
        rows = m_ref[d, 2 * ROWS :, :].astype(jnp.float32)
        values.append(rows[0:4] + rows[4:8] + rows[8:12])
    weights = [None] * PLANE
    for y in range(NY):
        sources = [x * NY + y for x in range(NX)]
        top = values[sources[0]][0:2]
        for d in sources[1:]:
            top = jnp.maximum(top, values[d][0:2])
        parts = [jnp.exp2(values[d][0:2] - top) * values[d][2:4] for d in sources]
        total = parts[0] + parts[1] + parts[2] + parts[3]
        for d, part in zip(sources, parts):
            weights[d] = part / total
    matrix = jnp.concatenate(weights + [jnp.zeros((128 - Q_BLOCKS, 128), jnp.float32)], axis=0).T
    token = lax.broadcasted_iota(jnp.int32, (ROWS, HEAD), 0) % BLOCK
    for y in range(NY):
        for j in range(2):
            out = jnp.zeros((ROWS, HEAD), jnp.float32)
            for x in range(NX):
                d = x * NY + y
                weight = matrix[:, 2 * d + j : 2 * d + j + 1]
                out += weight * m_ref[d, j * ROWS : (j + 1) * ROWS, :].astype(jnp.float32)
            out = jnp.where(blocks[j] * BLOCK + token < length[0], out, 0.0).astype(jnp.bfloat16)
            for g in range(GROUP):
                column = pl.multiple_of((heads[y] * GROUP + g) * HEAD, HEAD)
                o_ref[j * BLOCK : (j + 1) * BLOCK, pl.ds(column, HEAD)] = out[g * BLOCK : (g + 1) * BLOCK]


def ranks(ids):
    return jnp.sum(ids[..., None, :] < ids[..., :, None], axis=-1, dtype=jnp.int32)


def placed(values, rank):
    places = jnp.arange(values.shape[-1], dtype=jnp.int32)
    return jnp.sum(jnp.where(rank[..., None, :] == places[:, None], values[..., None, :], 0), axis=-1, dtype=jnp.int32)


def body(query, rotated_key_value, lengths, block_map, segment_head):
    place = lax.axis_index("blk")
    z, x, y = place // 16, (place // 4) % 4, place % 4
    y_groups = [[4 * g + i for i in range(4)] for g in range(N_BLK // 4)]
    x_groups = [[16 * a + 4 * i + c for i in range(4)] for a in range(NZ) for c in range(NY)]
    planes = [[16 * a + i for i in range(16)] for a in range(NZ)]

    def move(value, target):
        return lax.ppermute(value, "blk", [(s, target(s // 16, (s // 4) % 4, s % 4)) for s in range(N_BLK)])

    def index(zz, xx, yy):
        return (zz % NZ) * 16 + xx * 4 + yy

    def exchange(value, groups):
        return lax.all_to_all(value, "blk", 0, 0, axis_index_groups=groups, tiled=True)

    kv = pl.pallas_call(
        split_kv_kernel,
        out_shape=(jax.ShapeDtypeStruct((128, HEAD), jnp.bfloat16),) * NY,
        in_specs=[SMEM, VMEM],
        out_specs=(VMEM,) * NY,
        name="split_kv",
    )(segment_head, rotated_key_value.reshape(128, KEY_VALUE_HEADS * HEAD))
    line = [kv[0]] + [move(kv[k], lambda a, b, c, k=k: index(a, b, c ^ k)) for k in range(1, NY)]
    own = jnp.concatenate(line, axis=0)
    right = lambda v: move(v, lambda a, b, c: index(a + 1, b, c))
    left = lambda v: move(v, lambda a, b, c: index(a - 1, b, c))
    r1, l1 = right(own), left(own)
    q = pl.pallas_call(
        split_q_kernel,
        out_shape=jax.ShapeDtypeStruct((PLANE, 2 * ROWS, HEAD), jnp.bfloat16),
        in_specs=[SMEM, VMEM],
        out_specs=VMEM,
        compiler_params=SMALL,
        name="split_q",
    )(segment_head, query.reshape(2 * BLOCK, QUERY_HEADS * HEAD))
    q = exchange(q, planes).reshape(Q_BLOCKS, ROWS, HEAD)
    r2, l2 = right(r1), left(l1)
    r3, l3 = right(r2), left(l2)
    half = own.shape[0] // 2
    r4 = move(r2[:half], lambda a, b, c: index(a + 2, b, c))
    l4 = move(l2[half:], lambda a, b, c: index(a - 2, b, c))

    block_map, _ = lax.optimization_barrier((block_map, own))

    ids = block_map.reshape(NZ, NX, NY, 2).transpose(1, 0, 2, 3).reshape(NX, KEY_BLOCKS)
    rank = ranks(ids)
    ordered = placed(ids, rank)
    mine = lax.dynamic_index_in_dim(ordered, x, 0, keepdims=False)
    my_rank = lax.dynamic_index_in_dim(rank, x, 0, keepdims=False)
    q_ids = lax.dynamic_slice_in_dim(block_map, z * Q_BLOCKS, Q_BLOCKS)
    q_rank = ranks(q_ids)
    q_order = placed(jnp.arange(Q_BLOCKS, dtype=jnp.int32), q_rank)
    q_sorted = placed(q_ids, q_rank)
    grouped = q_sorted.reshape(Q_BLOCKS // JOINED, JOINED)
    lows = jnp.sum(mine[None, :] < grouped[:, :1] - WINDOW // BLOCK, axis=1, dtype=jnp.int32) // CHUNK_BLOCKS
    highs = jnp.sum(mine[None, :] <= grouped[:, -1:], axis=1, dtype=jnp.int32)
    highs = (highs + CHUNK_BLOCKS - 1) // CHUNK_BLOCKS
    table = jnp.concatenate([my_rank, q_order, q_sorted, lows, highs])
    kpos = mine[:, None] * BLOCK + jnp.arange(BLOCK, dtype=jnp.int32)[None, :]
    kpos = kpos.reshape(KEYS // CHUNK, CHUNK)

    pieces = (own, r1, r2, r3, l1, l2, l3, r4, l4)
    picked = pl.pallas_call(
        pick_kernel,
        out_shape=jax.ShapeDtypeStruct((NX, KEY_BLOCKS, 2 * HEAD), jnp.bfloat16),
        in_specs=[VMEM] * 9,
        out_specs=VMEM,
        cost_estimate=pl.CostEstimate(flops=20_000_000, bytes_accessed=1_200_000, transcendentals=0),
        compiler_params=SMALL,
        name="pick",
    )(*pieces)
    picked = move(picked, lambda a, b, c: index(2 * c + a % 2, b, a // 2))
    partial = pl.pallas_call(
        attention_kernel,
        out_shape=jax.ShapeDtypeStruct((PLANE, MESSAGE, HEAD), jnp.bfloat16),
        in_specs=[SMEM] + [VMEM] * 11,
        out_specs=VMEM,
        scratch_shapes=[
            pltpu.VMEM((KEYS, HEAD), jnp.bfloat16),
            pltpu.VMEM((HEAD, KEYS), jnp.bfloat16),
            pltpu.VMEM((KEYS, 2 * HEAD), jnp.bfloat16),
            pltpu.VMEM((KEYS // CHUNK, JOINED * ROWS, CHUNK), jnp.float32),
            pltpu.VMEM((ROWS, 128), jnp.float32),
        ],
        compiler_params=PARAMS,
        cost_estimate=pl.CostEstimate(flops=3_000_000_000, bytes_accessed=4_000_000, transcendentals=5_000_000),
        name="attention",
    )(table, q, kpos, *pieces)
    partial, picked = lax.optimization_barrier((partial, picked))
    out = exchange(partial, planes)

    kept = [move(picked[k], lambda a, b, c, k=k: index(a, b ^ k, c)) for k in range(1, NX)]
    blocks = jnp.arange(BLOCKS, dtype=jnp.int32)
    stored = jnp.sum(jnp.where(block_map[None, :] == blocks[:, None], blocks[None, :], 0), axis=1, dtype=jnp.int32)
    from_z, from_y = 2 * y + z % 2, z // 2
    row = ((stored // 8 % NX) ^ x) * KEY_BLOCKS + (stored // 32 - from_z) % NZ * 8
    row = row + ((stored // 2 % NY) ^ from_y) * 2 + stored % 2
    position = blocks * BLOCK + place % BLOCK
    choose = (row[:, None] == blocks[None, :]) & (position < lengths[0])[:, None]
    choose = choose.astype(jnp.bfloat16)
    my_blocks = lax.dynamic_slice_in_dim(block_map, 2 * place, 2)
    attended, cache = pl.pallas_call(
        combine_kernel,
        out_shape=(
            jax.ShapeDtypeStruct((2 * BLOCK, QUERY_HEADS * HEAD), jnp.bfloat16),
            jax.ShapeDtypeStruct((2, BLOCKS, HEAD), jnp.bfloat16),
        ),
        in_specs=[SMEM] * 3 + [VMEM] * 6,
        out_specs=(VMEM, VMEM),
        compiler_params=SMALL,
        name="combine",
    )(segment_head, my_blocks, lengths, choose, picked, *kept, out)
    return attended.reshape(1, 2 * BLOCK, QUERY_HEADS * HEAD), cache[None, :, None]


def solution(mesh):
    return jax.shard_map(
        body,
        mesh=mesh,
        in_specs=(P("req", "blk", None), P("req", None, "blk", None), P("req"), P(), P()),
        out_specs=(P("req", "blk", None), P("req", None, "blk", None, None)),
        check_vma=False,
    )
```
